256 devices in a mesh: ctx: 64 (over z, y, core), tp: 4 (over x).
Axes of the slice: x: 4, y: 4, z: 8, core: 2. Of those that a mesh axis runs over, the one named last changes fastest.
Arguments:
- query: bfloat16 [2, 8192, 2048], P(None, 'ctx', 'tp'), may hold values from -64 to 64
- key_states: bfloat16 [2, 8192, 1024], P(None, 'ctx', 'tp'), may hold values from -6 to 6
- value_state_rows: bfloat16 [2, 8192, 1024], P(None, 'ctx', 'tp'), may hold values from -6 to 6
- d_out: bfloat16 [2, 8192, 5376], P(None, ('ctx', 'tp')), may hold values from -24 to 24
- o_weight: bfloat16 [5376, 2048], P(None, 'tp'), may hold values from -0.125 to 0.125
- doc_start: int32 [2, 8192], P(None, 'ctx'), may hold values from 0 to 8191, as said below
Outputs:
- d_query: bfloat16 [2, 8192, 2048], P(None, 'ctx', 'tp')
- d_key: bfloat16 [2, 8192, 1024], P(None, 'ctx', 'tp')
- d_value: bfloat16 [2, 8192, 1024], P(None, 'ctx', 'tp')
- d_o_weight: float32 [5376, 2048], P('ctx', 'tp')
The draws below stay inside these ranges and needn't reach their ends.
Inputs may be any that keep to these rules, and one draw needn't show every extreme that they name: doc_start[s, t] is the position of the first token of the document holding token t of sequence s: it never falls along t, is at most t, equals t exactly where a document begins, and is 0 for the first document; the last token of every sequence begins a document of its own.
All inputs are finite; a program needn't handle non-finite values.
Results may differ from the reference program's by a relative error of at most 0.039.
Values may be sent and summed in bfloat16 or wider, within the bound.
No kernel may reach another device: no remote copies, remote signals or barrier semaphores. Data moves between devices by JAX's collectives and lax.ppermute only.
A program may use at most 128 MiB of HBM per device.

```python
import jax
import jax.numpy as jnp
from jax import lax

D = 5376
HEAD_SIZE = 128
WIN = 1024
QUERY_HEADS = 16
KEY_VALUE_HEADS = 8
TOKENS_PER_INDEX = 128
PACKED_SEQUENCES = 2
SEQUENCE_TOKENS = 8192
NHALO = 8


def shared_keys(key):
    random_base_key = jax.random.fold_in(key, 11)
    hidden_state_rows = jax.random.truncated_normal(random_base_key, -6.0, 6.0, (PACKED_SEQUENCES, SEQUENCE_TOKENS, KEY_VALUE_HEADS * HEAD_SIZE), jnp.float32)
    return hidden_state_rows


def draw_key_states(key, part):
    return shared_keys(key).astype(jnp.bfloat16)


def draw_query(key, part):
    noise_key = jax.random.fold_in(key, 23)
    fresh = jax.random.truncated_normal(noise_key, -6.0, 6.0, (PACKED_SEQUENCES, SEQUENCE_TOKENS, QUERY_HEADS * HEAD_SIZE), jnp.float32)
    return fresh.astype(jnp.bfloat16)


def draw_doc_start(key, part):
    positions = jnp.arange(SEQUENCE_TOKENS, dtype=jnp.int32)
    doc_total = SEQUENCE_TOKENS // 8 + 1

    def one_sequence(seq_key):
        lengths = jax.random.randint(seq_key, (doc_total,), 8, 4 * WIN, dtype=jnp.int32)
        bounds = jnp.cumsum(lengths).astype(jnp.int32)
        starts = jnp.concatenate([jnp.zeros((1,), jnp.int32), bounds[:-1]])
        starts = starts + (starts % 97 == 50).astype(jnp.int32)
        owner = (jnp.searchsorted(starts, positions, side='right') - 1).astype(jnp.int32)
        found = starts[owner]
        return jnp.where(positions == SEQUENCE_TOKENS - 1, positions, found).astype(jnp.int32)
    seq_keys = jax.random.split(jax.random.fold_in(key, 5), PACKED_SEQUENCES)
    return jax.vmap(one_sequence)(seq_keys).astype(jnp.int32)


def with_spikes(values, stream_key, source, target, shards_of, factor):
    def block_of(dim):
        return (jnp.arange(values.shape[dim]) // (values.shape[dim] // shards_of)).reshape((-1,) + (1,) * (values.ndim - 1 - dim))

    one_side = jax.random.permutation(stream_key, shards_of)[block_of(target)]
    other_side = (block_of(target) + shards_of // 2) % shards_of
    return jnp.where((block_of(source) == one_side) | (block_of(source) == other_side), factor * values, values)


def steps_of(stream_key, dims, shards, smallest, largest):
    loudness = 1.0
    for axis_at, blocks in shards:
        heights = jax.random.uniform(jax.random.fold_in(jax.random.fold_in(stream_key, 6), axis_at), (blocks,), jnp.float32, smallest / len(shards), largest / len(shards))
        loudness = loudness * jnp.repeat(jnp.exp(heights), dims[axis_at] // blocks).reshape((-1,) + (1,) * (len(dims) - 1 - axis_at))
    return loudness


def gaussian(rng, extent, deviation, limit, cuts=(), held_as=jnp.bfloat16):
    loudness = steps_of(rng, extent, cuts, -0.22, 0.18) if cuts else 1.0
    values = jax.random.normal(rng, extent, jnp.float32) * deviation * loudness
    return jnp.minimum(jnp.maximum(values, -limit), limit).astype(held_as)


def bell_draw_with(own_key, shape, spread, most, cuts, heavy, held_as=jnp.bfloat16):
    values = spread * jax.random.normal(own_key, shape, jnp.float32)
    if cuts:
        values = values * steps_of(own_key, shape, cuts, -0.22, 0.18)
    return jnp.clip(with_spikes(values, jax.random.fold_in(own_key, 3), *heavy), -most, most).astype(held_as)


def setup_inputs(seed: int = 0) -> dict:
    streams_of = jax.random.split(jax.random.key(seed), 7)
    query = draw_query(jax.random.fold_in(streams_of[6], 71), 0)
    key_states = draw_key_states(jax.random.fold_in(streams_of[6], 71), 0)
    value_state_rows = gaussian(streams_of[2], (PACKED_SEQUENCES, SEQUENCE_TOKENS, KEY_VALUE_HEADS * HEAD_SIZE), 1.0, 6.0, ((1, 64), (2, 4)))
    d_out = bell_draw_with(streams_of[3], (PACKED_SEQUENCES, SEQUENCE_TOKENS, D), 1.0, 24.0, ((1, 256),), (1, 2, 256, 6.0))
    o_weight = gaussian(streams_of[4], (D, QUERY_HEADS * HEAD_SIZE), (QUERY_HEADS * HEAD_SIZE) ** -0.5, 0.125, ((1, 4),))
    doc_start = draw_doc_start(jax.random.fold_in(streams_of[6], 71), 0)
    return {"query": query, "key_states": key_states, "value_state_rows": value_state_rows, "d_out": d_out, "o_weight": o_weight, "doc_start": doc_start}


score_scale = 168.0 ** -0.5


def sequence_grads(query, key_states, value_state_rows, d_out, doc_start, o_weight):
    attention_gradient_total = jnp.dot(d_out, o_weight, preferred_element_type=jnp.float32).astype(jnp.bfloat16)
    query_group_count = QUERY_HEADS // KEY_VALUE_HEADS
    window_edge = NHALO * TOKENS_PER_INDEX
    key_total_count = window_edge + TOKENS_PER_INDEX
    padded_key_rows = jnp.pad(key_states, ((window_edge, 0), (0, 0)))
    padded_value_rows = jnp.pad(value_state_rows, ((window_edge, 0), (0, 0)))

    def block_step(passing, block_id):
        key_gradient_rows, value_gradient_rows = passing
        first_row_index = (block_id * TOKENS_PER_INDEX).astype(jnp.int32)
        query_block_rows = lax.dynamic_slice_in_dim(query, first_row_index, TOKENS_PER_INDEX, 0).astype(jnp.float32).reshape(TOKENS_PER_INDEX, KEY_VALUE_HEADS, query_group_count, HEAD_SIZE)
        key_block_rows = lax.dynamic_slice_in_dim(padded_key_rows, first_row_index, key_total_count, 0).astype(jnp.float32).reshape(key_total_count, KEY_VALUE_HEADS, HEAD_SIZE)
        value_block_rows = lax.dynamic_slice_in_dim(padded_value_rows, first_row_index, key_total_count, 0).astype(jnp.float32).reshape(key_total_count, KEY_VALUE_HEADS, HEAD_SIZE)
        block_gradient = lax.dynamic_slice_in_dim(attention_gradient_total, first_row_index, TOKENS_PER_INDEX, 0).astype(jnp.float32).reshape(TOKENS_PER_INDEX, KEY_VALUE_HEADS, query_group_count, HEAD_SIZE)
        start_blk = lax.dynamic_slice_in_dim(doc_start, first_row_index, TOKENS_PER_INDEX, 0)
        query_pos = first_row_index + jnp.arange(TOKENS_PER_INDEX, dtype=jnp.int32)
        key_pos = first_row_index - window_edge + jnp.arange(key_total_count, dtype=jnp.int32)
        visible = (key_pos[None, :] <= query_pos[:, None]) & (key_pos[None, :] > query_pos[:, None] - WIN) & (key_pos[None, :] >= start_blk[:, None])
        scores = jnp.einsum("qhgd,khd->hgqk", query_block_rows, key_block_rows) * score_scale
        scores = jnp.where(visible[None, None], scores, -jnp.inf)
        row_max = jnp.max(scores, axis=-1, keepdims=True)
        expo = jnp.exp(scores - row_max)
        attn_weights = expo / jnp.sum(expo, axis=-1, keepdims=True)
        weights_b = attn_weights.astype(jnp.bfloat16)
        attn_blk = jnp.einsum("hgqk,khd->qhgd", weights_b.astype(jnp.float32), value_block_rows).astype(jnp.bfloat16)
        d_probs = jnp.einsum("qhgd,khd->hgqk", block_gradient, value_block_rows)
        row_delta = jnp.sum(block_gradient * attn_blk.astype(jnp.float32), axis=-1)
        row_delta = jnp.transpose(row_delta, (1, 2, 0))[..., None]
        d_scores = (attn_weights * (d_probs - row_delta)).astype(jnp.bfloat16)
        d_query = (jnp.einsum("hgqk,khd->qhgd", d_scores.astype(jnp.float32), key_block_rows) * score_scale).astype(jnp.bfloat16)
        key_block_gradient = jnp.einsum("hgqk,qhgd->khd", d_scores.astype(jnp.float32), query_block_rows) * score_scale
        value_block_gradient = jnp.einsum("hgqk,qhgd->khd", weights_b.astype(jnp.float32), block_gradient)
        prior_key_rows = lax.dynamic_slice_in_dim(key_gradient_rows, first_row_index, key_total_count, 0)
        key_gradient_rows = lax.dynamic_update_slice_in_dim(key_gradient_rows, prior_key_rows + key_block_gradient.reshape(key_total_count, KEY_VALUE_HEADS * HEAD_SIZE), first_row_index, 0)
        prior_value_rows = lax.dynamic_slice_in_dim(value_gradient_rows, first_row_index, key_total_count, 0)
        value_gradient_rows = lax.dynamic_update_slice_in_dim(value_gradient_rows, prior_value_rows + value_block_gradient.reshape(key_total_count, KEY_VALUE_HEADS * HEAD_SIZE), first_row_index, 0)
        return (key_gradient_rows, value_gradient_rows), (d_query.reshape(TOKENS_PER_INDEX, QUERY_HEADS * HEAD_SIZE), attn_blk.reshape(TOKENS_PER_INDEX, QUERY_HEADS * HEAD_SIZE))

    blocks = jnp.arange(SEQUENCE_TOKENS // TOKENS_PER_INDEX, dtype=jnp.int32)
    empty_filler = jnp.zeros((SEQUENCE_TOKENS + window_edge, KEY_VALUE_HEADS * HEAD_SIZE), jnp.float32)
    (key_gradient_rows, value_gradient_rows), (d_query, attn) = lax.scan(block_step, (empty_filler, empty_filler), blocks)
    attn = attn.reshape(SEQUENCE_TOKENS, QUERY_HEADS * HEAD_SIZE)
    weight_grad = jnp.dot(d_out.T, attn, preferred_element_type=jnp.float32)
    return (d_query.reshape(SEQUENCE_TOKENS, QUERY_HEADS * HEAD_SIZE), key_gradient_rows[window_edge:].astype(jnp.bfloat16), value_gradient_rows[window_edge:].astype(jnp.bfloat16), weight_grad)


def reference(query, key_states, value_state_rows, d_out, o_weight, doc_start):
    def one_sequence(packed):
        return sequence_grads(packed[0], packed[1], packed[2], packed[3], packed[4], o_weight)

    d_query, d_key, d_value, weight_grads = lax.map(one_sequence, (query, key_states, value_state_rows, d_out, doc_start))
    return (d_query, d_key, d_value, jnp.sum(weight_grads, axis=0))
```

```python
import jax
import jax.numpy as jnp
from jax import lax
from jax.experimental import pallas as pl
from jax.experimental.pallas import tpu as pltpu
from jax.sharding import PartitionSpec as P

HEAD_SIZE = 128
WIN = 1024
CORES = 2
CHIPS_Y = 4
CHIPS_Z = 8
TP = 4
HALO_CHIPS = 4
LOG2_E = 1.4426950408889634

score_scale = 168.0 ** (-0.5)

NT = (((1,), (1,)), ((), ()))
TN = (((0,), (0,)), ((), ()))
NN = (((1,), (0,)), ((), ()))


def dot(a, b, dims=NN):
    return lax.dot_general(a, b, dims, preferred_element_type=jnp.float32)


def ctx_shift(block, move):
    count = CORES * CHIPS_Y * CHIPS_Z
    return lax.ppermute(block, "ctx", [(i, move(i)) for i in range(count)])


def to_sibling(block):
    return ctx_shift(block, lambda i: i ^ 1)


def chips_ahead(block, distance):
    count = CORES * CHIPS_Y * CHIPS_Z
    return ctx_shift(block, lambda i: (i + CORES * distance) % count)


def y_ahead(block, distance):
    def move(i):
        core, y, z = i % CORES, i // CORES % CHIPS_Y, i // (CORES * CHIPS_Y)
        return (z * CHIPS_Y + (y + distance) % CHIPS_Y) * CORES + core

    return ctx_shift(block, move)


def z_exchange(blocks):
    lanes = CORES * CHIPS_Y
    groups = [[z * lanes + lane for z in range(CHIPS_Z)] for lane in range(lanes)]
    return lax.all_to_all(blocks, "ctx", 0, 0, axis_index_groups=groups, tiled=True)


def tp_ahead(block, distance):
    return lax.ppermute(block, "tp", [(i, (i + distance) % TP) for i in range(TP)])


def query_positions(core, chip_pos, rows):
    lane = lax.broadcasted_iota(jnp.int32, (1, 2 * rows), 1)
    other = lane >= rows
    first = jnp.where(other, (1 - core) * rows - rows, core * rows)
    return chip_pos + first + lane


def forward_kernel(scalars, mine, recv, kv0, kv1, kv2, kv3, kv4, doc_mine, doc_recv, attn, weights):
    core, chip_pos = scalars[0], scalars[3]
    rows = mine.shape[1]
    query_pos = query_positions(core, chip_pos, rows)
    doc = jnp.concatenate([doc_mine[0], doc_recv[0]], axis=1)
    lowest = jnp.maximum(doc, query_pos - (WIN - 1))
    index = lax.broadcasted_iota(jnp.int32, (2 * rows, 2 * rows), 0)
    offset = index + jnp.where(index >= rows, (1 - core) * rows - rows, core * rows)
    for h in range(2):
        cols = slice(h * HEAD_SIZE, (h + 1) * HEAD_SIZE)
        q = jnp.concatenate([mine[0, :, cols], recv[0, :, cols]], axis=0)
        scores = []
        for d, kv in enumerate((kv0, kv1, kv2, kv3, kv4)):
            s = dot(kv[0, :, :HEAD_SIZE], q, NT) * (score_scale * LOG2_E)
            key_pos = offset + (chip_pos - 2 * rows * d)
            visible = key_pos >= lowest
            if d == 0:
                visible = visible & (key_pos <= query_pos)
            scores.append(jnp.where(visible, s, -1e30))
        top = scores[0]
        for s in scores[1:]:
            top = jnp.maximum(top, s)
        top = jnp.max(top, axis=0, keepdims=True)
        expo = [jnp.exp2(s - top) for s in scores]
        total = expo[0]
        for e in expo[1:]:
            total = total + e
        inverse = 1.0 / jnp.sum(total, axis=0, keepdims=True)
        acc = None
        for d, kv in enumerate((kv0, kv1, kv2, kv3, kv4)):
            w = (expo[d] * inverse).astype(jnp.bfloat16)
            weights[0, h, 2 * rows * d : 2 * rows * (d + 1), :] = w
            part = dot(kv[0, :, HEAD_SIZE:], w, TN)
            acc = part if acc is None else acc + part
        attn[0, :, cols] = acc.T.astype(jnp.bfloat16)


def projection_kernel(
    scalars, r0, r1, r2a, r2b, r3, t0, t1, t2a, t2b, t3, attn, o_weight,
    d_attn, w0, w1, w2, w3, acc, attn_rows, partial,
):
    step = pl.program_id(0)
    tp, y = scalars[1], scalars[2]
    piece = r0.shape[1]
    out_rows = w0.shape[1]

    def place(core_block, rel, seq):
        here = 4 * piece * core_block + piece * ((tp + rel) % TP)
        return seq, pl.ds(pl.multiple_of(here, piece), piece)

    slots = [(b, s, q) for b in range(2) for s in range(TP) for q in range(2)]

    @pl.when(step == 0)
    def _():
        for n, slot in enumerate(slots):
            seq, here = place(*slot)
            attn_rows[n * piece : (n + 1) * piece, :] = attn[seq, here, :]

    parts = []
    for ref in (r0, r1, r2a, r2b, r3, t0, t1, t2a, t2b, t3):
        for seq in range(ref.shape[0]):
            parts.append(ref[seq])
    rows = jnp.concatenate(parts, axis=0)
    product = dot(rows, o_weight[...])

    @pl.when(step == 0)
    def _():
        acc[...] = product

    @pl.when(step > 0)
    def _():
        acc[...] = acc[...] + product

    partial[...] = dot(rows, attn_rows[...], TN)
    for k, out in enumerate((w0, w1, w2, w3)):
        target = (y + k) % CHIPS_Y
        for z in range(out.shape[0]):
            start = pl.multiple_of((CHIPS_Y * z + target) * out_rows, 8)
            out[z] = partial[pl.ds(start, out_rows), :].astype(jnp.bfloat16)

    @pl.when(step == pl.num_programs(0) - 1)
    def _():
        for n, slot in enumerate(slots):
            seq, here = place(*slot)
            d_attn[seq, here, :] = acc[n * piece : (n + 1) * piece, :].astype(jnp.bfloat16)


def backward_kernel(
    mine, recv, kv0, kv1, kv2, kv3, kv4, weights, attn, d_attn,
    dq_mine, dq_other, g0, g1, g2, g3, g4,
):
    rows = mine.shape[1]
    heads = []
    for h in range(2):
        cols = slice(h * HEAD_SIZE, (h + 1) * HEAD_SIZE)
        q = jnp.concatenate([mine[0, :, cols], recv[0, :, cols]], axis=0)
        da = d_attn[0, :, cols]
        product = da.astype(jnp.float32) * attn[0, :, cols].astype(jnp.float32)
        delta = jnp.sum(product.T, axis=0, keepdims=True)
        heads.append((q, da, delta))
    dq = [None, None]
    for d, (kv, grad) in enumerate(zip((kv0, kv1, kv2, kv3, kv4), (g0, g1, g2, g3, g4))):
        keys = kv[0, :, :HEAD_SIZE]
        values = kv[0, :, HEAD_SIZE:]
        dk = dv = None
        for h, (q, da, delta) in enumerate(heads):
            w = weights[0, h, 2 * rows * d : 2 * rows * (d + 1), :]
            dp = dot(values, da, NT)
            ds = (w.astype(jnp.float32) * (dp - delta)).astype(jnp.bfloat16)
            v_part = dot(w, da)
            k_part = dot(ds, q)
            q_part = dot(keys, ds, TN)
            dv = v_part if dv is None else dv + v_part
            dk = k_part if dk is None else dk + k_part
            dq[h] = q_part if dq[h] is None else dq[h] + q_part
        grad[0, :, :HEAD_SIZE] = (dk * score_scale).astype(grad.dtype)
        grad[0, :, HEAD_SIZE:] = dv.astype(grad.dtype)
    for h in range(2):
        cols = slice(h * HEAD_SIZE, (h + 1) * HEAD_SIZE)
        full = (dq[h].T * score_scale).astype(jnp.bfloat16)
        dq_mine[0, :, cols] = full[:rows]
        dq_other[0, :, cols] = full[rows:]


def by_seq(shape):
    return pl.BlockSpec((1,) + shape[1:], lambda s, *_: (s,) + (0,) * (len(shape) - 1))


def forward(scalars, mine, recv, kvs, doc_mine, doc_recv):
    seqs, rows, width = mine.shape
    keys = 2 * rows * len(kvs)
    outs = (
        jax.ShapeDtypeStruct((seqs, 2 * rows, width // 2), jnp.bfloat16),
        jax.ShapeDtypeStruct((seqs, 2, keys, 2 * rows), jnp.bfloat16),
    )
    query_spec = pl.BlockSpec((1, rows, width // 2), lambda s, *_: (s, 0, 0))
    return pl.pallas_call(
        forward_kernel,
        out_shape=outs,
        grid_spec=pltpu.PrefetchScalarGridSpec(
            num_scalar_prefetch=1,
            grid=(seqs,),
            in_specs=[query_spec, query_spec]
            + [by_seq(kv.shape) for kv in kvs]
            + [by_seq(doc_mine.shape), by_seq(doc_recv.shape)],
            out_specs=[by_seq(o.shape) for o in outs],
        ),
        compiler_params=pltpu.CompilerParams(vmem_limit_bytes=48 << 20),
        name="attention_forward",
    )(scalars, mine, recv, *kvs, doc_mine, doc_recv)


def projection(scalars, pieces, attn, o_weight):
    seqs, chip_rows, width = attn.shape
    features = o_weight.shape[0]
    steps = 2
    block = features // steps
    out_rows = features // (CHIPS_Y * CHIPS_Z)
    slab = jax.ShapeDtypeStruct((CHIPS_Z, out_rows, width), jnp.bfloat16)
    slab_spec = pl.BlockSpec((CHIPS_Z // steps, out_rows, width), lambda i, *_: (i, 0, 0))
    whole = pl.BlockSpec(attn.shape, lambda i, *_: (0, 0, 0))
    return pl.pallas_call(
        projection_kernel,
        out_shape=(jax.ShapeDtypeStruct(attn.shape, jnp.bfloat16),) + (slab,) * CHIPS_Y,
        grid_spec=pltpu.PrefetchScalarGridSpec(
            num_scalar_prefetch=1,
            grid=(steps,),
            in_specs=[pl.BlockSpec(p.shape[:2] + (block,), lambda i, *_: (0, 0, i)) for p in pieces]
            + [whole, pl.BlockSpec((block, width), lambda i, scalars: (i, scalars[0]))],
            out_specs=[whole] + [slab_spec] * CHIPS_Y,
            scratch_shapes=[
                pltpu.VMEM((seqs * chip_rows, width), jnp.float32),
                pltpu.VMEM((seqs * chip_rows, width), jnp.bfloat16),
                pltpu.VMEM((block, width), jnp.float32),
            ],
        ),
        compiler_params=pltpu.CompilerParams(vmem_limit_bytes=56 << 20),
        name="projection_grads",
    )(scalars, *pieces, attn, o_weight)


def backward(mine, recv, kvs, weights, attn, d_attn):
    seqs, rows, width = mine.shape
    half = jax.ShapeDtypeStruct((seqs, rows, width // 2), jnp.bfloat16)
    outs = (half, half) + tuple(
        jax.ShapeDtypeStruct(kv.shape, jnp.float32 if d == 0 else jnp.bfloat16)
        for d, kv in enumerate(kvs)
    )
    query_spec = pl.BlockSpec((1, rows, width // 2), lambda s, *_: (s, 0, 0))
    return pl.pallas_call(
        backward_kernel,
        out_shape=outs,
        grid=(seqs,),
        in_specs=[query_spec, query_spec]
        + [by_seq(a.shape) for a in (*kvs, weights, attn, d_attn)],
        out_specs=[by_seq(o.shape) for o in outs],
        compiler_params=pltpu.CompilerParams(vmem_limit_bytes=48 << 20),
        name="attention_backward",
    )(mine, recv, *kvs, weights, attn, d_attn)


def local(query, key_states, value_state_rows, d_out, o_weight, doc_start):
    seq_count, shard_rows, query_width = query.shape
    ctx = lax.axis_index("ctx")
    tp = lax.axis_index("tp")
    core = ctx % CORES
    y = ctx // CORES % CHIPS_Y
    chip_pos = ctx // CORES * (CORES * shard_rows)
    scalars = jnp.stack([core, tp, y, chip_pos]).astype(jnp.int32)
    first = core == 0

    def halves(a):
        w = a.shape[-1] // 2
        return a[..., :w], a[..., w:]

    def head_share(core_zero):
        parts = [
            jnp.where(core_zero, *halves(a)) for a in (query, key_states, value_state_rows)
        ]
        return jnp.concatenate(parts, axis=-1)

    mine = head_share(first)
    recv = to_sibling(head_share(~first))
    doc_mine = doc_start[:, None, :]
    doc_recv = to_sibling(doc_mine)

    r0 = d_out
    r3 = tp_ahead(r0, 1)
    r1 = tp_ahead(r0, -1)
    r2a = tp_ahead(r3[:1], 1)
    r2b = tp_ahead(r1[1:], -1)
    pieces = [r0, r1, r2a, r2b, r3]
    pieces = pieces + [to_sibling(p) for p in pieces]

    kv_width = 2 * HEAD_SIZE
    kv0 = jnp.concatenate([mine[..., -kv_width:], recv[..., -kv_width:]], axis=1)
    kvs = [kv0] + [chips_ahead(kv0, d) for d in range(1, HALO_CHIPS + 1)]

    attn, weights = forward(scalars, mine, recv, kvs, doc_mine, doc_recv)
    d_attn, w0, *w_sent = projection(scalars, pieces, attn, o_weight)
    w_arrived = [y_ahead(w, k + 1) for k, w in enumerate(w_sent)]
    dq_mine, dq_other, g0, *g_sent = backward(mine, recv, kvs, weights, attn, d_attn)
    g_arrived = [chips_ahead(g, -d - 1) for d, g in enumerate(g_sent)]
    dq_recv = to_sibling(dq_other)

    w_sum = w0.astype(jnp.float32)
    for w in w_arrived:
        w_sum = w_sum + w.astype(jnp.float32)
    w_all = z_exchange(w_sum.astype(jnp.bfloat16))
    w_rows = jnp.sum(w_all.astype(jnp.float32), axis=0)
    half_rows = w_rows.shape[0] // 2
    w_top, w_bottom = w_rows[:half_rows], w_rows[half_rows:]
    w_mine = jnp.where(first, w_top, w_bottom)
    w_recv = to_sibling(jnp.where(first, w_bottom, w_top))

    grads = g0
    for g in g_arrived:
        grads = grads + g.astype(jnp.float32)
    grads = grads.astype(jnp.bfloat16)
    g_mine = grads[:, :shard_rows]
    g_recv = to_sibling(grads[:, shard_rows:])

    def by_core(own, other):
        return jnp.concatenate(
            [jnp.where(first, own, other), jnp.where(first, other, own)], axis=-1
        )

    return (
        by_core(dq_mine, dq_recv),
        by_core(g_mine[..., :HEAD_SIZE], g_recv[..., :HEAD_SIZE]),
        by_core(g_mine[..., HEAD_SIZE:], g_recv[..., HEAD_SIZE:]),
        by_core(w_mine, w_recv),
    )


def solution(mesh):
    return jax.shard_map(
        local,
        mesh=mesh,
        in_specs=(
            P(None, "ctx", "tp"),
            P(None, "ctx", "tp"),
            P(None, "ctx", "tp"),
            P(None, ("ctx", "tp"), None),
            P(None, "tp"),
            P(None, "ctx"),
        ),
        out_specs=(
            P(None, "ctx", "tp"),
            P(None, "ctx", "tp"),
            P(None, "ctx", "tp"),
            P("ctx", "tp"),
        ),
        check_vma=False,
    )
```

```python
import jax
import jax.numpy as jnp
from jax import lax
from jax.experimental import pallas as pl
from jax.experimental.pallas import tpu as pltpu
from jax.sharding import PartitionSpec as P

HEAD_SIZE = 128
WIN = 1024
CORES = 2
CHIPS_Y = 4
CHIPS_Z = 8
TP = 4
HALO_CHIPS = 4
LOG2_E = 1.4426950408889634

score_scale = 168.0 ** (-0.5)

NT = (((1,), (1,)), ((), ()))
TN = (((0,), (0,)), ((), ()))
NN = (((1,), (0,)), ((), ()))


def dot(a, b, dims=NN):
    return lax.dot_general(a, b, dims, preferred_element_type=jnp.float32)


def ctx_shift(block, move):
    count = CORES * CHIPS_Y * CHIPS_Z
    return lax.ppermute(block, "ctx", [(i, move(i)) for i in range(count)])


def to_sibling(block):
    return ctx_shift(block, lambda i: i ^ 1)


def chips_ahead(block, distance):
    count = CORES * CHIPS_Y * CHIPS_Z
    return ctx_shift(block, lambda i: (i + CORES * distance) % count)


def y_pair(y):
    return y ^ 1


def y_mirror(y):
    return CHIPS_Y - 1 - y


def y_route(block, target):
    def move(i):
        core, y, z = i % CORES, i // CORES % CHIPS_Y, i // (CORES * CHIPS_Y)
        return (z * CHIPS_Y + target(y)) * CORES + core

    return ctx_shift(block, move)


def y_exchange(blocks):
    groups = [
        [(z * CHIPS_Y + y) * CORES + core for y in range(CHIPS_Y)]
        for z in range(CHIPS_Z)
        for core in range(CORES)
    ]
    return lax.all_to_all(blocks, "ctx", 0, 0, axis_index_groups=groups, tiled=True)


def z_exchange(blocks):
    lanes = CORES * CHIPS_Y
    groups = [[z * lanes + lane for z in range(CHIPS_Z)] for lane in range(lanes)]
    return lax.all_to_all(blocks, "ctx", 0, 0, axis_index_groups=groups, tiled=True)


def tp_ahead(block, distance):
    return lax.ppermute(block, "tp", [(i, (i + distance) % TP) for i in range(TP)])


def query_positions(core, chip_pos, rows):
    lane = lax.broadcasted_iota(jnp.int32, (1, 2 * rows), 1)
    other = lane >= rows
    first = jnp.where(other, (1 - core) * rows - rows, core * rows)
    return chip_pos + first + lane


def forward_kernel(scalars, mine, recv, kv0, kv1, kv2, kv3, kv4, doc_mine, doc_recv, attn, weights):
    core, chip_pos = scalars[0], scalars[3]
    rows = mine.shape[1]
    query_pos = query_positions(core, chip_pos, rows)
    doc = jnp.concatenate([doc_mine[0], doc_recv[0]], axis=1)
    lowest = jnp.maximum(doc, query_pos - (WIN - 1))
    index = lax.broadcasted_iota(jnp.int32, (2 * rows, 2 * rows), 0)
    offset = index + jnp.where(index >= rows, (1 - core) * rows - rows, core * rows)
    for h in range(2):
        cols = slice(h * HEAD_SIZE, (h + 1) * HEAD_SIZE)
        q = jnp.concatenate([mine[0, :, cols], recv[0, :, cols]], axis=0)
        scores = []
        for d, kv in enumerate((kv0, kv1, kv2, kv3, kv4)):
            s = dot(kv[0, :, :HEAD_SIZE], q, NT) * (score_scale * LOG2_E)
            key_pos = offset + (chip_pos - 2 * rows * d)
            visible = key_pos >= lowest
            if d == 0:
                visible = visible & (key_pos <= query_pos)
            scores.append(jnp.where(visible, s, -1e30))
        top = scores[0]
        for s in scores[1:]:
            top = jnp.maximum(top, s)
        top = jnp.max(top, axis=0, keepdims=True)
        expo = [jnp.exp2(s - top) for s in scores]
        total = expo[0]
        for e in expo[1:]:
            total = total + e
        inverse = 1.0 / jnp.sum(total, axis=0, keepdims=True)
        acc = None
        for d, kv in enumerate((kv0, kv1, kv2, kv3, kv4)):
            w = (expo[d] * inverse).astype(jnp.bfloat16)
            weights[0, h, 2 * rows * d : 2 * rows * (d + 1), :] = w
            part = dot(kv[0, :, HEAD_SIZE:], w, TN)
            acc = part if acc is None else acc + part
        attn[0, :, cols] = acc.T.astype(jnp.bfloat16)


def early_kernel(scalars, *refs):
    *pieces, o_weight, d_attn, rows_t, acc = refs
    step = pl.program_id(0)
    parts = [ref[seq] for ref in pieces for seq in range(ref.shape[0])]
    rows = jnp.concatenate(parts, axis=0)
    product = dot(rows, o_weight[...])

    @pl.when(step == 0)
    def _():
        acc[...] = product

    @pl.when(step > 0)
    def _():
        acc[...] = acc[...] + product

    rows_t[...] = rows.T

    @pl.when(step == pl.num_programs(0) - 1)
    def _():
        d_attn[...] = acc[...].astype(jnp.bfloat16)


def place(tp, piece, core_block, rel, seq):
    here = TP * piece * core_block + piece * ((tp + rel) % TP)
    return seq, pl.ds(pl.multiple_of(here, piece), piece)


OWN_SLOTS = [(b, 0, q) for b in range(2) for q in range(2)]
NEAR_SLOTS = [(b, s, q) for b in range(2) for s in (1, 3) for q in range(2)]
FAR_SLOTS = [(b, 2, q) for b in range(2) for q in range(2)]


def late_kernel(
    scalars, r2a, r2b, t2a, t2b, own_t, near_t, attn, own, near, o_weight,
    d_attn, sent_a, kept_a, sent_b, kept_b, acc, attn_own, attn_near, attn_far, partial,
):
    step = pl.program_id(0)
    tp, y = scalars[1], scalars[2]
    piece = r2a.shape[1]
    out_rows = sent_a.shape[2]

    @pl.when(step == 0)
    def _():
        for slots, kept in ((OWN_SLOTS, attn_own), (NEAR_SLOTS, attn_near), (FAR_SLOTS, attn_far)):
            for n, slot in enumerate(slots):
                seq, here = place(tp, piece, *slot)
                kept[n * piece : (n + 1) * piece, :] = attn[seq, here, :]
        for slots, done in ((OWN_SLOTS, own), (NEAR_SLOTS, near)):
            for n, slot in enumerate(slots):
                seq, here = place(tp, piece, *slot)
                d_attn[seq, here, :] = done[n * piece : (n + 1) * piece, :]

    rows = jnp.concatenate([r2a[0], r2b[0], t2a[0], t2b[0]], axis=0)
    partial[...] = (
        dot(own_t[...], attn_own[...])
        + dot(near_t[...], attn_near[...])
        + dot(rows.T, attn_far[...])
    )

    def emit(out, order):
        for n, target in enumerate(order):
            for z in range(out.shape[1]):
                start = pl.multiple_of((CHIPS_Y * z + target) * out_rows, 8)
                out[n, z] = partial[pl.ds(start, out_rows), :].astype(jnp.bfloat16)

    pair = y + 1 - 2 * (y % 2)
    mirror = CHIPS_Y - 1 - y
    mirror_pair = mirror + 1 - 2 * (mirror % 2)

    product = dot(rows, o_weight[...])

    @pl.when(step == 0)
    def _():
        emit(sent_a, (pair, CHIPS_Y - 1 - pair))
        emit(kept_a, (y, mirror))
        acc[...] = product

    @pl.when(step == 1)
    def _():
        emit(sent_b, (mirror, mirror_pair))
        emit(kept_b, (y, pair))
        total = (acc[...] + product).astype(jnp.bfloat16)
        for n, slot in enumerate(FAR_SLOTS):
            seq, here = place(tp, piece, *slot)
            d_attn[seq, here, :] = total[n * piece : (n + 1) * piece, :]


def backward_kernel(
    scalars, mine, recv, kv0, kv1, kv2, kv3, kv4, weights, attn, d_attn,
    dq_mine, dq_other, g_own, g_sent,
):
    rows = mine.shape[1]
    y = scalars[2]
    heads = []
    for h in range(2):
        cols = slice(h * HEAD_SIZE, (h + 1) * HEAD_SIZE)
        q = jnp.concatenate([mine[0, :, cols], recv[0, :, cols]], axis=0)
        da = d_attn[0, :, cols]
        product = da.astype(jnp.float32) * attn[0, :, cols].astype(jnp.float32)
        delta = jnp.sum(product.T, axis=0, keepdims=True)
        heads.append((q, da, delta))
    dq = [None, None]
    for d, kv in enumerate((kv0, kv1, kv2, kv3, kv4)):
        keys = kv[0, :, :HEAD_SIZE]
        values = kv[0, :, HEAD_SIZE:]
        dk = dv = None
        for h, (q, da, delta) in enumerate(heads):
            w = weights[0, h, 2 * rows * d : 2 * rows * (d + 1), :]
            dp = dot(values, da, NT)
            ds = (w.astype(jnp.float32) * (dp - delta)).astype(jnp.bfloat16)
            v_part = dot(w, da)
            k_part = dot(ds, q)
            q_part = dot(keys, ds, TN)
            dv = v_part if dv is None else dv + v_part
            dk = k_part if dk is None else dk + k_part
            dq[h] = q_part if dq[h] is None else dq[h] + q_part
        if d == 0:
            g_own[0, :, :HEAD_SIZE] = dk * score_scale
            g_own[0, :, HEAD_SIZE:] = dv
        else:
            column = (y + CHIPS_Y - d) % CHIPS_Y
            g_sent[column, 0, :, :HEAD_SIZE] = (dk * score_scale).astype(jnp.bfloat16)
            g_sent[column, 0, :, HEAD_SIZE:] = dv.astype(jnp.bfloat16)
    for h in range(2):
        cols = slice(h * HEAD_SIZE, (h + 1) * HEAD_SIZE)
        full = (dq[h].T * score_scale).astype(jnp.bfloat16)
        dq_mine[0, :, cols] = full[:rows]
        dq_other[0, :, cols] = full[rows:]


def by_seq(shape):
    return pl.BlockSpec((1,) + shape[1:], lambda s, *_: (s,) + (0,) * (len(shape) - 1))


def forward(scalars, mine, recv, kvs, doc_mine, doc_recv):
    seqs, rows, width = mine.shape
    keys = 2 * rows * len(kvs)
    outs = (
        jax.ShapeDtypeStruct((seqs, 2 * rows, width // 2), jnp.bfloat16),
        jax.ShapeDtypeStruct((seqs, 2, keys, 2 * rows), jnp.bfloat16),
    )
    query_spec = pl.BlockSpec((1, rows, width // 2), lambda s, *_: (s, 0, 0))
    return pl.pallas_call(
        forward_kernel,
        out_shape=outs,
        grid_spec=pltpu.PrefetchScalarGridSpec(
            num_scalar_prefetch=1,
            grid=(seqs,),
            in_specs=[query_spec, query_spec]
            + [by_seq(kv.shape) for kv in kvs]
            + [by_seq(doc_mine.shape), by_seq(doc_recv.shape)],
            out_specs=[by_seq(o.shape) for o in outs],
        ),
        compiler_params=pltpu.CompilerParams(vmem_limit_bytes=20 << 20),
        cost_estimate=pl.CostEstimate(
            flops=4 * seqs * 2 * 2 * rows * keys * HEAD_SIZE,
            transcendentals=seqs * 2 * 2 * rows * keys,
            bytes_accessed=8 << 20,
        ),
        name="attention_forward",
    )(scalars, mine, recv, *kvs, doc_mine, doc_recv)


def early_projection(scalars, pieces, o_weight):
    rows = sum(p.shape[0] * p.shape[1] for p in pieces)
    features, both = o_weight.shape
    width = both // 2
    steps = 7
    block = features // steps
    outs = (
        jax.ShapeDtypeStruct((rows, width), jnp.bfloat16),
        jax.ShapeDtypeStruct((features, rows), jnp.bfloat16),
    )
    return pl.pallas_call(
        early_kernel,
        out_shape=outs,
        grid_spec=pltpu.PrefetchScalarGridSpec(
            num_scalar_prefetch=1,
            grid=(steps,),
            in_specs=[pl.BlockSpec(p.shape[:2] + (block,), lambda i, *_: (0, 0, i)) for p in pieces]
            + [pl.BlockSpec((block, width), lambda i, scalars: (i, scalars[0]))],
            out_specs=[
                pl.BlockSpec((rows, width), lambda i, *_: (0, 0)),
                pl.BlockSpec((block, rows), lambda i, *_: (i, 0)),
            ],
            scratch_shapes=[pltpu.VMEM((rows, width), jnp.float32)],
        ),
        compiler_params=pltpu.CompilerParams(vmem_limit_bytes=16 << 20),
        cost_estimate=pl.CostEstimate(
            flops=20 * rows * features * width, transcendentals=0, bytes_accessed=12 << 20
        ),
        name="projection_early",
    )(scalars, *pieces, o_weight)


def late_projection(scalars, pieces, rows_t, attn, early, o_weight):
    width = attn.shape[-1]
    features = o_weight.shape[0]
    late_rows = sum(p.shape[0] * p.shape[1] for p in pieces)
    steps = 2
    block = features // steps
    out_rows = features // (CHIPS_Y * CHIPS_Z)
    slab = jax.ShapeDtypeStruct((2, CHIPS_Z // 2, out_rows, width), jnp.bfloat16)

    def whole(a):
        return pl.BlockSpec(a.shape, lambda i, *_: (0,) * len(a.shape))

    return pl.pallas_call(
        late_kernel,
        out_shape=(jax.ShapeDtypeStruct(attn.shape, jnp.bfloat16),) + (slab,) * 4,
        grid_spec=pltpu.PrefetchScalarGridSpec(
            num_scalar_prefetch=1,
            grid=(steps,),
            in_specs=[pl.BlockSpec(p.shape[:2] + (block,), lambda i, *_: (0, 0, i)) for p in pieces]
            + [pl.BlockSpec((block, r.shape[1]), lambda i, *_: (i, 0)) for r in rows_t]
            + [whole(attn)]
            + [whole(e) for e in early]
            + [pl.BlockSpec((block, width), lambda i, scalars: (i, scalars[0]))],
            out_specs=[whole(attn)] + [whole(slab)] * 4,
            scratch_shapes=[pltpu.VMEM((late_rows, width), jnp.float32)]
            + [pltpu.VMEM((r.shape[1], width), jnp.bfloat16) for r in rows_t]
            + [
                pltpu.VMEM((late_rows, width), jnp.bfloat16),
                pltpu.VMEM((block, width), jnp.float32),
            ],
        ),
        compiler_params=pltpu.CompilerParams(vmem_limit_bytes=32 << 20),
        cost_estimate=pl.CostEstimate(
            flops=2 * 6 * late_rows * features * width, transcendentals=0, bytes_accessed=12 << 20
        ),
        name="projection_late",
    )(scalars, *pieces, *rows_t, attn, *early, o_weight)


def backward(scalars, mine, recv, kvs, weights, attn, d_attn):
    seqs, rows, width = mine.shape
    half = jax.ShapeDtypeStruct((seqs, rows, width // 2), jnp.bfloat16)
    shape = kvs[0].shape
    own = jax.ShapeDtypeStruct(shape, jnp.float32)
    sent = jax.ShapeDtypeStruct((CHIPS_Y,) + shape, jnp.bfloat16)
    query_spec = pl.BlockSpec((1, rows, width // 2), lambda s, *_: (s, 0, 0))
    return pl.pallas_call(
        backward_kernel,
        out_shape=(half, half, own, sent),
        grid_spec=pltpu.PrefetchScalarGridSpec(
            num_scalar_prefetch=1,
            grid=(seqs,),
            in_specs=[query_spec, query_spec]
            + [by_seq(a.shape) for a in (*kvs, weights, attn, d_attn)],
            out_specs=[
                by_seq(half.shape),
                by_seq(half.shape),
                by_seq(own.shape),
                pl.BlockSpec((CHIPS_Y, 1) + shape[1:], lambda s, *_: (0, s, 0, 0)),
            ],
        ),
        compiler_params=pltpu.CompilerParams(vmem_limit_bytes=20 << 20),
        cost_estimate=pl.CostEstimate(
            flops=10 * seqs * 2 * 2 * rows * 10 * rows * HEAD_SIZE,
            transcendentals=0,
            bytes_accessed=8 << 20,
        ),
        name="attention_backward",
    )(scalars, mine, recv, *kvs, weights, attn, d_attn)


def local(query, key_states, value_state_rows, d_out, o_weight, doc_start):
    seq_count, shard_rows, query_width = query.shape
    ctx = lax.axis_index("ctx")
    tp = lax.axis_index("tp")
    core = ctx % CORES
    y = ctx // CORES % CHIPS_Y
    chip_pos = ctx // CORES * (CORES * shard_rows)
    scalars = jnp.stack([core, tp, y, chip_pos]).astype(jnp.int32)
    first = core == 0

    def halves(a):
        w = a.shape[-1] // 2
        return a[..., :w], a[..., w:]

    def head_share(core_zero):
        parts = [
            jnp.where(core_zero, *halves(a)) for a in (query, key_states, value_state_rows)
        ]
        return jnp.concatenate(parts, axis=-1)

    r3 = tp_ahead(d_out, 1)
    r1 = tp_ahead(d_out, -1)
    mine = head_share(first)
    recv = to_sibling(head_share(~first))
    doc_mine = doc_start[:, None, :]
    doc_recv = to_sibling(doc_mine)
    t0 = to_sibling(d_out)
    recv, doc_recv, t0 = lax.optimization_barrier((recv, doc_recv, t0))

    kv_width = 2 * HEAD_SIZE
    kv0 = jnp.concatenate([mine[..., -kv_width:], recv[..., -kv_width:]], axis=1)
    kv1, kv2, kv3 = (chips_ahead(kv0, d) for d in (1, 2, 3))
    own, own_t = early_projection(scalars, [d_out, t0], o_weight)

    r1, r3, own = lax.optimization_barrier((r1, r3, own))
    r2a = tp_ahead(r3[:1], 1)
    r2b = tp_ahead(r1[1:], -1)
    kv1, kv2, kv3, kv_again, r1, r3 = lax.optimization_barrier((kv1, kv2, kv3, kv0, r1, r3))
    kv4 = chips_ahead(kv_again, 4)
    t1, t3, kv4 = lax.optimization_barrier((to_sibling(r1), to_sibling(r3), kv4))
    near, near_t = early_projection(scalars, [r1, r3, t1, t3], o_weight)
    kv1, near, r2a, r2b = lax.optimization_barrier((kv1, near, r2a, r2b))
    kvs = [kv0, kv1, kv2, kv3, kv4]
    attn, weights = forward(scalars, mine, recv, kvs, doc_mine, doc_recv)
    d_attn, sent_a, kept_a, sent_b, kept_b = late_projection(
        scalars,
        [r2a, r2b, to_sibling(r2a), to_sibling(r2b)],
        [own_t, near_t],
        attn,
        [own, near],
        o_weight,
    )
    got_a = y_route(sent_a, y_pair)
    got_b = y_route(sent_b, y_mirror)
    dq_mine, dq_other, g_own, g_sent = backward(scalars, mine, recv, kvs, weights, attn, d_attn)
    dq_recv = to_sibling(dq_other)

    def added(*blocks):
        total = blocks[0].astype(jnp.float32)
        for block in blocks[1:]:
            total = total + block.astype(jnp.float32)
        return total

    next_a = added(kept_a[1], got_a[1]).astype(jnp.bfloat16)
    next_b = added(kept_b[1], got_b[1]).astype(jnp.bfloat16)
    next_a, next_b, g_sent = lax.optimization_barrier((next_a, next_b, g_sent))
    last_a = y_route(next_a, y_mirror)
    last_b = y_route(next_b, y_pair)
    g_columns = y_exchange(g_sent)
    w_sum = jnp.concatenate(
        [
            added(kept_a[0], got_a[0], last_a).astype(jnp.bfloat16),
            added(kept_b[0], got_b[0], last_b).astype(jnp.bfloat16),
        ],
        axis=0,
    )
    w_all = z_exchange(w_sum)

    g_before = jnp.zeros(g_own.shape, jnp.float32)
    grads = g_own
    for column in range(CHIPS_Y):
        block = g_columns[column].astype(jnp.float32)
        grads = grads + jnp.where(column > y, block, 0.0)
        g_before = g_before + jnp.where(column > y, 0.0, block)
    g_before = chips_ahead(g_before.astype(jnp.bfloat16), -HALO_CHIPS)
    grads = (grads + g_before.astype(jnp.float32)).astype(jnp.bfloat16)
    g_mine = grads[:, :shard_rows]
    g_recv = to_sibling(grads[:, shard_rows:])

    w_rows = jnp.sum(w_all.astype(jnp.float32), axis=0)
    half_rows = w_rows.shape[0] // 2
    w_top, w_bottom = w_rows[:half_rows], w_rows[half_rows:]
    w_mine = jnp.where(first, w_top, w_bottom)
    w_recv = to_sibling(jnp.where(first, w_bottom, w_top))

    def by_core(own, other):
        return jnp.concatenate(
            [jnp.where(first, own, other), jnp.where(first, other, own)], axis=-1
        )

    return (
        by_core(dq_mine, dq_recv),
        by_core(g_mine[..., :HEAD_SIZE], g_recv[..., :HEAD_SIZE]),
        by_core(g_mine[..., HEAD_SIZE:], g_recv[..., HEAD_SIZE:]),
        by_core(w_mine, w_recv),
    )


def solution(mesh):
    return jax.shard_map(
        local,
        mesh=mesh,
        in_specs=(
            P(None, "ctx", "tp"),
            P(None, "ctx", "tp"),
            P(None, "ctx", "tp"),
            P(None, ("ctx", "tp"), None),
            P(None, "tp"),
            P(None, "ctx"),
        ),
        out_specs=(
            P(None, "ctx", "tp"),
            P(None, "ctx", "tp"),
            P(None, "ctx", "tp"),
            P("ctx", "tp"),
        ),
        check_vma=False,
    )
```

```python
import jax
import jax.numpy as jnp
from jax import lax
from jax.experimental import pallas as pl
from jax.experimental.pallas import tpu as pltpu
from jax.sharding import PartitionSpec as P

HEAD_SIZE = 128
WIN = 1024
CORES = 2
CHIPS_Y = 4
CHIPS_Z = 8
TP = 4
LOG2_E = 1.4426950408889634

score_scale = 168.0 ** (-0.5)

NT = (((1,), (1,)), ((), ()))
TN = (((0,), (0,)), ((), ()))
NN = (((1,), (0,)), ((), ()))


def dot(a, b, dims=NN):
    return lax.dot_general(a, b, dims, preferred_element_type=jnp.float32)


def ctx_shift(block, move):
    count = CORES * CHIPS_Y * CHIPS_Z
    return lax.ppermute(block, "ctx", [(i, move(i)) for i in range(count)])


def to_sibling(block):
    return ctx_shift(block, lambda i: i ^ 1)


def y_pair(y):
    return y ^ 1


def y_mirror(y):
    return CHIPS_Y - 1 - y


def y_route(block, target, inner=False):
    route = []
    for i in range(CORES * CHIPS_Y * CHIPS_Z):
        core, y, z = i % CORES, i // CORES % CHIPS_Y, i // (CORES * CHIPS_Y)
        if not inner or 0 < y < CHIPS_Y - 1:
            route.append((i, (z * CHIPS_Y + target(y)) * CORES + core))
    return lax.ppermute(block, "ctx", route)


def y_exchange(blocks):
    groups = [
        [(z * CHIPS_Y + y) * CORES + core for y in range(CHIPS_Y)]
        for z in range(CHIPS_Z)
        for core in range(CORES)
    ]
    return lax.all_to_all(blocks, "ctx", 0, 0, axis_index_groups=groups, tiled=True)


def z_exchange(blocks):
    groups = [
        [(z * CHIPS_Y + y) * CORES + core for z in range(CHIPS_Z) for core in range(CORES)]
        for y in range(CHIPS_Y)
    ]
    return lax.all_to_all(blocks, "ctx", 0, 0, axis_index_groups=groups, tiled=True)


def y_ahead(block, distance):
    return y_route(block, lambda y: (y + distance) % CHIPS_Y)


def z_ahead(block, distance, other_core=False):
    count = CORES * CHIPS_Y * CHIPS_Z
    step = CORES * CHIPS_Y * distance
    return ctx_shift(block, lambda i: (i + step) % count ^ int(other_core))


def tp_ahead(block, distance):
    return lax.ppermute(block, "tp", [(i, (i + distance) % TP) for i in range(TP)])


def query_positions(core, chip_pos, rows):
    lane = lax.broadcasted_iota(jnp.int32, (1, 2 * rows), 1)
    other = lane >= rows
    first = jnp.where(other, (1 - core) * rows - rows, core * rows)
    return chip_pos + first + lane


def forward_kernel(scalars, mine, recv, kv0, kv1, kv2, kv3, kv4, doc_mine, doc_recv, attn, weights):
    core, chip_pos = scalars[0], scalars[3]
    rows = mine.shape[1]
    query_pos = query_positions(core, chip_pos, rows)
    doc = jnp.concatenate([doc_mine[0], doc_recv[0]], axis=1)
    lowest = jnp.maximum(doc, query_pos - (WIN - 1))
    index = lax.broadcasted_iota(jnp.int32, (2 * rows, 2 * rows), 0)
    offset = index + jnp.where(index >= rows, (1 - core) * rows - rows, core * rows)
    for h in range(2):
        cols = slice(h * HEAD_SIZE, (h + 1) * HEAD_SIZE)
        q = jnp.concatenate([mine[0, :, cols], recv[0, :, cols]], axis=0)
        scores = []
        for d, kv in enumerate((kv0, kv1, kv2, kv3, kv4)):
            s = dot(kv[0, :, :HEAD_SIZE], q, NT) * (score_scale * LOG2_E)
            key_pos = offset + (chip_pos - 2 * rows * d)
            visible = key_pos >= lowest
            if d == 0:
                visible = visible & (key_pos <= query_pos)
            scores.append(jnp.where(visible, s, -1e30))
        top = scores[0]
        for s in scores[1:]:
            top = jnp.maximum(top, s)
        top = jnp.max(top, axis=0, keepdims=True)
        expo = [jnp.exp2(s - top) for s in scores]
        total = expo[0]
        for e in expo[1:]:
            total = total + e
        inverse = 1.0 / jnp.sum(total, axis=0, keepdims=True)
        acc = None
        for d, kv in enumerate((kv0, kv1, kv2, kv3, kv4)):
            w = (expo[d] * inverse).astype(jnp.bfloat16)
            weights[0, h, 2 * rows * d : 2 * rows * (d + 1), :] = w
            part = dot(kv[0, :, HEAD_SIZE:], w, TN)
            acc = part if acc is None else acc + part
        attn[0, :, cols] = acc.T.astype(jnp.bfloat16)


def early_kernel(scalars, *refs):
    *pieces, o_weight, d_attn, rows_t, acc = refs
    step = pl.program_id(0)
    parts = [ref[seq] for ref in pieces for seq in range(ref.shape[0])]
    rows = jnp.concatenate(parts, axis=0)
    product = dot(rows, o_weight[...])

    @pl.when(step == 0)
    def _():
        acc[...] = product

    @pl.when(step > 0)
    def _():
        acc[...] = acc[...] + product

    rows_t[...] = rows.T

    @pl.when(step == pl.num_programs(0) - 1)
    def _():
        d_attn[...] = acc[...].astype(jnp.bfloat16)


def place(tp, piece, core_block, rel, seq):
    here = TP * piece * core_block + piece * ((tp + rel) % TP)
    return seq, pl.ds(pl.multiple_of(here, piece), piece)


OWN_SLOTS = [(b, 0, q) for b in range(2) for q in range(2)]
NEAR_SLOTS = [(b, s, q) for b in range(2) for s in (1, 3) for q in range(2)]
FAR_SLOTS = [(b, 2, q) for b in range(2) for q in range(2)]


def late_kernel(
    scalars, r2a, r2b, t2a, t2b, own_t, near_t, attn, own, near, o_weight,
    d_attn, sent_a, kept_a, sent_b, kept_b, acc, attn_own, attn_near, attn_far, partial,
):
    step = pl.program_id(0)
    tp, y = scalars[1], scalars[2]
    piece = r2a.shape[1]
    out_rows = sent_a.shape[2]

    @pl.when(step == 0)
    def _():
        for slots, kept in ((OWN_SLOTS, attn_own), (NEAR_SLOTS, attn_near), (FAR_SLOTS, attn_far)):
            for n, slot in enumerate(slots):
                seq, here = place(tp, piece, *slot)
                kept[n * piece : (n + 1) * piece, :] = attn[seq, here, :]
        for slots, done in ((OWN_SLOTS, own), (NEAR_SLOTS, near)):
            for n, slot in enumerate(slots):
                seq, here = place(tp, piece, *slot)
                d_attn[seq, here, :] = done[n * piece : (n + 1) * piece, :]

    rows = jnp.concatenate([r2a[0], r2b[0], t2a[0], t2b[0]], axis=0)
    partial[...] = (
        dot(own_t[...], attn_own[...])
        + dot(near_t[...], attn_near[...])
        + dot(rows.T, attn_far[...])
    )

    def emit(out, order):
        for n, target in enumerate(order):
            for z in range(out.shape[1]):
                start = pl.multiple_of((CHIPS_Y * z + target) * out_rows, 8)
                out[n, z] = partial[pl.ds(start, out_rows), :].astype(jnp.bfloat16)

    pair = y + 1 - 2 * (y % 2)
    mirror = CHIPS_Y - 1 - y
    mirror_pair = mirror + 1 - 2 * (mirror % 2)

    product = dot(rows, o_weight[...])

    @pl.when(step == 0)
    def _():
        emit(sent_a, (pair, CHIPS_Y - 1 - pair))
        emit(kept_a, (y, mirror))
        acc[...] = product

    @pl.when(step == 1)
    def _():
        emit(sent_b, (mirror, mirror_pair))
        emit(kept_b, (y, pair))
        total = (acc[...] + product).astype(jnp.bfloat16)
        for n, slot in enumerate(FAR_SLOTS):
            seq, here = place(tp, piece, *slot)
            d_attn[seq, here, :] = total[n * piece : (n + 1) * piece, :]


def backward_kernel(
    mine, recv, kv0, kv1, kv2, kv3, kv4, weights, attn, d_attn,
    dq_mine, dq_other, g_own, g1, g2, g3, g4,
):
    rows = mine.shape[1]
    heads = []
    for h in range(2):
        cols = slice(h * HEAD_SIZE, (h + 1) * HEAD_SIZE)
        q = jnp.concatenate([mine[0, :, cols], recv[0, :, cols]], axis=0)
        da = d_attn[0, :, cols]
        product = da.astype(jnp.float32) * attn[0, :, cols].astype(jnp.float32)
        delta = jnp.sum(product.T, axis=0, keepdims=True)
        heads.append((q, da, delta))
    dq = [None, None]
    grads = (g_own, g1, g2, g3, g4)
    for kv_index, (kv, grad) in enumerate(zip((kv0, kv1, kv2, kv3, kv4), grads)):
        keys = kv[0, :, :HEAD_SIZE]
        values = kv[0, :, HEAD_SIZE:]
        dk = dv = None
        for h, (q, da, delta) in enumerate(heads):
            w = weights[0, h, 2 * rows * kv_index : 2 * rows * (kv_index + 1), :]
            dp = dot(values, da, NT)
            ds = (w.astype(jnp.float32) * (dp - delta)).astype(jnp.bfloat16)
            v_part = dot(w, da)
            k_part = dot(ds, q)
            q_part = dot(keys, ds, TN)
            dv = v_part if dv is None else dv + v_part
            dk = k_part if dk is None else dk + k_part
            dq[h] = q_part if dq[h] is None else dq[h] + q_part
        grad[0, :, :HEAD_SIZE] = (dk * score_scale).astype(grad.dtype)
        grad[0, :, HEAD_SIZE:] = dv.astype(grad.dtype)
    for h in range(2):
        cols = slice(h * HEAD_SIZE, (h + 1) * HEAD_SIZE)
        full = (dq[h].T * score_scale).astype(jnp.bfloat16)
        dq_mine[0, :, cols] = full[:rows]
        dq_other[0, :, cols] = full[rows:]


def merge_kernel(kept_a, got_a, last_a, kept_b, got_b, last_b, out):
    half = kept_a.shape[1]
    rows = out.shape[1]
    for part, (kept, got, last) in enumerate(((kept_a, got_a, last_a), (kept_b, got_b, last_b))):
        for z in range(half):
            total = (
                kept[0, z].astype(jnp.float32)
                + got[0, z].astype(jnp.float32)
                + last[z].astype(jnp.float32)
            )
            for core in range(CORES):
                slot = CORES * (half * part + z) + core
                out[slot] = total[core * rows : (core + 1) * rows].astype(jnp.bfloat16)


def finish_kernel(blocks, out):
    width = blocks.shape[2]
    for core in range(CORES):
        total = blocks[core].astype(jnp.float32)
        for z in range(1, CHIPS_Z):
            total = total + blocks[CORES * z + core].astype(jnp.float32)
        out[:, core * width : (core + 1) * width] = total


def merge(kept_a, got_a, last_a, kept_b, got_b, last_b):
    _, half, rows, width = kept_a.shape
    front = pl.BlockSpec((1, half, rows, width), lambda i: (0, 0, 0, 0))
    flat = pl.BlockSpec((half, rows, width), lambda i: (0, 0, 0))
    shape = (CORES * 2 * half, rows // CORES, width)
    return pl.pallas_call(
        merge_kernel,
        out_shape=jax.ShapeDtypeStruct(shape, jnp.bfloat16),
        grid=(1,),
        in_specs=[front, front, flat] * 2,
        out_specs=pl.BlockSpec(shape, lambda i: (0, 0, 0)),
        compiler_params=pltpu.CompilerParams(vmem_limit_bytes=16 << 20),
        name="projection_merge",
    )(kept_a, got_a, last_a, kept_b, got_b, last_b)


def finish(blocks):
    count, rows, width = blocks.shape
    return pl.pallas_call(
        finish_kernel,
        out_shape=jax.ShapeDtypeStruct((rows, CORES * width), jnp.float32),
        name="projection_finish",
    )(blocks)


def by_seq(shape):
    return pl.BlockSpec((1,) + shape[1:], lambda s, *_: (s,) + (0,) * (len(shape) - 1))


def forward(scalars, mine, recv, kvs, doc_mine, doc_recv):
    seqs, rows, width = mine.shape
    keys = 2 * rows * len(kvs)
    outs = (
        jax.ShapeDtypeStruct((seqs, 2 * rows, width // 2), jnp.bfloat16),
        jax.ShapeDtypeStruct((seqs, 2, keys, 2 * rows), jnp.bfloat16),
    )
    query_spec = pl.BlockSpec((1, rows, width // 2), lambda s, *_: (s, 0, 0))
    return pl.pallas_call(
        forward_kernel,
        out_shape=outs,
        grid_spec=pltpu.PrefetchScalarGridSpec(
            num_scalar_prefetch=1,
            grid=(seqs,),
            in_specs=[query_spec, query_spec]
            + [by_seq(kv.shape) for kv in kvs]
            + [by_seq(doc_mine.shape), by_seq(doc_recv.shape)],
            out_specs=[by_seq(o.shape) for o in outs],
        ),
        compiler_params=pltpu.CompilerParams(vmem_limit_bytes=20 << 20),
        cost_estimate=pl.CostEstimate(
            flops=4 * seqs * 2 * 2 * rows * keys * HEAD_SIZE,
            transcendentals=seqs * 2 * 2 * rows * keys,
            bytes_accessed=8 << 20,
        ),
        name="attention_forward",
    )(scalars, mine, recv, *kvs, doc_mine, doc_recv)


def early_projection(scalars, pieces, o_weight):
    rows = sum(p.shape[0] * p.shape[1] for p in pieces)
    features, both = o_weight.shape
    width = both // 2
    steps = 7
    block = features // steps
    outs = (
        jax.ShapeDtypeStruct((rows, width), jnp.bfloat16),
        jax.ShapeDtypeStruct((features, rows), jnp.bfloat16),
    )
    return pl.pallas_call(
        early_kernel,
        out_shape=outs,
        grid_spec=pltpu.PrefetchScalarGridSpec(
            num_scalar_prefetch=1,
            grid=(steps,),
            in_specs=[pl.BlockSpec(p.shape[:2] + (block,), lambda i, *_: (0, 0, i)) for p in pieces]
            + [pl.BlockSpec((block, width), lambda i, scalars: (i, scalars[0]))],
            out_specs=[
                pl.BlockSpec((rows, width), lambda i, *_: (0, 0)),
                pl.BlockSpec((block, rows), lambda i, *_: (i, 0)),
            ],
            scratch_shapes=[pltpu.VMEM((rows, width), jnp.float32)],
        ),
        compiler_params=pltpu.CompilerParams(vmem_limit_bytes=16 << 20),
        cost_estimate=pl.CostEstimate(
            flops=20 * rows * features * width, transcendentals=0, bytes_accessed=12 << 20
        ),
        name="projection_early",
    )(scalars, *pieces, o_weight)


def late_projection(scalars, pieces, rows_t, attn, early, o_weight):
    width = attn.shape[-1]
    features = o_weight.shape[0]
    late_rows = sum(p.shape[0] * p.shape[1] for p in pieces)
    steps = 2
    block = features // steps
    out_rows = features // (CHIPS_Y * CHIPS_Z)
    slab = jax.ShapeDtypeStruct((2, CHIPS_Z // 2, out_rows, width), jnp.bfloat16)

    def whole(a):
        return pl.BlockSpec(a.shape, lambda i, *_: (0,) * len(a.shape))

    return pl.pallas_call(
        late_kernel,
        out_shape=(jax.ShapeDtypeStruct(attn.shape, jnp.bfloat16),) + (slab,) * 4,
        grid_spec=pltpu.PrefetchScalarGridSpec(
            num_scalar_prefetch=1,
            grid=(steps,),
            in_specs=[pl.BlockSpec(p.shape[:2] + (block,), lambda i, *_: (0, 0, i)) for p in pieces]
            + [pl.BlockSpec((block, r.shape[1]), lambda i, *_: (i, 0)) for r in rows_t]
            + [whole(attn)]
            + [whole(e) for e in early]
            + [pl.BlockSpec((block, width), lambda i, scalars: (i, scalars[0]))],
            out_specs=[whole(attn)] + [whole(slab)] * 4,
            scratch_shapes=[pltpu.VMEM((late_rows, width), jnp.float32)]
            + [pltpu.VMEM((r.shape[1], width), jnp.bfloat16) for r in rows_t]
            + [
                pltpu.VMEM((late_rows, width), jnp.bfloat16),
                pltpu.VMEM((block, width), jnp.float32),
            ],
        ),
        compiler_params=pltpu.CompilerParams(vmem_limit_bytes=32 << 20),
        cost_estimate=pl.CostEstimate(
            flops=2 * 6 * late_rows * features * width, transcendentals=0, bytes_accessed=12 << 20
        ),
        name="projection_late",
    )(scalars, *pieces, *rows_t, attn, *early, o_weight)


def backward(mine, recv, kvs, weights, attn, d_attn):
    seqs, rows, width = mine.shape
    half = jax.ShapeDtypeStruct((seqs, rows, width // 2), jnp.bfloat16)
    shape = kvs[0].shape
    own = jax.ShapeDtypeStruct(shape, jnp.float32)
    sent = jax.ShapeDtypeStruct(shape, jnp.bfloat16)
    outs = (half, half, own) + (sent,) * (len(kvs) - 1)
    query_spec = pl.BlockSpec((1, rows, width // 2), lambda s, *_: (s, 0, 0))
    return pl.pallas_call(
        backward_kernel,
        out_shape=outs,
        grid=(seqs,),
        in_specs=[query_spec, query_spec]
        + [by_seq(a.shape) for a in (*kvs, weights, attn, d_attn)],
        out_specs=[by_seq(o.shape) for o in outs],
        compiler_params=pltpu.CompilerParams(vmem_limit_bytes=20 << 20),
        cost_estimate=pl.CostEstimate(
            flops=10 * seqs * 2 * 2 * rows * 10 * rows * HEAD_SIZE,
            transcendentals=0,
            bytes_accessed=8 << 20,
        ),
        name="attention_backward",
    )(mine, recv, *kvs, weights, attn, d_attn)


def local(query, key_states, value_state_rows, d_out, o_weight, doc_start):
    seq_count, shard_rows, query_width = query.shape
    ctx = lax.axis_index("ctx")
    tp = lax.axis_index("tp")
    core = ctx % CORES
    y = ctx // CORES % CHIPS_Y
    chip_pos = ctx // CORES * (CORES * shard_rows)
    scalars = jnp.stack([core, tp, y, chip_pos]).astype(jnp.int32)
    first = core == 0

    def halves(a):
        w = a.shape[-1] // 2
        return a[..., :w], a[..., w:]

    def head_share(core_zero):
        parts = [
            jnp.where(core_zero, *halves(a)) for a in (query, key_states, value_state_rows)
        ]
        return jnp.concatenate(parts, axis=-1)

    kv_width = 2 * HEAD_SIZE
    first_seq, second_seq = d_out[:1], d_out[1:]
    r3a = tp_ahead(first_seq, 1)
    r1b = tp_ahead(second_seq, -1)
    mine = head_share(first)
    shared = head_share(~first)
    z_same = z_ahead(mine[..., -kv_width:], 1)
    z_other = z_ahead(shared[..., -kv_width:], 1, other_core=True)
    recv = to_sibling(shared)
    z_same, z_other, recv, r3a, r1b, first_seq, second_seq, doc_mine, rows = (
        lax.optimization_barrier(
            (z_same, z_other, recv, r3a, r1b, first_seq, second_seq, doc_start[:, None, :], d_out)
        )
    )
    r3b = tp_ahead(second_seq, 1)
    r1a = tp_ahead(first_seq, -1)
    doc_recv = to_sibling(doc_mine)
    t0 = to_sibling(rows)
    kv0 = jnp.concatenate([mine[..., -kv_width:], recv[..., -kv_width:]], axis=1)
    kv4 = jnp.concatenate([z_same, z_other], axis=1)
    kv1, kv3 = (y_ahead(jnp.where(y + d < CHIPS_Y, kv0, kv4), d) for d in (1, CHIPS_Y - 1))
    own, own_t = early_projection(scalars, [d_out, t0], o_weight)

    near_rows = [r1a, r1b, r3a, r3b]
    *near_rows, kv1, kv3, own, doc_recv = lax.optimization_barrier(
        (*near_rows, kv1, kv3, own, doc_recv)
    )
    low = y_route(kv3, lambda y: y - 1, inner=True)
    high = y_route(kv1, lambda y: y + 1, inner=True)
    r2a = tp_ahead(near_rows[2], 1)
    r2b = tp_ahead(near_rows[1], -1)
    near_rows = near_rows + [to_sibling(r) for r in near_rows]
    kv2 = jnp.where(y < CHIPS_Y // 2, low, high)
    near, near_t = early_projection(scalars, near_rows, o_weight)
    near, r2a, r2b = lax.optimization_barrier((near, r2a, r2b))
    kvs = [kv0, kv1, kv2, kv3, kv4]
    attn, weights = forward(scalars, mine, recv, kvs, doc_mine, doc_recv)
    d_attn, sent_a, kept_a, sent_b, kept_b = late_projection(
        scalars,
        [r2a, r2b, to_sibling(r2a), to_sibling(r2b)],
        [own_t, near_t],
        attn,
        [own, near],
        o_weight,
    )
    got_a = y_route(sent_a, y_pair)
    got_b = y_route(sent_b, y_mirror)
    dq_mine, dq_other, g_own, *g_sent, g_before = backward(
        mine, recv, kvs, weights, attn, d_attn
    )
    got_a, got_b, g_own = lax.optimization_barrier((got_a, got_b, g_own))
    dq_recv = to_sibling(dq_other)

    def added(*blocks):
        total = blocks[0].astype(jnp.float32)
        for block in blocks[1:]:
            total = total + block.astype(jnp.float32)
        return total

    next_a = added(kept_a[1], got_a[1]).astype(jnp.bfloat16)
    next_b = added(kept_b[1], got_b[1]).astype(jnp.bfloat16)
    last_a = y_route(next_a, y_mirror)
    last_b = y_route(next_b, y_pair)
    w_sum = merge(kept_a, got_a, last_a, kept_b, got_b, last_b)
    w_sum, g_sent = lax.optimization_barrier((w_sum, g_sent))
    w_all = z_exchange(w_sum)

    grads = g_own
    g_before = g_before.astype(jnp.float32)
    for d, sent in enumerate(g_sent, 1):
        block = y_ahead(sent, -d).astype(jnp.float32)
        here = y + d < CHIPS_Y
        grads = grads + jnp.where(here, block, 0.0)
        g_before = g_before + jnp.where(here, 0.0, block)
    g_before = g_before.astype(jnp.bfloat16)
    z_same = z_ahead(g_before[:, :shard_rows], -1)
    z_other = z_ahead(g_before[:, shard_rows:], -1, other_core=True)
    sibling = to_sibling(grads[:, shard_rows:].astype(jnp.bfloat16))
    g_mine = added(grads[:, :shard_rows], z_same).astype(jnp.bfloat16)
    g_recv = added(sibling, z_other).astype(jnp.bfloat16)

    def by_core(own, other):
        return jnp.concatenate(
            [jnp.where(first, own, other), jnp.where(first, other, own)], axis=-1
        )

    return (
        by_core(dq_mine, dq_recv),
        by_core(g_mine[..., :HEAD_SIZE], g_recv[..., :HEAD_SIZE]),
        by_core(g_mine[..., HEAD_SIZE:], g_recv[..., HEAD_SIZE:]),
        finish(w_all),
    )


def solution(mesh):
    return jax.shard_map(
        local,
        mesh=mesh,
        in_specs=(
            P(None, "ctx", "tp"),
            P(None, "ctx", "tp"),
            P(None, "ctx", "tp"),
            P(None, ("ctx", "tp"), None),
            P(None, "tp"),
            P(None, "ctx"),
        ),
        out_specs=(
            P(None, "ctx", "tp"),
            P(None, "ctx", "tp"),
            P(None, "ctx", "tp"),
            P("ctx", "tp"),
        ),
        check_vma=False,
    )
```

```python
import jax
import jax.numpy as jnp
from jax import lax
from jax.experimental import pallas as pl
from jax.experimental.pallas import tpu as pltpu
from jax.sharding import PartitionSpec as P

HEAD_SIZE = 128
WIN = 1024
CORES = 2
CHIPS_Y = 4
CHIPS_Z = 8
TP = 4
LOG2_E = 1.4426950408889634

score_scale = 168.0 ** (-0.5)

NT = (((1,), (1,)), ((), ()))
TN = (((0,), (0,)), ((), ()))
NN = (((1,), (0,)), ((), ()))


def dot(a, b, dims=NN):
    return lax.dot_general(a, b, dims, preferred_element_type=jnp.float32)


def ctx_shift(block, move):
    count = CORES * CHIPS_Y * CHIPS_Z
    return lax.ppermute(block, "ctx", [(i, move(i)) for i in range(count)])


def to_sibling(block):
    return ctx_shift(block, lambda i: i ^ 1)


def y_pair(y):
    return y ^ 1


def y_mirror(y):
    return CHIPS_Y - 1 - y


def y_route(block, target, inner=False):
    route = []
    for i in range(CORES * CHIPS_Y * CHIPS_Z):
        core, y, z = i % CORES, i // CORES % CHIPS_Y, i // (CORES * CHIPS_Y)
        if not inner or 0 < y < CHIPS_Y - 1:
            route.append((i, (z * CHIPS_Y + target(y)) * CORES + core))
    return lax.ppermute(block, "ctx", route)


def y_exchange(blocks):
    groups = [
        [(z * CHIPS_Y + y) * CORES + core for y in range(CHIPS_Y)]
        for z in range(CHIPS_Z)
        for core in range(CORES)
    ]
    return lax.all_to_all(blocks, "ctx", 0, 0, axis_index_groups=groups, tiled=True)


def z_exchange(blocks):
    groups = [
        [(z * CHIPS_Y + y) * CORES + core for z in range(CHIPS_Z) for core in range(CORES)]
        for y in range(CHIPS_Y)
    ]
    return lax.all_to_all(blocks, "ctx", 0, 0, axis_index_groups=groups, tiled=True)


def y_ahead(block, distance):
    return y_route(block, lambda y: (y + distance) % CHIPS_Y)


def z_ahead(block, distance, other_core=False):
    count = CORES * CHIPS_Y * CHIPS_Z
    step = CORES * CHIPS_Y * distance
    return ctx_shift(block, lambda i: (i + step) % count ^ int(other_core))


def tp_ahead(block, distance):
    return lax.ppermute(block, "tp", [(i, (i + distance) % TP) for i in range(TP)])


def query_positions(core, chip_pos, rows):
    lane = lax.broadcasted_iota(jnp.int32, (1, 2 * rows), 1)
    other = lane >= rows
    first = jnp.where(other, (1 - core) * rows - rows, core * rows)
    return chip_pos + first + lane


def key_values(y, kv0, kv1, low, high, kv3, kv4):
    kv2 = jnp.where(y < CHIPS_Y // 2, low[0], high[0])
    return kv0[0], kv1[0], kv2, kv3[0], kv4[0]


def forward_kernel(
    scalars, mine, recv, kv0, kv1, low, high, kv3, kv4, doc_mine, doc_recv, attn, weights
):
    core, y, chip_pos = scalars[0], scalars[2], scalars[3]
    kvs = key_values(y, kv0, kv1, low, high, kv3, kv4)
    rows = mine.shape[1]
    query_pos = query_positions(core, chip_pos, rows)
    doc = jnp.concatenate([doc_mine[0], doc_recv[0]], axis=1)
    lowest = jnp.maximum(doc, query_pos - (WIN - 1))
    index = lax.broadcasted_iota(jnp.int32, (2 * rows, 2 * rows), 0)
    offset = index + jnp.where(index >= rows, (1 - core) * rows - rows, core * rows)
    for h in range(2):
        cols = slice(h * HEAD_SIZE, (h + 1) * HEAD_SIZE)
        q = jnp.concatenate([mine[0, :, cols], recv[0, :, cols]], axis=0)
        scores = []
        for d, kv in enumerate(kvs):
            s = dot(kv[:, :HEAD_SIZE], q, NT) * (score_scale * LOG2_E)
            key_pos = offset + (chip_pos - 2 * rows * d)
            visible = key_pos >= lowest
            if d == 0:
                visible = visible & (key_pos <= query_pos)
            scores.append(jnp.where(visible, s, -1e30))
        top = scores[0]
        for s in scores[1:]:
            top = jnp.maximum(top, s)
        top = jnp.max(top, axis=0, keepdims=True)
        expo = [jnp.exp2(s - top) for s in scores]
        total = expo[0]
        for e in expo[1:]:
            total = total + e
        inverse = 1.0 / jnp.sum(total, axis=0, keepdims=True)
        acc = None
        for d, kv in enumerate(kvs):
            w = (expo[d] * inverse).astype(jnp.bfloat16)
            weights[0, h, 2 * rows * d : 2 * rows * (d + 1), :] = w
            part = dot(kv[:, HEAD_SIZE:], w, TN)
            acc = part if acc is None else acc + part
        attn[0, :, cols] = acc.T.astype(jnp.bfloat16)


def early_kernel(scalars, *refs):
    *pieces, o_weight, d_attn, rows_t, acc = refs
    step = pl.program_id(0)
    parts = [ref[seq] for ref in pieces for seq in range(ref.shape[0])]
    rows = jnp.concatenate(parts, axis=0)
    product = dot(rows, o_weight[...])

    @pl.when(step == 0)
    def _():
        acc[...] = product

    @pl.when(step > 0)
    def _():
        acc[...] = acc[...] + product

    rows_t[...] = rows.T

    @pl.when(step == pl.num_programs(0) - 1)
    def _():
        d_attn[...] = acc[...].astype(jnp.bfloat16)


def place(tp, piece, core_block, rel, seq):
    here = TP * piece * core_block + piece * ((tp + rel) % TP)
    return seq, pl.ds(pl.multiple_of(here, piece), piece)


OWN_SLOTS = [(b, 0, q) for b in range(2) for q in range(2)]
NEAR_SLOTS = [(b, s, q) for b in range(2) for s in (1, 3) for q in range(2)]
FAR_SLOTS = [(b, 2, q) for b in range(2) for q in range(2)]


def late_kernel(
    scalars, r2a, r2b, t2a, t2b, own_t, near_t, attn, own, near, o_weight,
    d_attn, sent_a, kept_a, sent_b, kept_b, acc, attn_own, attn_near, attn_far, partial,
):
    step = pl.program_id(0)
    tp, y = scalars[1], scalars[2]
    piece = r2a.shape[1]
    out_rows = sent_a.shape[2]

    @pl.when(step == 0)
    def _():
        for slots, kept in ((OWN_SLOTS, attn_own), (NEAR_SLOTS, attn_near), (FAR_SLOTS, attn_far)):
            for n, slot in enumerate(slots):
                seq, here = place(tp, piece, *slot)
                kept[n * piece : (n + 1) * piece, :] = attn[seq, here, :]
        for slots, done in ((OWN_SLOTS, own), (NEAR_SLOTS, near)):
            for n, slot in enumerate(slots):
                seq, here = place(tp, piece, *slot)
                d_attn[seq, here, :] = done[n * piece : (n + 1) * piece, :]

    rows = jnp.concatenate([r2a[0], r2b[0], t2a[0], t2b[0]], axis=0)
    partial[...] = (
        dot(own_t[...], attn_own[...])
        + dot(near_t[...], attn_near[...])
        + dot(rows.T, attn_far[...])
    )

    def emit(out, order):
        for n, target in enumerate(order):
            for z in range(out.shape[1]):
                start = pl.multiple_of((CHIPS_Y * z + target) * out_rows, 8)
                out[n, z] = partial[pl.ds(start, out_rows), :].astype(jnp.bfloat16)

    pair = y + 1 - 2 * (y % 2)
    mirror = CHIPS_Y - 1 - y
    mirror_pair = mirror + 1 - 2 * (mirror % 2)

    product = dot(rows, o_weight[...])

    @pl.when(step == 0)
    def _():
        emit(sent_a, (pair, CHIPS_Y - 1 - pair))
        emit(kept_a, (y, mirror))
        acc[...] = product

    @pl.when(step == 1)
    def _():
        emit(sent_b, (mirror, mirror_pair))
        emit(kept_b, (y, pair))
        total = (acc[...] + product).astype(jnp.bfloat16)
        for n, slot in enumerate(FAR_SLOTS):
            seq, here = place(tp, piece, *slot)
            d_attn[seq, here, :] = total[n * piece : (n + 1) * piece, :]


def backward_kernel(
    scalars, mine, recv, kv0, kv1, low, high, kv3, kv4, weights, attn, d_attn,
    dq_mine, dq_other, g_own, g1, g2, g3, g4,
):
    rows = mine.shape[1]
    kvs = key_values(scalars[2], kv0, kv1, low, high, kv3, kv4)
    heads = []
    for h in range(2):
        cols = slice(h * HEAD_SIZE, (h + 1) * HEAD_SIZE)
        q = jnp.concatenate([mine[0, :, cols], recv[0, :, cols]], axis=0)
        da = d_attn[0, :, cols]
        product = da.astype(jnp.float32) * attn[0, :, cols].astype(jnp.float32)
        delta = jnp.sum(product.T, axis=0, keepdims=True)
        heads.append((q, da, delta))
    dq = [None, None]
    grads = (g_own, g1, g2, g3, g4)
    for kv_index, (kv, grad) in enumerate(zip(kvs, grads)):
        keys = kv[:, :HEAD_SIZE]
        values = kv[:, HEAD_SIZE:]
        dk = dv = None
        for h, (q, da, delta) in enumerate(heads):
            w = weights[0, h, 2 * rows * kv_index : 2 * rows * (kv_index + 1), :]
            dp = dot(values, da, NT)
            ds = (w.astype(jnp.float32) * (dp - delta)).astype(jnp.bfloat16)
            v_part = dot(w, da)
            k_part = dot(ds, q)
            q_part = dot(keys, ds, TN)
            dv = v_part if dv is None else dv + v_part
            dk = k_part if dk is None else dk + k_part
            dq[h] = q_part if dq[h] is None else dq[h] + q_part
        grad[0, :, :HEAD_SIZE] = (dk * score_scale).astype(grad.dtype)
        grad[0, :, HEAD_SIZE:] = dv.astype(grad.dtype)
    for h in range(2):
        cols = slice(h * HEAD_SIZE, (h + 1) * HEAD_SIZE)
        full = (dq[h].T * score_scale).astype(jnp.bfloat16)
        dq_mine[0, :, cols] = full[:rows]
        dq_other[0, :, cols] = full[rows:]


def merge_kernel(kept_a, got_a, last_a, kept_b, got_b, last_b, out):
    half = kept_a.shape[1]
    rows = out.shape[1]
    for part, (kept, got, last) in enumerate(((kept_a, got_a, last_a), (kept_b, got_b, last_b))):
        for z in range(half):
            total = (
                kept[0, z].astype(jnp.float32)
                + got[0, z].astype(jnp.float32)
                + last[z].astype(jnp.float32)
            )
            for core in range(CORES):
                slot = CORES * (half * part + z) + core
                out[slot] = total[core * rows : (core + 1) * rows].astype(jnp.bfloat16)


def finish_kernel(blocks, out):
    width = blocks.shape[2]
    for core in range(CORES):
        total = blocks[core].astype(jnp.float32)
        for z in range(1, CHIPS_Z):
            total = total + blocks[CORES * z + core].astype(jnp.float32)
        out[:, core * width : (core + 1) * width] = total


def merge(kept_a, got_a, last_a, kept_b, got_b, last_b):
    _, half, rows, width = kept_a.shape
    front = pl.BlockSpec((1, half, rows, width), lambda i: (0, 0, 0, 0))
    flat = pl.BlockSpec((half, rows, width), lambda i: (0, 0, 0))
    shape = (CORES * 2 * half, rows // CORES, width)
    return pl.pallas_call(
        merge_kernel,
        out_shape=jax.ShapeDtypeStruct(shape, jnp.bfloat16),
        grid=(1,),
        in_specs=[front, front, flat] * 2,
        out_specs=pl.BlockSpec(shape, lambda i: (0, 0, 0)),
        compiler_params=pltpu.CompilerParams(vmem_limit_bytes=16 << 20),
        name="projection_merge",
    )(kept_a, got_a, last_a, kept_b, got_b, last_b)


def finish(blocks):
    count, rows, width = blocks.shape
    return pl.pallas_call(
        finish_kernel,
        out_shape=jax.ShapeDtypeStruct((rows, CORES * width), jnp.float32),
        compiler_params=pltpu.CompilerParams(vmem_limit_bytes=16 << 20),
        name="projection_finish",
    )(blocks)


def split_kernel(
    scalars, q_own, q_other, k_own, k_other, v_own, v_other,
    q_mine, sent, kv_mine, kv_sent,
):
    width = q_other.shape[2]
    q_mine[...] = q_own[...]
    sent[:, :, :width] = q_other[...]
    sent[:, :, width : width + HEAD_SIZE] = k_other[...]
    sent[:, :, width + HEAD_SIZE :] = v_other[...]
    kv_mine[:, :, :HEAD_SIZE] = k_own[...]
    kv_mine[:, :, HEAD_SIZE:] = v_own[...]
    kv_sent[:, :, :HEAD_SIZE] = k_other[...]
    kv_sent[:, :, HEAD_SIZE:] = v_other[...]


def split_heads(scalars, query, keys, values):
    seqs, rows, width = query.shape
    out = jax.ShapeDtypeStruct((seqs, rows, width // 2), jnp.bfloat16)
    whole = jax.ShapeDtypeStruct(query.shape, jnp.bfloat16)
    outs = (out, whole, out, out)

    def half(a):
        shape = a.shape[:2] + (a.shape[2] // 2,)
        return [
            pl.BlockSpec(shape, lambda i, scalars: (0, 0, scalars[0])),
            pl.BlockSpec(shape, lambda i, scalars: (0, 0, 1 - scalars[0])),
        ]

    return pl.pallas_call(
        split_kernel,
        out_shape=outs,
        grid_spec=pltpu.PrefetchScalarGridSpec(
            num_scalar_prefetch=1,
            grid=(1,),
            in_specs=half(query) + half(keys) + half(values),
            out_specs=[pl.BlockSpec(o.shape, lambda i, *_: (0, 0, 0)) for o in outs],
        ),
        compiler_params=pltpu.CompilerParams(vmem_limit_bytes=16 << 20),
        name="split_heads",
    )(scalars, query, query, keys, keys, values, values)


def by_seq(shape):
    return pl.BlockSpec((1,) + shape[1:], lambda s, *_: (s,) + (0,) * (len(shape) - 1))


def forward(scalars, mine, recv, kvs, doc_mine, doc_recv):
    seqs, rows, width = mine.shape
    keys = 2 * rows * (len(kvs) - 1)
    outs = (
        jax.ShapeDtypeStruct((seqs, 2 * rows, width), jnp.bfloat16),
        jax.ShapeDtypeStruct((seqs, 2, keys, 2 * rows), jnp.bfloat16),
    )
    query_spec = by_seq(mine.shape)
    recv_spec = pl.BlockSpec((1, rows, width), lambda s, *_: (s, 0, 0))
    return pl.pallas_call(
        forward_kernel,
        out_shape=outs,
        grid_spec=pltpu.PrefetchScalarGridSpec(
            num_scalar_prefetch=1,
            grid=(seqs,),
            in_specs=[query_spec, recv_spec]
            + [by_seq(kv.shape) for kv in kvs]
            + [by_seq(doc_mine.shape), by_seq(doc_recv.shape)],
            out_specs=[by_seq(o.shape) for o in outs],
        ),
        compiler_params=pltpu.CompilerParams(vmem_limit_bytes=20 << 20),
        cost_estimate=pl.CostEstimate(
            flops=4 * seqs * 2 * 2 * rows * keys * HEAD_SIZE,
            transcendentals=seqs * 2 * 2 * rows * keys,
            bytes_accessed=8 << 20,
        ),
        name="attention_forward",
    )(scalars, mine, recv, *kvs, doc_mine, doc_recv)


def early_projection(scalars, pieces, o_weight):
    rows = sum(p.shape[0] * p.shape[1] for p in pieces)
    features, both = o_weight.shape
    width = both // 2
    steps = 7
    block = features // steps
    outs = (
        jax.ShapeDtypeStruct((rows, width), jnp.bfloat16),
        jax.ShapeDtypeStruct((features, rows), jnp.bfloat16),
    )
    return pl.pallas_call(
        early_kernel,
        out_shape=outs,
        grid_spec=pltpu.PrefetchScalarGridSpec(
            num_scalar_prefetch=1,
            grid=(steps,),
            in_specs=[pl.BlockSpec(p.shape[:2] + (block,), lambda i, *_: (0, 0, i)) for p in pieces]
            + [pl.BlockSpec((block, width), lambda i, scalars: (i, scalars[0]))],
            out_specs=[
                pl.BlockSpec((rows, width), lambda i, *_: (0, 0)),
                pl.BlockSpec((block, rows), lambda i, *_: (i, 0)),
            ],
            scratch_shapes=[pltpu.VMEM((rows, width), jnp.float32)],
        ),
        compiler_params=pltpu.CompilerParams(vmem_limit_bytes=16 << 20),
        cost_estimate=pl.CostEstimate(
            flops=20 * rows * features * width, transcendentals=0, bytes_accessed=12 << 20
        ),
        name="projection_early",
    )(scalars, *pieces, o_weight)


def late_projection(scalars, pieces, rows_t, attn, early, o_weight):
    width = attn.shape[-1]
    features = o_weight.shape[0]
    late_rows = sum(p.shape[0] * p.shape[1] for p in pieces)
    steps = 2
    block = features // steps
    out_rows = features // (CHIPS_Y * CHIPS_Z)
    slab = jax.ShapeDtypeStruct((2, CHIPS_Z // 2, out_rows, width), jnp.bfloat16)

    def whole(a):
        return pl.BlockSpec(a.shape, lambda i, *_: (0,) * len(a.shape))

    return pl.pallas_call(
        late_kernel,
        out_shape=(jax.ShapeDtypeStruct(attn.shape, jnp.bfloat16),) + (slab,) * 4,
        grid_spec=pltpu.PrefetchScalarGridSpec(
            num_scalar_prefetch=1,
            grid=(steps,),
            in_specs=[pl.BlockSpec(p.shape[:2] + (block,), lambda i, *_: (0, 0, i)) for p in pieces]
            + [pl.BlockSpec((block, r.shape[1]), lambda i, *_: (i, 0)) for r in rows_t]
            + [whole(attn)]
            + [whole(e) for e in early]
            + [pl.BlockSpec((block, width), lambda i, scalars: (i, scalars[0]))],
            out_specs=[whole(attn)] + [whole(slab)] * 4,
            scratch_shapes=[pltpu.VMEM((late_rows, width), jnp.float32)]
            + [pltpu.VMEM((r.shape[1], width), jnp.bfloat16) for r in rows_t]
            + [
                pltpu.VMEM((late_rows, width), jnp.bfloat16),
                pltpu.VMEM((block, width), jnp.float32),
            ],
        ),
        compiler_params=pltpu.CompilerParams(vmem_limit_bytes=32 << 20),
        cost_estimate=pl.CostEstimate(
            flops=2 * 6 * late_rows * features * width, transcendentals=0, bytes_accessed=12 << 20
        ),
        name="projection_late",
    )(scalars, *pieces, *rows_t, attn, *early, o_weight)


def backward(scalars, mine, recv, kvs, weights, attn, d_attn):
    seqs, rows, width = mine.shape
    half = jax.ShapeDtypeStruct((seqs, rows, width), jnp.bfloat16)
    shape = kvs[0].shape
    own = jax.ShapeDtypeStruct(shape, jnp.float32)
    sent = jax.ShapeDtypeStruct(shape, jnp.bfloat16)
    outs = (half, half, own) + (sent,) * CHIPS_Y
    query_spec = by_seq(mine.shape)
    recv_spec = pl.BlockSpec((1, rows, width), lambda s, *_: (s, 0, 0))
    return pl.pallas_call(
        backward_kernel,
        out_shape=outs,
        grid_spec=pltpu.PrefetchScalarGridSpec(
            num_scalar_prefetch=1,
            grid=(seqs,),
            in_specs=[query_spec, recv_spec]
            + [by_seq(a.shape) for a in (*kvs, weights, attn, d_attn)],
            out_specs=[by_seq(o.shape) for o in outs],
        ),
        compiler_params=pltpu.CompilerParams(vmem_limit_bytes=20 << 20),
        cost_estimate=pl.CostEstimate(
            flops=10 * seqs * 2 * 2 * rows * 10 * rows * HEAD_SIZE,
            transcendentals=0,
            bytes_accessed=8 << 20,
        ),
        name="attention_backward",
    )(scalars, mine, recv, *kvs, weights, attn, d_attn)


def local(query, key_states, value_state_rows, d_out, o_weight, doc_start):
    seq_count, shard_rows, query_width = query.shape
    ctx = lax.axis_index("ctx")
    tp = lax.axis_index("tp")
    core = ctx % CORES
    y = ctx // CORES % CHIPS_Y
    chip_pos = ctx // CORES * (CORES * shard_rows)
    scalars = jnp.stack([core, tp, y, chip_pos]).astype(jnp.int32)
    first = core == 0
    early_y = [y + d < CHIPS_Y for d in range(1, CHIPS_Y)]
    q_mine, sent, kv_mine, kv_sent = split_heads(scalars, query, key_states, value_state_rows)

    first_seq, second_seq = d_out[:1], d_out[1:]
    r3a = tp_ahead(first_seq, 1)
    r1b = tp_ahead(second_seq, -1)
    doc_mine = doc_start[:, None, :]
    doc_recv = to_sibling(doc_mine)
    z_same = z_ahead(kv_mine, 1)
    z_other = z_ahead(kv_sent, 1, other_core=True)
    recv = to_sibling(sent)
    (
        z_same, z_other, recv, r3a, r1b, first_seq, second_seq, rows, doc_recv,
        scalars, first, *early_y,
    ) = lax.optimization_barrier(
        (
            z_same, z_other, recv, r3a, r1b, first_seq, second_seq, d_out, doc_recv,
            scalars, first, *early_y,
        )
    )
    r3b = tp_ahead(second_seq, 1)
    r1a = tp_ahead(first_seq, -1)
    kv0 = jnp.concatenate([kv_mine, recv[..., -2 * HEAD_SIZE :]], axis=1)
    kv4 = jnp.concatenate([z_same, z_other], axis=1)
    kv_next = jnp.where(early_y[0], kv0, kv4)
    kv_back = jnp.where(early_y[2], kv0, kv4)
    kv_next, kv_back, t0, t1b, t3a = lax.optimization_barrier(
        (kv_next, kv_back, to_sibling(rows), to_sibling(r1b), to_sibling(r3a))
    )
    kv1, kv3 = y_ahead(kv_next, 1), y_ahead(kv_back, 3)
    own, own_t = early_projection(scalars, [d_out, t0], o_weight)

    near_rows = [r1a, r1b, r3a, r3b]
    *near_rows, kv1, kv3, own = lax.optimization_barrier((*near_rows, kv1, kv3, own))
    low = y_route(kv3, lambda y: y - 1, inner=True)
    high = y_route(kv1, lambda y: y + 1, inner=True)
    r2a = tp_ahead(near_rows[2], 1)
    r2b = tp_ahead(near_rows[1], -1)
    r1a, r1b, r3a, r3b = near_rows
    near_rows = [r1a, r1b, r3a, r3b, to_sibling(r1a), t1b, t3a, to_sibling(r3b)]
    *near_rows, low, high = lax.optimization_barrier((*near_rows, low, high))
    near, near_t = early_projection(scalars, near_rows, o_weight)
    near, r2a, r2b = lax.optimization_barrier((near, r2a, r2b))
    kvs = [kv0, kv1, low, high, kv3, kv4]
    attn, weights = forward(scalars, q_mine, recv, kvs, doc_mine, doc_recv)
    d_attn, sent_a, kept_a, sent_b, kept_b = late_projection(
        scalars,
        [r2a, r2b, to_sibling(r2a), to_sibling(r2b)],
        [own_t, near_t],
        attn,
        [own, near],
        o_weight,
    )
    got_a = y_route(sent_a, y_pair)
    got_b = y_route(sent_b, y_mirror)
    dq_mine, dq_other, g_own, *g_sent, g_before = backward(
        scalars, q_mine, recv, kvs, weights, attn, d_attn
    )
    got_a, got_b, g_own = lax.optimization_barrier((got_a, got_b, g_own))
    dq_recv = to_sibling(dq_other)

    def added(*blocks):
        total = blocks[0].astype(jnp.float32)
        for block in blocks[1:]:
            total = total + block.astype(jnp.float32)
        return total

    next_a = added(kept_a[1], got_a[1]).astype(jnp.bfloat16)
    next_b = added(kept_b[1], got_b[1]).astype(jnp.bfloat16)
    last_a = y_route(next_a, y_mirror)
    last_b = y_route(next_b, y_pair)
    w_sum = merge(kept_a, got_a, last_a, kept_b, got_b, last_b)
    w_all = z_exchange(w_sum)

    grads = g_own
    g_before = g_before.astype(jnp.float32)
    for d, sent in enumerate(g_sent, 1):
        block = y_ahead(sent, -d).astype(jnp.float32)
        grads = grads + jnp.where(early_y[d - 1], block, 0.0)
        g_before = g_before + jnp.where(early_y[d - 1], 0.0, block)
    g_before = g_before.astype(jnp.bfloat16)
    z_same = z_ahead(g_before[:, :shard_rows], -1)
    z_other = z_ahead(g_before[:, shard_rows:], -1, other_core=True)
    sibling = to_sibling(grads[:, shard_rows:].astype(jnp.bfloat16))
    g_mine = added(grads[:, :shard_rows], z_same).astype(jnp.bfloat16)
    g_recv = added(sibling, z_other).astype(jnp.bfloat16)

    def by_core(own, other):
        return jnp.concatenate(
            [jnp.where(first, own, other), jnp.where(first, other, own)], axis=-1
        )

    return (
        by_core(dq_mine, dq_recv),
        by_core(g_mine[..., :HEAD_SIZE], g_recv[..., :HEAD_SIZE]),
        by_core(g_mine[..., HEAD_SIZE:], g_recv[..., HEAD_SIZE:]),
        finish(w_all),
    )


def solution(mesh):
    return jax.shard_map(
        local,
        mesh=mesh,
        in_specs=(
            P(None, "ctx", "tp"),
            P(None, "ctx", "tp"),
            P(None, "ctx", "tp"),
            P(None, ("ctx", "tp"), None),
            P(None, "tp"),
            P(None, "ctx"),
        ),
        out_specs=(
            P(None, "ctx", "tp"),
            P(None, "ctx", "tp"),
            P(None, "ctx", "tp"),
            P("ctx", "tp"),
        ),
        check_vma=False,
    )
```

```python
import jax
import jax.numpy as jnp
from jax import lax
from jax.experimental import pallas as pl
from jax.experimental.pallas import tpu as pltpu
from jax.sharding import PartitionSpec as P

HEAD_SIZE = 128
WIN = 1024
CORES = 2
CHIPS_Y = 4
CHIPS_Z = 8
TP = 4
LOG2_E = 1.4426950408889634

score_scale = 168.0 ** (-0.5)

NT = (((1,), (1,)), ((), ()))
TN = (((0,), (0,)), ((), ()))
NN = (((1,), (0,)), ((), ()))


def dot(a, b, dims=NN):
    return lax.dot_general(a, b, dims, preferred_element_type=jnp.float32)


def ctx_shift(block, move):
    count = CORES * CHIPS_Y * CHIPS_Z
    return lax.ppermute(block, "ctx", [(i, move(i)) for i in range(count)])


def to_sibling(block):
    return ctx_shift(block, lambda i: i ^ 1)


def y_pair(y):
    return y ^ 1


def y_mirror(y):
    return CHIPS_Y - 1 - y


def y_route(block, target):
    def move(i):
        core, y, z = i % CORES, i // CORES % CHIPS_Y, i // (CORES * CHIPS_Y)
        return (z * CHIPS_Y + target(y)) * CORES + core

    return ctx_shift(block, move)


def z_exchange(blocks):
    groups = [
        [(z * CHIPS_Y + y) * CORES + core for z in range(CHIPS_Z) for core in range(CORES)]
        for y in range(CHIPS_Y)
    ]
    return lax.all_to_all(blocks, "ctx", 0, 0, axis_index_groups=groups, tiled=True)


def chips_ahead(block, distance):
    count = CORES * CHIPS_Y * CHIPS_Z
    return ctx_shift(block, lambda i: (i + CORES * distance) % count)


def tp_ahead(block, distance):
    return lax.ppermute(block, "tp", [(i, (i + distance) % TP) for i in range(TP)])


def query_positions(core, chip_pos, rows):
    lane = lax.broadcasted_iota(jnp.int32, (1, 2 * rows), 1)
    other = lane >= rows
    first = jnp.where(other, (1 - core) * rows - rows, core * rows)
    return chip_pos + first + lane


def forward_kernel(
    scalars, mine, recv, kv0, kv1, kv2, kv3, kv4, doc_mine, doc_recv, attn, weights
):
    core, chip_pos = scalars[0], scalars[3]
    kvs = [kv[0] for kv in (kv0, kv1, kv2, kv3, kv4)]
    rows = mine.shape[1]
    query_pos = query_positions(core, chip_pos, rows)
    doc = jnp.concatenate([doc_mine[0], doc_recv[0]], axis=1)
    lowest = jnp.maximum(doc, query_pos - (WIN - 1))
    index = lax.broadcasted_iota(jnp.int32, (2 * rows, 2 * rows), 0)
    offset = index + jnp.where(index >= rows, (1 - core) * rows - rows, core * rows)
    for h in range(2):
        cols = slice(h * HEAD_SIZE, (h + 1) * HEAD_SIZE)
        q = jnp.concatenate([mine[0, :, cols], recv[0, :, cols]], axis=0)
        scores = []
        for d, kv in enumerate(kvs):
            s = dot(kv[:, :HEAD_SIZE], q, NT) * (score_scale * LOG2_E)
            key_pos = offset + (chip_pos - 2 * rows * d)
            visible = key_pos >= lowest
            if d == 0:
                visible = visible & (key_pos <= query_pos)
            scores.append(jnp.where(visible, s, -1e30))
        top = scores[0]
        for s in scores[1:]:
            top = jnp.maximum(top, s)
        top = jnp.max(top, axis=0, keepdims=True)
        expo = [jnp.exp2(s - top) for s in scores]
        total = expo[0]
        for e in expo[1:]:
            total = total + e
        inverse = 1.0 / jnp.sum(total, axis=0, keepdims=True)
        acc = None
        for d, kv in enumerate(kvs):
            w = (expo[d] * inverse).astype(jnp.bfloat16)
            weights[0, h, 2 * rows * d : 2 * rows * (d + 1), :] = w
            part = dot(kv[:, HEAD_SIZE:], w, TN)
            acc = part if acc is None else acc + part
        attn[0, :, cols] = acc.T.astype(jnp.bfloat16)


def early_kernel(scalars, *refs):
    *pieces, o_weight, d_attn, rows_t, acc = refs
    step = pl.program_id(0)
    parts = [ref[seq] for ref in pieces for seq in range(ref.shape[0])]
    rows = jnp.concatenate(parts, axis=0)
    product = dot(rows, o_weight[...])

    @pl.when(step == 0)
    def _():
        acc[...] = product

    @pl.when(step > 0)
    def _():
        acc[...] = acc[...] + product

    rows_t[...] = rows.T

    @pl.when(step == pl.num_programs(0) - 1)
    def _():
        d_attn[...] = acc[...].astype(jnp.bfloat16)


def place(tp, piece, core_block, rel, seq):
    here = TP * piece * core_block + piece * ((tp + rel) % TP)
    return seq, pl.ds(pl.multiple_of(here, piece), piece)


OWN_SLOTS = [(b, 0, q) for b in range(2) for q in range(2)]
NEAR_SLOTS = [(b, s, q) for b in range(2) for s in (1, 3) for q in range(2)]
FAR_SLOTS = [(b, 2, q) for b in range(2) for q in range(2)]


def late_kernel(
    scalars, r2a, r2b, t2a, t2b, own_t, near_t, attn, own, near, o_weight,
    d_attn, sent_a, kept_a, sent_b, kept_b, acc, attn_own, attn_near, attn_far, partial,
):
    step = pl.program_id(0)
    tp, y = scalars[1], scalars[2]
    piece = r2a.shape[1]
    out_rows = sent_a.shape[2]

    @pl.when(step == 0)
    def _():
        for slots, kept in ((OWN_SLOTS, attn_own), (NEAR_SLOTS, attn_near), (FAR_SLOTS, attn_far)):
            for n, slot in enumerate(slots):
                seq, here = place(tp, piece, *slot)
                kept[n * piece : (n + 1) * piece, :] = attn[seq, here, :]
        for slots, done in ((OWN_SLOTS, own), (NEAR_SLOTS, near)):
            for n, slot in enumerate(slots):
                seq, here = place(tp, piece, *slot)
                d_attn[seq, here, :] = done[n * piece : (n + 1) * piece, :]

    rows = jnp.concatenate([r2a[0], r2b[0], t2a[0], t2b[0]], axis=0)
    partial[...] = (
        dot(own_t[...], attn_own[...])
        + dot(near_t[...], attn_near[...])
        + dot(rows.T, attn_far[...])
    )

    def emit(out, order):
        for n, target in enumerate(order):
            for z in range(out.shape[1]):
                start = pl.multiple_of((CHIPS_Y * z + target) * out_rows, 8)
                out[n, z] = partial[pl.ds(start, out_rows), :].astype(jnp.bfloat16)

    pair = y + 1 - 2 * (y % 2)
    mirror = CHIPS_Y - 1 - y
    mirror_pair = mirror + 1 - 2 * (mirror % 2)

    product = dot(rows, o_weight[...])

    @pl.when(step == 0)
    def _():
        emit(sent_a, (pair, CHIPS_Y - 1 - pair))
        emit(kept_a, (y, mirror))
        acc[...] = product

    @pl.when(step == 1)
    def _():
        emit(sent_b, (mirror, mirror_pair))
        emit(kept_b, (y, pair))
        total = (acc[...] + product).astype(jnp.bfloat16)
        for n, slot in enumerate(FAR_SLOTS):
            seq, here = place(tp, piece, *slot)
            d_attn[seq, here, :] = total[n * piece : (n + 1) * piece, :]


def backward_kernel(
    mine, recv, kv0, kv1, kv2, kv3, kv4, weights, attn, d_attn,
    dq_mine, dq_other, g_own, g1, g2, g3, g4,
):
    rows = mine.shape[1]
    kvs = [kv[0] for kv in (kv0, kv1, kv2, kv3, kv4)]
    heads = []
    for h in range(2):
        cols = slice(h * HEAD_SIZE, (h + 1) * HEAD_SIZE)
        q = jnp.concatenate([mine[0, :, cols], recv[0, :, cols]], axis=0)
        da = d_attn[0, :, cols]
        product = da.astype(jnp.float32) * attn[0, :, cols].astype(jnp.float32)
        delta = jnp.sum(product.T, axis=0, keepdims=True)
        heads.append((q, da, delta))
    dq = [None, None]
    grads = (g_own, g1, g2, g3, g4)
    for kv_index, (kv, grad) in enumerate(zip(kvs, grads)):
        keys = kv[:, :HEAD_SIZE]
        values = kv[:, HEAD_SIZE:]
        dk = dv = None
        for h, (q, da, delta) in enumerate(heads):
            w = weights[0, h, 2 * rows * kv_index : 2 * rows * (kv_index + 1), :]
            dp = dot(values, da, NT)
            ds = (w.astype(jnp.float32) * (dp - delta)).astype(jnp.bfloat16)
            v_part = dot(w, da)
            k_part = dot(ds, q)
            q_part = dot(keys, ds, TN)
            dv = v_part if dv is None else dv + v_part
            dk = k_part if dk is None else dk + k_part
            dq[h] = q_part if dq[h] is None else dq[h] + q_part
        grad[0, :, :HEAD_SIZE] = (dk * score_scale).astype(grad.dtype)
        grad[0, :, HEAD_SIZE:] = dv.astype(grad.dtype)
    for h in range(2):
        cols = slice(h * HEAD_SIZE, (h + 1) * HEAD_SIZE)
        full = (dq[h].T * score_scale).astype(jnp.bfloat16)
        dq_mine[0, :, cols] = full[:rows]
        dq_other[0, :, cols] = full[rows:]


def merge_kernel(kept_a, got_a, last_a, kept_b, got_b, last_b, out):
    half = kept_a.shape[1]
    rows = out.shape[1]
    for part, (kept, got, last) in enumerate(((kept_a, got_a, last_a), (kept_b, got_b, last_b))):
        for z in range(half):
            total = (
                kept[0, z].astype(jnp.float32)
                + got[0, z].astype(jnp.float32)
                + last[z].astype(jnp.float32)
            )
            for core in range(CORES):
                slot = CORES * (half * part + z) + core
                out[slot] = total[core * rows : (core + 1) * rows].astype(jnp.bfloat16)


def finish_kernel(blocks, out):
    width = blocks.shape[2]
    for core in range(CORES):
        total = blocks[core].astype(jnp.float32)
        for z in range(1, CHIPS_Z):
            total = total + blocks[CORES * z + core].astype(jnp.float32)
        out[:, core * width : (core + 1) * width] = total


def merge(kept_a, got_a, last_a, kept_b, got_b, last_b):
    _, half, rows, width = kept_a.shape
    front = pl.BlockSpec((1, half, rows, width), lambda i: (0, 0, 0, 0))
    flat = pl.BlockSpec((half, rows, width), lambda i: (0, 0, 0))
    shape = (CORES * 2 * half, rows // CORES, width)
    return pl.pallas_call(
        merge_kernel,
        out_shape=jax.ShapeDtypeStruct(shape, jnp.bfloat16),
        grid=(1,),
        in_specs=[front, front, flat] * 2,
        out_specs=pl.BlockSpec(shape, lambda i: (0, 0, 0)),
        compiler_params=pltpu.CompilerParams(vmem_limit_bytes=16 << 20),
        name="projection_merge",
    )(kept_a, got_a, last_a, kept_b, got_b, last_b)


def finish(blocks):
    count, rows, width = blocks.shape
    return pl.pallas_call(
        finish_kernel,
        out_shape=jax.ShapeDtypeStruct((rows, CORES * width), jnp.float32),
        compiler_params=pltpu.CompilerParams(vmem_limit_bytes=16 << 20),
        name="projection_finish",
    )(blocks)


def split_kernel(
    scalars, q_own, q_other, k_own, k_other, v_own, v_other,
    q_mine, sent, kv_mine,
):
    width = q_other.shape[2]
    q_mine[...] = q_own[...]
    sent[:, :, :width] = q_other[...]
    sent[:, :, width : width + HEAD_SIZE] = k_other[...]
    sent[:, :, width + HEAD_SIZE :] = v_other[...]
    kv_mine[:, :, :HEAD_SIZE] = k_own[...]
    kv_mine[:, :, HEAD_SIZE:] = v_own[...]


def split_heads(scalars, query, keys, values):
    seqs, rows, width = query.shape
    out = jax.ShapeDtypeStruct((seqs, rows, width // 2), jnp.bfloat16)
    whole = jax.ShapeDtypeStruct(query.shape, jnp.bfloat16)
    outs = (out, whole, out)

    def half(a):
        shape = a.shape[:2] + (a.shape[2] // 2,)
        return [
            pl.BlockSpec(shape, lambda i, scalars: (0, 0, scalars[0])),
            pl.BlockSpec(shape, lambda i, scalars: (0, 0, 1 - scalars[0])),
        ]

    return pl.pallas_call(
        split_kernel,
        out_shape=outs,
        grid_spec=pltpu.PrefetchScalarGridSpec(
            num_scalar_prefetch=1,
            grid=(1,),
            in_specs=half(query) + half(keys) + half(values),
            out_specs=[pl.BlockSpec(o.shape, lambda i, *_: (0, 0, 0)) for o in outs],
        ),
        compiler_params=pltpu.CompilerParams(vmem_limit_bytes=16 << 20),
        name="split_heads",
    )(scalars, query, query, keys, keys, values, values)


def by_seq(shape):
    return pl.BlockSpec((1,) + shape[1:], lambda s, *_: (s,) + (0,) * (len(shape) - 1))


def forward(scalars, mine, recv, kvs, doc_mine, doc_recv):
    seqs, rows, width = mine.shape
    keys = 2 * rows * len(kvs)
    outs = (
        jax.ShapeDtypeStruct((seqs, 2 * rows, width), jnp.bfloat16),
        jax.ShapeDtypeStruct((seqs, 2, keys, 2 * rows), jnp.bfloat16),
    )
    query_spec = by_seq(mine.shape)
    recv_spec = pl.BlockSpec((1, rows, width), lambda s, *_: (s, 0, 0))
    return pl.pallas_call(
        forward_kernel,
        out_shape=outs,
        grid_spec=pltpu.PrefetchScalarGridSpec(
            num_scalar_prefetch=1,
            grid=(seqs,),
            in_specs=[query_spec, recv_spec]
            + [by_seq(kv.shape) for kv in kvs]
            + [by_seq(doc_mine.shape), by_seq(doc_recv.shape)],
            out_specs=[by_seq(o.shape) for o in outs],
        ),
        compiler_params=pltpu.CompilerParams(vmem_limit_bytes=20 << 20),
        cost_estimate=pl.CostEstimate(
            flops=4 * seqs * 2 * 2 * rows * keys * HEAD_SIZE,
            transcendentals=seqs * 2 * 2 * rows * keys,
            bytes_accessed=8 << 20,
        ),
        name="attention_forward",
    )(scalars, mine, recv, *kvs, doc_mine, doc_recv)


def early_projection(scalars, pieces, o_weight):
    rows = sum(p.shape[0] * p.shape[1] for p in pieces)
    features, both = o_weight.shape
    width = both // 2
    steps = 7
    block = features // steps
    outs = (
        jax.ShapeDtypeStruct((rows, width), jnp.bfloat16),
        jax.ShapeDtypeStruct((features, rows), jnp.bfloat16),
    )
    return pl.pallas_call(
        early_kernel,
        out_shape=outs,
        grid_spec=pltpu.PrefetchScalarGridSpec(
            num_scalar_prefetch=1,
            grid=(steps,),
            in_specs=[pl.BlockSpec(p.shape[:2] + (block,), lambda i, *_: (0, 0, i)) for p in pieces]
            + [pl.BlockSpec((block, width), lambda i, scalars: (i, scalars[0]))],
            out_specs=[
                pl.BlockSpec((rows, width), lambda i, *_: (0, 0)),
                pl.BlockSpec((block, rows), lambda i, *_: (i, 0)),
            ],
            scratch_shapes=[pltpu.VMEM((rows, width), jnp.float32)],
        ),
        compiler_params=pltpu.CompilerParams(vmem_limit_bytes=16 << 20),
        cost_estimate=pl.CostEstimate(
            flops=20 * rows * features * width, transcendentals=0, bytes_accessed=12 << 20
        ),
        name="projection_early",
    )(scalars, *pieces, o_weight)


def late_projection(scalars, pieces, rows_t, attn, early, o_weight):
    width = attn.shape[-1]
    features = o_weight.shape[0]
    late_rows = sum(p.shape[0] * p.shape[1] for p in pieces)
    steps = 2
    block = features // steps
    out_rows = features // (CHIPS_Y * CHIPS_Z)
    slab = jax.ShapeDtypeStruct((2, CHIPS_Z // 2, out_rows, width), jnp.bfloat16)

    def whole(a):
        return pl.BlockSpec(a.shape, lambda i, *_: (0,) * len(a.shape))

    return pl.pallas_call(
        late_kernel,
        out_shape=(jax.ShapeDtypeStruct(attn.shape, jnp.bfloat16),) + (slab,) * 4,
        grid_spec=pltpu.PrefetchScalarGridSpec(
            num_scalar_prefetch=1,
            grid=(steps,),
            in_specs=[pl.BlockSpec(p.shape[:2] + (block,), lambda i, *_: (0, 0, i)) for p in pieces]
            + [pl.BlockSpec((block, r.shape[1]), lambda i, *_: (i, 0)) for r in rows_t]
            + [whole(attn)]
            + [whole(e) for e in early]
            + [pl.BlockSpec((block, width), lambda i, scalars: (i, scalars[0]))],
            out_specs=[whole(attn)] + [whole(slab)] * 4,
            scratch_shapes=[pltpu.VMEM((late_rows, width), jnp.float32)]
            + [pltpu.VMEM((r.shape[1], width), jnp.bfloat16) for r in rows_t]
            + [
                pltpu.VMEM((late_rows, width), jnp.bfloat16),
                pltpu.VMEM((block, width), jnp.float32),
            ],
        ),
        compiler_params=pltpu.CompilerParams(vmem_limit_bytes=32 << 20),
        cost_estimate=pl.CostEstimate(
            flops=2 * 6 * late_rows * features * width, transcendentals=0, bytes_accessed=12 << 20
        ),
        name="projection_late",
    )(scalars, *pieces, *rows_t, attn, *early, o_weight)


def backward(mine, recv, kvs, weights, attn, d_attn):
    seqs, rows, width = mine.shape
    half = jax.ShapeDtypeStruct((seqs, rows, width), jnp.bfloat16)
    shape = kvs[0].shape
    own = jax.ShapeDtypeStruct(shape, jnp.float32)
    sent = jax.ShapeDtypeStruct(shape, jnp.bfloat16)
    outs = (half, half, own) + (sent,) * (len(kvs) - 1)
    query_spec = by_seq(mine.shape)
    recv_spec = pl.BlockSpec((1, rows, width), lambda s, *_: (s, 0, 0))
    return pl.pallas_call(
        backward_kernel,
        out_shape=outs,
        grid=(seqs,),
        in_specs=[query_spec, recv_spec]
        + [by_seq(a.shape) for a in (*kvs, weights, attn, d_attn)],
        out_specs=[by_seq(o.shape) for o in outs],
        compiler_params=pltpu.CompilerParams(vmem_limit_bytes=20 << 20),
        cost_estimate=pl.CostEstimate(
            flops=10 * seqs * 2 * 2 * rows * 10 * rows * HEAD_SIZE,
            transcendentals=0,
            bytes_accessed=8 << 20,
        ),
        name="attention_backward",
    )(mine, recv, *kvs, weights, attn, d_attn)


def local(query, key_states, value_state_rows, d_out, o_weight, doc_start):
    seq_count, shard_rows, query_width = query.shape
    ctx = lax.axis_index("ctx")
    tp = lax.axis_index("tp")
    core = ctx % CORES
    y = ctx // CORES % CHIPS_Y
    chip_pos = ctx // CORES * (CORES * shard_rows)
    scalars = jnp.stack([core, tp, y, chip_pos]).astype(jnp.int32)
    first = core == 0
    q_mine, sent, kv_mine = split_heads(scalars, query, key_states, value_state_rows)

    r3 = tp_ahead(d_out, 1)
    r1 = tp_ahead(d_out, -1)
    recv = to_sibling(sent)
    doc_mine = doc_start[:, None, :]
    doc_recv = to_sibling(doc_mine)
    t0 = to_sibling(d_out)
    recv, doc_recv, t0, scalars, first = lax.optimization_barrier(
        (recv, doc_recv, t0, scalars, first)
    )
    kv0 = jnp.concatenate([kv_mine, recv[..., -2 * HEAD_SIZE :]], axis=1)
    kv1, kv3, kv4 = (chips_ahead(kv0, d) for d in (1, 3, 4))
    own, own_t = early_projection(scalars, [d_out, t0], o_weight)

    r1, r3, own, kv1, kv3, kv4, kv_again = lax.optimization_barrier(
        (r1, r3, own, kv1, kv3, kv4, kv0)
    )
    kv2 = chips_ahead(kv_again, 2)
    r2a = tp_ahead(r3[:1], 1)
    r2b = tp_ahead(r1[1:], -1)
    near, near_t = early_projection(
        scalars, [r1, r3, to_sibling(r1), to_sibling(r3)], o_weight
    )
    near, r2a, r2b, kv2 = lax.optimization_barrier((near, r2a, r2b, kv2))
    kvs = [kv0, kv1, kv2, kv3, kv4]
    attn, weights = forward(scalars, q_mine, recv, kvs, doc_mine, doc_recv)
    d_attn, sent_a, kept_a, sent_b, kept_b = late_projection(
        scalars,
        [r2a, r2b, to_sibling(r2a), to_sibling(r2b)],
        [own_t, near_t],
        attn,
        [own, near],
        o_weight,
    )
    got_a = y_route(sent_a, y_pair)
    got_b = y_route(sent_b, y_mirror)
    dq_mine, dq_other, g_own, *g_sent = backward(
        q_mine, recv, kvs, weights, attn, d_attn
    )
    *g_near, g_far = (chips_ahead(g, -d) for d, g in enumerate(g_sent, 1))
    got_a, got_b, g_own, *g_near = lax.optimization_barrier((got_a, got_b, g_own, *g_near))
    dq_recv = to_sibling(dq_other)

    def added(*blocks):
        total = blocks[0].astype(jnp.float32)
        for block in blocks[1:]:
            total = total + block.astype(jnp.float32)
        return total

    next_a = added(kept_a[1], got_a[1]).astype(jnp.bfloat16)
    next_b = added(kept_b[1], got_b[1]).astype(jnp.bfloat16)
    last_a = y_route(next_a, y_mirror)
    last_b = y_route(next_b, y_pair)
    last_a, last_b, g_far = lax.optimization_barrier((last_a, last_b, g_far))
    w_sum = merge(kept_a, got_a, last_a, kept_b, got_b, last_b)
    w_all = z_exchange(w_sum)

    grads = added(g_own, *g_near, g_far).astype(jnp.bfloat16)
    g_mine = grads[:, :shard_rows]
    g_recv = to_sibling(grads[:, shard_rows:])

    def by_core(own, other):
        return jnp.concatenate(
            [jnp.where(first, own, other), jnp.where(first, other, own)], axis=-1
        )

    return (
        by_core(dq_mine, dq_recv),
        by_core(g_mine[..., :HEAD_SIZE], g_recv[..., :HEAD_SIZE]),
        by_core(g_mine[..., HEAD_SIZE:], g_recv[..., HEAD_SIZE:]),
        finish(w_all),
    )


def solution(mesh):
    return jax.shard_map(
        local,
        mesh=mesh,
        in_specs=(
            P(None, "ctx", "tp"),
            P(None, "ctx", "tp"),
            P(None, "ctx", "tp"),
            P(None, ("ctx", "tp"), None),
            P(None, "tp"),
            P(None, "ctx"),
        ),
        out_specs=(
            P(None, "ctx", "tp"),
            P(None, "ctx", "tp"),
            P(None, "ctx", "tp"),
            P("ctx", "tp"),
        ),
        check_vma=False,
    )
```

```python
import jax
import jax.numpy as jnp
from jax import lax
from jax.experimental import pallas as pl
from jax.experimental.pallas import tpu as pltpu
from jax.sharding import PartitionSpec as P

HEAD_SIZE = 128
WIN = 1024
CORES = 2
CHIPS_Y = 4
CHIPS_Z = 8
TP = 4
LOG2_E = 1.4426950408889634

score_scale = 168.0 ** (-0.5)

NT = (((1,), (1,)), ((), ()))
TN = (((0,), (0,)), ((), ()))
NN = (((1,), (0,)), ((), ()))


def dot(a, b, dims=NN):
    return lax.dot_general(a, b, dims, preferred_element_type=jnp.float32)


def ctx_shift(block, move):
    count = CORES * CHIPS_Y * CHIPS_Z
    return lax.ppermute(block, "ctx", [(i, move(i)) for i in range(count)])


def to_sibling(block):
    return ctx_shift(block, lambda i: i ^ 1)


def y_pair(y):
    return y ^ 1


def y_mirror(y):
    return CHIPS_Y - 1 - y


def y_route(block, target):
    def move(i):
        core, y, z = i % CORES, i // CORES % CHIPS_Y, i // (CORES * CHIPS_Y)
        return (z * CHIPS_Y + target(y)) * CORES + core

    return ctx_shift(block, move)


def z_exchange(blocks):
    groups = [
        [(z * CHIPS_Y + y) * CORES + core for z in range(CHIPS_Z) for core in range(CORES)]
        for y in range(CHIPS_Y)
    ]
    return lax.all_to_all(blocks, "ctx", 0, 0, axis_index_groups=groups, tiled=True)


def chips_ahead(block, distance):
    count = CORES * CHIPS_Y * CHIPS_Z
    return ctx_shift(block, lambda i: (i + CORES * distance) % count)


def tp_ahead(block, distance):
    return lax.ppermute(block, "tp", [(i, (i + distance) % TP) for i in range(TP)])


def query_positions(core, chip_pos, rows):
    lane = lax.broadcasted_iota(jnp.int32, (1, 2 * rows), 1)
    other = lane >= rows
    first = jnp.where(other, (1 - core) * rows - rows, core * rows)
    return chip_pos + first + lane


def forward_kernel(
    scalars, mine, recv, kv0, kv1, kv2, kv3, kv4, doc_mine, doc_recv, attn, weights
):
    core, chip_pos = scalars[0], scalars[3]
    kvs = [kv[0] for kv in (kv0, kv1, kv2, kv3, kv4)]
    rows = mine.shape[1]
    query_pos = query_positions(core, chip_pos, rows)
    doc = jnp.concatenate([doc_mine[0], doc_recv[0]], axis=1)
    lowest = jnp.maximum(doc, query_pos - (WIN - 1))
    index = lax.broadcasted_iota(jnp.int32, (2 * rows, 2 * rows), 0)
    offset = index + jnp.where(index >= rows, (1 - core) * rows - rows, core * rows)
    for h in range(2):
        cols = slice(h * HEAD_SIZE, (h + 1) * HEAD_SIZE)
        q = jnp.concatenate([mine[0, :, cols], recv[0, :, cols]], axis=0)
        scores = []
        for d, kv in enumerate(kvs):
            s = dot(kv[:, :HEAD_SIZE], q, NT) * (score_scale * LOG2_E)
            key_pos = offset + (chip_pos - 2 * rows * d)
            visible = key_pos >= lowest
            if d == 0:
                visible = visible & (key_pos <= query_pos)
            scores.append(jnp.where(visible, s, -1e30))
        top = scores[0]
        for s in scores[1:]:
            top = jnp.maximum(top, s)
        top = jnp.max(top, axis=0, keepdims=True)
        expo = [jnp.exp2(s - top) for s in scores]
        total = expo[0]
        for e in expo[1:]:
            total = total + e
        inverse = 1.0 / jnp.sum(total, axis=0, keepdims=True)
        acc = None
        for d, kv in enumerate(kvs):
            w = (expo[d] * inverse).astype(jnp.bfloat16)
            weights[0, h, 2 * rows * d : 2 * rows * (d + 1), :] = w
            part = dot(kv[:, HEAD_SIZE:], w, TN)
            acc = part if acc is None else acc + part
        attn[0, :, cols] = acc.T.astype(jnp.bfloat16)


def early_kernel(scalars, *refs):
    *pieces, o_weight, d_attn, rows_t, acc = refs
    step = pl.program_id(0)
    parts = [ref[seq] for ref in pieces for seq in range(ref.shape[0])]
    rows = jnp.concatenate(parts, axis=0)
    product = dot(rows, o_weight[...])

    @pl.when(step == 0)
    def _():
        acc[...] = product

    @pl.when(step > 0)
    def _():
        acc[...] = acc[...] + product

    rows_t[...] = rows.T

    @pl.when(step == pl.num_programs(0) - 1)
    def _():
        d_attn[...] = acc[...].astype(jnp.bfloat16)


def place(tp, piece, core_block, rel, seq):
    here = TP * piece * core_block + piece * ((tp + rel) % TP)
    return seq, pl.ds(pl.multiple_of(here, piece), piece)


OWN_SLOTS = [(b, 0, q) for b in range(2) for q in range(2)]
NEAR_SLOTS = [(b, s, q) for b in range(2) for s in (1, 3) for q in range(2)]
FAR_SLOTS = [(b, 2, q) for b in range(2) for q in range(2)]


def late_kernel(
    scalars, r2a, r2b, t2a, t2b, own_t, near_t, attn, own, near, o_weight,
    d_attn, sent_a, kept_a, sent_b, kept_b, acc, attn_own, attn_near, attn_far, partial,
):
    step = pl.program_id(0)
    tp, y = scalars[1], scalars[2]
    piece = r2a.shape[1]
    out_rows = sent_a.shape[2]

    @pl.when(step == 0)
    def _():
        for slots, kept in ((OWN_SLOTS, attn_own), (NEAR_SLOTS, attn_near), (FAR_SLOTS, attn_far)):
            for n, slot in enumerate(slots):
                seq, here = place(tp, piece, *slot)
                kept[n * piece : (n + 1) * piece, :] = attn[seq, here, :]
        for slots, done in ((OWN_SLOTS, own), (NEAR_SLOTS, near)):
            for n, slot in enumerate(slots):
                seq, here = place(tp, piece, *slot)
                d_attn[seq, here, :] = done[n * piece : (n + 1) * piece, :]

    rows = jnp.concatenate([r2a[0], r2b[0], t2a[0], t2b[0]], axis=0)
    partial[...] = (
        dot(own_t[...], attn_own[...])
        + dot(near_t[...], attn_near[...])
        + dot(rows.T, attn_far[...])
    )

    def emit(out, order):
        for n, target in enumerate(order):
            for z in range(out.shape[1]):
                start = pl.multiple_of((CHIPS_Y * z + target) * out_rows, 8)
                out[n, z] = partial[pl.ds(start, out_rows), :].astype(jnp.bfloat16)

    pair = y + 1 - 2 * (y % 2)
    mirror = CHIPS_Y - 1 - y
    mirror_pair = mirror + 1 - 2 * (mirror % 2)

    product = dot(rows, o_weight[...])

    @pl.when(step == 0)
    def _():
        emit(sent_a, (pair, CHIPS_Y - 1 - pair))
        emit(kept_a, (y, mirror))
        acc[...] = product

    @pl.when(step == 1)
    def _():
        emit(sent_b, (mirror, mirror_pair))
        emit(kept_b, (y, pair))
        total = (acc[...] + product).astype(jnp.bfloat16)
        for n, slot in enumerate(FAR_SLOTS):
            seq, here = place(tp, piece, *slot)
            d_attn[seq, here, :] = total[n * piece : (n + 1) * piece, :]


def backward_kernel(
    mine, recv, kv0, kv1, kv2, kv3, kv4, weights, attn, d_attn,
    dq_mine, dq_other, g_own, g1, g2, g3, g4,
):
    rows = mine.shape[1]
    kvs = [kv[0] for kv in (kv0, kv1, kv2, kv3, kv4)]
    heads = []
    for h in range(2):
        cols = slice(h * HEAD_SIZE, (h + 1) * HEAD_SIZE)
        q = jnp.concatenate([mine[0, :, cols], recv[0, :, cols]], axis=0)
        da = d_attn[0, :, cols]
        product = da.astype(jnp.float32) * attn[0, :, cols].astype(jnp.float32)
        delta = jnp.sum(product.T, axis=0, keepdims=True)
        heads.append((q, da, delta))
    dq = [None, None]
    grads = (g_own, g1, g2, g3, g4)
    for kv_index, (kv, grad) in enumerate(zip(kvs, grads)):
        keys = kv[:, :HEAD_SIZE]
        values = kv[:, HEAD_SIZE:]
        dk = dv = None
        for h, (q, da, delta) in enumerate(heads):
            w = weights[0, h, 2 * rows * kv_index : 2 * rows * (kv_index + 1), :]
            dp = dot(values, da, NT)
            ds = (w.astype(jnp.float32) * (dp - delta)).astype(jnp.bfloat16)
            v_part = dot(w, da)
            k_part = dot(ds, q)
            q_part = dot(keys, ds, TN)
            dv = v_part if dv is None else dv + v_part
            dk = k_part if dk is None else dk + k_part
            dq[h] = q_part if dq[h] is None else dq[h] + q_part
        grad[0, :, :HEAD_SIZE] = (dk * score_scale).astype(grad.dtype)
        grad[0, :, HEAD_SIZE:] = dv.astype(grad.dtype)
    for h in range(2):
        cols = slice(h * HEAD_SIZE, (h + 1) * HEAD_SIZE)
        full = (dq[h].T * score_scale).astype(jnp.bfloat16)
        dq_mine[0, :, cols] = full[:rows]
        dq_other[0, :, cols] = full[rows:]


def merge_kernel(kept_a, got_a, last_a, kept_b, got_b, last_b, out):
    half = kept_a.shape[1]
    rows = out.shape[1]
    for part, (kept, got, last) in enumerate(((kept_a, got_a, last_a), (kept_b, got_b, last_b))):
        for z in range(half):
            total = (
                kept[0, z].astype(jnp.float32)
                + got[0, z].astype(jnp.float32)
                + last[z].astype(jnp.float32)
            )
            for core in range(CORES):
                slot = CORES * (half * part + z) + core
                out[slot] = total[core * rows : (core + 1) * rows].astype(jnp.bfloat16)


def finish_kernel(blocks, out):
    width = blocks.shape[2]
    for core in range(CORES):
        total = blocks[core].astype(jnp.float32)
        for z in range(1, CHIPS_Z):
            total = total + blocks[CORES * z + core].astype(jnp.float32)
        out[:, core * width : (core + 1) * width] = total


def merge(kept_a, got_a, last_a, kept_b, got_b, last_b):
    _, half, rows, width = kept_a.shape
    front = pl.BlockSpec((1, half, rows, width), lambda i: (0, 0, 0, 0))
    flat = pl.BlockSpec((half, rows, width), lambda i: (0, 0, 0))
    shape = (CORES * 2 * half, rows // CORES, width)
    return pl.pallas_call(
        merge_kernel,
        out_shape=jax.ShapeDtypeStruct(shape, jnp.bfloat16),
        grid=(1,),
        in_specs=[front, front, flat] * 2,
        out_specs=pl.BlockSpec(shape, lambda i: (0, 0, 0)),
        compiler_params=pltpu.CompilerParams(vmem_limit_bytes=16 << 20),
        name="projection_merge",
    )(kept_a, got_a, last_a, kept_b, got_b, last_b)


def finish(blocks):
    count, rows, width = blocks.shape
    return pl.pallas_call(
        finish_kernel,
        out_shape=jax.ShapeDtypeStruct((rows, CORES * width), jnp.float32),
        compiler_params=pltpu.CompilerParams(vmem_limit_bytes=16 << 20),
        name="projection_finish",
    )(blocks)


def split_kernel(
    scalars, q_own, q_other, k_own, k_other, v_own, v_other,
    q_mine, sent, kv_mine,
):
    width = q_other.shape[2]
    q_mine[...] = q_own[...]
    sent[:, :, :width] = q_other[...]
    sent[:, :, width : width + HEAD_SIZE] = k_other[...]
    sent[:, :, width + HEAD_SIZE :] = v_other[...]
    kv_mine[:, :, :HEAD_SIZE] = k_own[...]
    kv_mine[:, :, HEAD_SIZE:] = v_own[...]


def split_heads(scalars, query, keys, values):
    seqs, rows, width = query.shape
    out = jax.ShapeDtypeStruct((seqs, rows, width // 2), jnp.bfloat16)
    whole = jax.ShapeDtypeStruct(query.shape, jnp.bfloat16)
    outs = (out, whole, out)

    def half(a):
        shape = a.shape[:2] + (a.shape[2] // 2,)
        return [
            pl.BlockSpec(shape, lambda i, scalars: (0, 0, scalars[0])),
            pl.BlockSpec(shape, lambda i, scalars: (0, 0, 1 - scalars[0])),
        ]

    return pl.pallas_call(
        split_kernel,
        out_shape=outs,
        grid_spec=pltpu.PrefetchScalarGridSpec(
            num_scalar_prefetch=1,
            grid=(1,),
            in_specs=half(query) + half(keys) + half(values),
            out_specs=[pl.BlockSpec(o.shape, lambda i, *_: (0, 0, 0)) for o in outs],
        ),
        compiler_params=pltpu.CompilerParams(vmem_limit_bytes=16 << 20),
        name="split_heads",
    )(scalars, query, query, keys, keys, values, values)


def by_seq(shape):
    return pl.BlockSpec((1,) + shape[1:], lambda s, *_: (s,) + (0,) * (len(shape) - 1))


def forward(scalars, mine, recv, kvs, doc_mine, doc_recv):
    seqs, rows, width = mine.shape
    keys = 2 * rows * len(kvs)
    outs = (
        jax.ShapeDtypeStruct((seqs, 2 * rows, width), jnp.bfloat16),
        jax.ShapeDtypeStruct((seqs, 2, keys, 2 * rows), jnp.bfloat16),
    )
    query_spec = by_seq(mine.shape)
    recv_spec = pl.BlockSpec((1, rows, width), lambda s, *_: (s, 0, 0))
    return pl.pallas_call(
        forward_kernel,
        out_shape=outs,
        grid_spec=pltpu.PrefetchScalarGridSpec(
            num_scalar_prefetch=1,
            grid=(seqs,),
            in_specs=[query_spec, recv_spec]
            + [by_seq(kv.shape) for kv in kvs]
            + [by_seq(doc_mine.shape), by_seq(doc_recv.shape)],
            out_specs=[by_seq(o.shape) for o in outs],
        ),
        compiler_params=pltpu.CompilerParams(vmem_limit_bytes=20 << 20),
        cost_estimate=pl.CostEstimate(
            flops=4 * seqs * 2 * 2 * rows * keys * HEAD_SIZE,
            transcendentals=seqs * 2 * 2 * rows * keys,
            bytes_accessed=8 << 20,
        ),
        name="attention_forward",
    )(scalars, mine, recv, *kvs, doc_mine, doc_recv)


def early_projection(scalars, pieces, o_weight):
    rows = sum(p.shape[0] * p.shape[1] for p in pieces)
    features, both = o_weight.shape
    width = both // 2
    steps = 7
    block = features // steps
    outs = (
        jax.ShapeDtypeStruct((rows, width), jnp.bfloat16),
        jax.ShapeDtypeStruct((features, rows), jnp.bfloat16),
    )
    return pl.pallas_call(
        early_kernel,
        out_shape=outs,
        grid_spec=pltpu.PrefetchScalarGridSpec(
            num_scalar_prefetch=1,
            grid=(steps,),
            in_specs=[pl.BlockSpec(p.shape[:2] + (block,), lambda i, *_: (0, 0, i)) for p in pieces]
            + [pl.BlockSpec((block, width), lambda i, scalars: (i, scalars[0]))],
            out_specs=[
                pl.BlockSpec((rows, width), lambda i, *_: (0, 0)),
                pl.BlockSpec((block, rows), lambda i, *_: (i, 0)),
            ],
            scratch_shapes=[pltpu.VMEM((rows, width), jnp.float32)],
        ),
        compiler_params=pltpu.CompilerParams(vmem_limit_bytes=16 << 20),
        cost_estimate=pl.CostEstimate(
            flops=20 * rows * features * width, transcendentals=0, bytes_accessed=12 << 20
        ),
        name="projection_early",
    )(scalars, *pieces, o_weight)


def late_projection(scalars, pieces, rows_t, attn, early, o_weight):
    width = attn.shape[-1]
    features = o_weight.shape[0]
    late_rows = sum(p.shape[0] * p.shape[1] for p in pieces)
    steps = 2
    block = features // steps
    out_rows = features // (CHIPS_Y * CHIPS_Z)
    slab = jax.ShapeDtypeStruct((2, CHIPS_Z // 2, out_rows, width), jnp.bfloat16)

    def whole(a):
        return pl.BlockSpec(a.shape, lambda i, *_: (0,) * len(a.shape))

    return pl.pallas_call(
        late_kernel,
        out_shape=(jax.ShapeDtypeStruct(attn.shape, jnp.bfloat16),) + (slab,) * 4,
        grid_spec=pltpu.PrefetchScalarGridSpec(
            num_scalar_prefetch=1,
            grid=(steps,),
            in_specs=[pl.BlockSpec(p.shape[:2] + (block,), lambda i, *_: (0, 0, i)) for p in pieces]
            + [pl.BlockSpec((block, r.shape[1]), lambda i, *_: (i, 0)) for r in rows_t]
            + [whole(attn)]
            + [whole(e) for e in early]
            + [pl.BlockSpec((block, width), lambda i, scalars: (i, scalars[0]))],
            out_specs=[whole(attn)] + [whole(slab)] * 4,
            scratch_shapes=[pltpu.VMEM((late_rows, width), jnp.float32)]
            + [pltpu.VMEM((r.shape[1], width), jnp.bfloat16) for r in rows_t]
            + [
                pltpu.VMEM((late_rows, width), jnp.bfloat16),
                pltpu.VMEM((block, width), jnp.float32),
            ],
        ),
        compiler_params=pltpu.CompilerParams(vmem_limit_bytes=32 << 20),
        cost_estimate=pl.CostEstimate(
            flops=2 * 6 * late_rows * features * width, transcendentals=0, bytes_accessed=12 << 20
        ),
        name="projection_late",
    )(scalars, *pieces, *rows_t, attn, *early, o_weight)


def backward(mine, recv, kvs, weights, attn, d_attn):
    seqs, rows, width = mine.shape
    half = jax.ShapeDtypeStruct((seqs, rows, width), jnp.bfloat16)
    shape = kvs[0].shape
    own = jax.ShapeDtypeStruct(shape, jnp.float32)
    sent = jax.ShapeDtypeStruct(shape, jnp.bfloat16)
    outs = (half, half, own) + (sent,) * (len(kvs) - 1)
    query_spec = by_seq(mine.shape)
    recv_spec = pl.BlockSpec((1, rows, width), lambda s, *_: (s, 0, 0))
    return pl.pallas_call(
        backward_kernel,
        out_shape=outs,
        grid=(seqs,),
        in_specs=[query_spec, recv_spec]
        + [by_seq(a.shape) for a in (*kvs, weights, attn, d_attn)],
        out_specs=[by_seq(o.shape) for o in outs],
        compiler_params=pltpu.CompilerParams(vmem_limit_bytes=20 << 20),
        cost_estimate=pl.CostEstimate(
            flops=10 * seqs * 2 * 2 * rows * 10 * rows * HEAD_SIZE,
            transcendentals=0,
            bytes_accessed=8 << 20,
        ),
        name="attention_backward",
    )(mine, recv, *kvs, weights, attn, d_attn)


def local(query, key_states, value_state_rows, d_out, o_weight, doc_start):
    seq_count, shard_rows, query_width = query.shape
    ctx = lax.axis_index("ctx")
    tp = lax.axis_index("tp")
    core = ctx % CORES
    y = ctx // CORES % CHIPS_Y
    chip_pos = ctx // CORES * (CORES * shard_rows)
    scalars = jnp.stack([core, tp, y, chip_pos]).astype(jnp.int32)
    first = core == 0
    q_mine, sent, kv_mine = split_heads(scalars, query, key_states, value_state_rows)

    r3 = tp_ahead(d_out, 1)
    r1 = tp_ahead(d_out, -1)
    recv = to_sibling(sent)
    doc_mine = doc_start[:, None, :]
    doc_recv = to_sibling(doc_mine)
    t0 = to_sibling(d_out)
    recv, doc_recv, t0, scalars, first = lax.optimization_barrier(
        (recv, doc_recv, t0, scalars, first)
    )
    kv0 = jnp.concatenate([kv_mine, recv[..., -2 * HEAD_SIZE :]], axis=1)
    kv1, kv3, kv4 = (chips_ahead(kv0, d) for d in (1, 3, 4))
    own, own_t = early_projection(scalars, [d_out, t0], o_weight)

    r1, r3, own, kv1, kv3, kv4, kv_again = lax.optimization_barrier(
        (r1, r3, own, kv1, kv3, kv4, kv0)
    )
    kv2 = chips_ahead(kv_again, 2)
    r2a = tp_ahead(r3[:1], 1)
    r2b = tp_ahead(r1[1:], -1)
    near, near_t = early_projection(
        scalars, [r1, r3, to_sibling(r1), to_sibling(r3)], o_weight
    )
    near, r2a, r2b, kv2 = lax.optimization_barrier((near, r2a, r2b, kv2))
    kvs = [kv0, kv1, kv2, kv3, kv4]
    attn, weights = forward(scalars, q_mine, recv, kvs, doc_mine, doc_recv)
    d_attn, sent_a, kept_a, sent_b, kept_b = late_projection(
        scalars,
        [r2a, r2b, to_sibling(r2a), to_sibling(r2b)],
        [own_t, near_t],
        attn,
        [own, near],
        o_weight,
    )
    got_a = y_route(sent_a, y_pair)
    got_b = y_route(sent_b, y_mirror)
    dq_mine, dq_other, g_own, *g_sent = backward(
        q_mine, recv, kvs, weights, attn, d_attn
    )
    *g_near, g_far = g_sent
    g_far = chips_ahead(g_far, -4)
    dq_recv = to_sibling(dq_other)
    got_a, got_b, g_own, g_far, dq_recv = lax.optimization_barrier(
        (got_a, got_b, g_own, g_far, dq_recv)
    )

    def added(*blocks):
        total = blocks[0].astype(jnp.float32)
        for block in blocks[1:]:
            total = total + block.astype(jnp.float32)
        return total

    next_a = added(kept_a[1], got_a[1]).astype(jnp.bfloat16)
    next_b = added(kept_b[1], got_b[1]).astype(jnp.bfloat16)
    last_a = y_route(next_a, y_mirror)
    last_b = y_route(next_b, y_pair)
    w_sum = merge(kept_a, got_a, last_a, kept_b, got_b, last_b)
    w_sum, *g_near = lax.optimization_barrier((w_sum, *g_near))
    w_all = z_exchange(w_sum)
    g_near = [chips_ahead(g, -d) for d, g in enumerate(g_near, 1)]

    grads = added(g_own, *g_near, g_far).astype(jnp.bfloat16)
    g_mine = grads[:, :shard_rows]
    g_recv = to_sibling(grads[:, shard_rows:])

    def by_core(own, other):
        return jnp.concatenate(
            [jnp.where(first, own, other), jnp.where(first, other, own)], axis=-1
        )

    return (
        by_core(dq_mine, dq_recv),
        by_core(g_mine[..., :HEAD_SIZE], g_recv[..., :HEAD_SIZE]),
        by_core(g_mine[..., HEAD_SIZE:], g_recv[..., HEAD_SIZE:]),
        finish(w_all),
    )


def solution(mesh):
    return jax.shard_map(
        local,
        mesh=mesh,
        in_specs=(
            P(None, "ctx", "tp"),
            P(None, "ctx", "tp"),
            P(None, "ctx", "tp"),
            P(None, ("ctx", "tp"), None),
            P(None, "tp"),
            P(None, "ctx"),
        ),
        out_specs=(
            P(None, "ctx", "tp"),
            P(None, "ctx", "tp"),
            P(None, "ctx", "tp"),
            P("ctx", "tp"),
        ),
        check_vma=False,
    )
```

```python
import jax
import jax.numpy as jnp
from jax import lax
from jax.experimental import pallas as pl
from jax.experimental.pallas import tpu as pltpu
from jax.sharding import PartitionSpec as P

HEAD_SIZE = 128
WIN = 1024
CORES = 2
CHIPS_Y = 4
CHIPS_Z = 8
TP = 4
LOG2_E = 1.4426950408889634

score_scale = 168.0 ** (-0.5)

NT = (((1,), (1,)), ((), ()))
TN = (((0,), (0,)), ((), ()))
NN = (((1,), (0,)), ((), ()))


def dot(a, b, dims=NN):
    return lax.dot_general(a, b, dims, preferred_element_type=jnp.float32)


def ctx_shift(block, move):
    count = CORES * CHIPS_Y * CHIPS_Z
    return lax.ppermute(block, "ctx", [(i, move(i)) for i in range(count)])


def to_sibling(block):
    return ctx_shift(block, lambda i: i ^ 1)


def y_pair(y):
    return y ^ 1


def y_mirror(y):
    return CHIPS_Y - 1 - y


def y_route(block, target):
    def move(i):
        core, y, z = i % CORES, i // CORES % CHIPS_Y, i // (CORES * CHIPS_Y)
        return (z * CHIPS_Y + target(y)) * CORES + core

    return ctx_shift(block, move)


def z_exchange(blocks):
    groups = [
        [(z * CHIPS_Y + y) * CORES + core for z in range(CHIPS_Z) for core in range(CORES)]
        for y in range(CHIPS_Y)
    ]
    return lax.all_to_all(blocks, "ctx", 0, 0, axis_index_groups=groups, tiled=True)


def chips_ahead(block, distance):
    count = CORES * CHIPS_Y * CHIPS_Z
    return ctx_shift(block, lambda i: (i + CORES * distance) % count)


def tp_ahead(block, distance):
    return lax.ppermute(block, "tp", [(i, (i + distance) % TP) for i in range(TP)])


def query_positions(core, chip_pos, rows):
    lane = lax.broadcasted_iota(jnp.int32, (1, 2 * rows), 1)
    other = lane >= rows
    first = jnp.where(other, (1 - core) * rows - rows, core * rows)
    return chip_pos + first + lane


def forward_kernel(
    scalars, mine, recv, kv0, kv1, kv2, kv3, kv4, doc_mine, doc_recv, attn, weights
):
    core, chip_pos = scalars[0], scalars[3]
    kvs = [kv[0] for kv in (kv0, kv1, kv2, kv3, kv4)]
    rows = mine.shape[1]
    query_pos = query_positions(core, chip_pos, rows)
    doc = jnp.concatenate([doc_mine[0], doc_recv[0]], axis=1)
    lowest = jnp.maximum(doc, query_pos - (WIN - 1))
    index = lax.broadcasted_iota(jnp.int32, (2 * rows, 2 * rows), 0)
    offset = index + jnp.where(index >= rows, (1 - core) * rows - rows, core * rows)
    for h in range(2):
        cols = slice(h * HEAD_SIZE, (h + 1) * HEAD_SIZE)
        q = jnp.concatenate([mine[0, :, cols], recv[0, :, cols]], axis=0)
        scores = []
        for d, kv in enumerate(kvs):
            s = dot(kv[:, :HEAD_SIZE], q, NT) * (score_scale * LOG2_E)
            key_pos = offset + (chip_pos - 2 * rows * d)
            visible = key_pos >= lowest
            if d == 0:
                visible = visible & (key_pos <= query_pos)
            scores.append(jnp.where(visible, s, -1e30))
        top = scores[0]
        for s in scores[1:]:
            top = jnp.maximum(top, s)
        top = jnp.max(top, axis=0, keepdims=True)
        expo = [jnp.exp2(s - top) for s in scores]
        total = expo[0]
        for e in expo[1:]:
            total = total + e
        inverse = 1.0 / jnp.sum(total, axis=0, keepdims=True)
        acc = None
        for d, kv in enumerate(kvs):
            w = (expo[d] * inverse).astype(jnp.bfloat16)
            weights[0, h, 2 * rows * d : 2 * rows * (d + 1), :] = w
            part = dot(kv[:, HEAD_SIZE:], w, TN)
            acc = part if acc is None else acc + part
        attn[0, :, cols] = acc.T.astype(jnp.bfloat16)


def early_kernel(scalars, *refs):
    *pieces, o_weight, d_attn, rows_t, acc = refs
    step = pl.program_id(0)
    parts = [ref[seq] for ref in pieces for seq in range(ref.shape[0])]
    rows = jnp.concatenate(parts, axis=0)
    product = dot(rows, o_weight[...])

    @pl.when(step == 0)
    def _():
        acc[...] = product

    @pl.when(step > 0)
    def _():
        acc[...] = acc[...] + product

    rows_t[...] = rows.T

    @pl.when(step == pl.num_programs(0) - 1)
    def _():
        d_attn[...] = acc[...].astype(jnp.bfloat16)


def place(tp, piece, core_block, rel, seq):
    here = TP * piece * core_block + piece * ((tp + rel) % TP)
    return seq, pl.ds(pl.multiple_of(here, piece), piece)


OWN_SLOTS = [(b, 0, q) for b in range(2) for q in range(2)]
NEAR_SLOTS = [(b, s, q) for b in range(2) for s in (1, 3) for q in range(2)]
FAR_SLOTS = [(b, 2, q) for b in range(2) for q in range(2)]


def late_kernel(
    scalars, r2a, r2b, t2a, t2b, own_t, near_t, attn, own, near, o_weight,
    d_attn, sent_a, kept_a, sent_b, kept_b, acc, attn_own, attn_near, attn_far, partial,
):
    step = pl.program_id(0)
    tp, y = scalars[1], scalars[2]
    piece = r2a.shape[1]
    out_rows = sent_a.shape[2]

    @pl.when(step == 0)
    def _():
        for slots, kept in ((OWN_SLOTS, attn_own), (NEAR_SLOTS, attn_near), (FAR_SLOTS, attn_far)):
            for n, slot in enumerate(slots):
                seq, here = place(tp, piece, *slot)
                kept[n * piece : (n + 1) * piece, :] = attn[seq, here, :]
        for slots, done in ((OWN_SLOTS, own), (NEAR_SLOTS, near)):
            for n, slot in enumerate(slots):
                seq, here = place(tp, piece, *slot)
                d_attn[seq, here, :] = done[n * piece : (n + 1) * piece, :]

    rows = jnp.concatenate([r2a[0], r2b[0], t2a[0], t2b[0]], axis=0)
    partial[...] = (
        dot(own_t[...], attn_own[...])
        + dot(near_t[...], attn_near[...])
        + dot(rows.T, attn_far[...])
    )

    def emit(out, order):
        for n, target in enumerate(order):
            for z in range(out.shape[1]):
                start = pl.multiple_of((CHIPS_Y * z + target) * out_rows, 8)
                out[n, z] = partial[pl.ds(start, out_rows), :].astype(jnp.bfloat16)

    pair = y + 1 - 2 * (y % 2)
    mirror = CHIPS_Y - 1 - y
    mirror_pair = mirror + 1 - 2 * (mirror % 2)

    product = dot(rows, o_weight[...])

    @pl.when(step == 0)
    def _():
        emit(sent_a, (pair, CHIPS_Y - 1 - pair))
        emit(kept_a, (y, mirror))
        acc[...] = product

    @pl.when(step == 1)
    def _():
        emit(sent_b, (mirror, mirror_pair))
        emit(kept_b, (y, pair))
        total = (acc[...] + product).astype(jnp.bfloat16)
        for n, slot in enumerate(FAR_SLOTS):
            seq, here = place(tp, piece, *slot)
            d_attn[seq, here, :] = total[n * piece : (n + 1) * piece, :]


def backward_kernel(
    mine, recv, kv0, kv1, kv2, kv3, kv4, weights, attn, d_attn,
    dq_mine, dq_other, g_own, g1, g2, g3, g4,
):
    rows = mine.shape[1]
    kvs = [kv[0] for kv in (kv0, kv1, kv2, kv3, kv4)]
    heads = []
    for h in range(2):
        cols = slice(h * HEAD_SIZE, (h + 1) * HEAD_SIZE)
        q = jnp.concatenate([mine[0, :, cols], recv[0, :, cols]], axis=0)
        da = d_attn[0, :, cols]
        product = da.astype(jnp.float32) * attn[0, :, cols].astype(jnp.float32)
        delta = jnp.sum(product.T, axis=0, keepdims=True)
        heads.append((q, da, delta))
    dq = [None, None]
    grads = (g_own, g1, g2, g3, g4)
    for kv_index, (kv, grad) in enumerate(zip(kvs, grads)):
        keys = kv[:, :HEAD_SIZE]
        values = kv[:, HEAD_SIZE:]
        dk = dv = None
        for h, (q, da, delta) in enumerate(heads):
            w = weights[0, h, 2 * rows * kv_index : 2 * rows * (kv_index + 1), :]
            dp = dot(values, da, NT)
            ds = (w.astype(jnp.float32) * (dp - delta)).astype(jnp.bfloat16)
            v_part = dot(w, da)
            k_part = dot(ds, q)
            q_part = dot(keys, ds, TN)
            dv = v_part if dv is None else dv + v_part
            dk = k_part if dk is None else dk + k_part
            dq[h] = q_part if dq[h] is None else dq[h] + q_part
        grad[0, :, :HEAD_SIZE] = (dk * score_scale).astype(grad.dtype)
        grad[0, :, HEAD_SIZE:] = dv.astype(grad.dtype)
    for h in range(2):
        cols = slice(h * HEAD_SIZE, (h + 1) * HEAD_SIZE)
        full = (dq[h].T * score_scale).astype(jnp.bfloat16)
        dq_mine[0, :, cols] = full[:rows]
        dq_other[0, :, cols] = full[rows:]


def merge_kernel(kept_a, got_a, last_a, kept_b, got_b, last_b, out):
    half = kept_a.shape[1]
    rows = out.shape[1]
    for part, (kept, got, last) in enumerate(((kept_a, got_a, last_a), (kept_b, got_b, last_b))):
        for z in range(half):
            total = (
                kept[0, z].astype(jnp.float32)
                + got[0, z].astype(jnp.float32)
                + last[z].astype(jnp.float32)
            )
            for core in range(CORES):
                slot = CORES * (half * part + z) + core
                out[slot] = total[core * rows : (core + 1) * rows].astype(jnp.bfloat16)


def finish_kernel(blocks, out):
    width = blocks.shape[2]
    for core in range(CORES):
        total = blocks[core].astype(jnp.float32)
        for z in range(1, CHIPS_Z):
            total = total + blocks[CORES * z + core].astype(jnp.float32)
        out[:, core * width : (core + 1) * width] = total


def merge(kept_a, got_a, last_a, kept_b, got_b, last_b):
    _, half, rows, width = kept_a.shape
    front = pl.BlockSpec((1, half, rows, width), lambda i: (0, 0, 0, 0))
    flat = pl.BlockSpec((half, rows, width), lambda i: (0, 0, 0))
    shape = (CORES * 2 * half, rows // CORES, width)
    return pl.pallas_call(
        merge_kernel,
        out_shape=jax.ShapeDtypeStruct(shape, jnp.bfloat16),
        grid=(1,),
        in_specs=[front, front, flat] * 2,
        out_specs=pl.BlockSpec(shape, lambda i: (0, 0, 0)),
        compiler_params=pltpu.CompilerParams(vmem_limit_bytes=16 << 20),
        name="projection_merge",
    )(kept_a, got_a, last_a, kept_b, got_b, last_b)


def finish(blocks):
    count, rows, width = blocks.shape
    return pl.pallas_call(
        finish_kernel,
        out_shape=jax.ShapeDtypeStruct((rows, CORES * width), jnp.float32),
        compiler_params=pltpu.CompilerParams(vmem_limit_bytes=16 << 20),
        name="projection_finish",
    )(blocks)


def split_kernel(
    scalars, q_own, q_other, k_own, k_other, v_own, v_other,
    q_mine, sent, kv_mine,
):
    width = q_other.shape[2]
    q_mine[...] = q_own[...]
    sent[:, :, :width] = q_other[...]
    sent[:, :, width : width + HEAD_SIZE] = k_other[...]
    sent[:, :, width + HEAD_SIZE :] = v_other[...]
    kv_mine[:, :, :HEAD_SIZE] = k_own[...]
    kv_mine[:, :, HEAD_SIZE:] = v_own[...]


def split_heads(scalars, query, keys, values):
    seqs, rows, width = query.shape
    out = jax.ShapeDtypeStruct((seqs, rows, width // 2), jnp.bfloat16)
    whole = jax.ShapeDtypeStruct(query.shape, jnp.bfloat16)
    outs = (out, whole, out)

    def half(a):
        shape = a.shape[:2] + (a.shape[2] // 2,)
        return [
            pl.BlockSpec(shape, lambda i, scalars: (0, 0, scalars[0])),
            pl.BlockSpec(shape, lambda i, scalars: (0, 0, 1 - scalars[0])),
        ]

    return pl.pallas_call(
        split_kernel,
        out_shape=outs,
        grid_spec=pltpu.PrefetchScalarGridSpec(
            num_scalar_prefetch=1,
            grid=(1,),
            in_specs=half(query) + half(keys) + half(values),
            out_specs=[pl.BlockSpec(o.shape, lambda i, *_: (0, 0, 0)) for o in outs],
        ),
        compiler_params=pltpu.CompilerParams(vmem_limit_bytes=16 << 20),
        name="split_heads",
    )(scalars, query, query, keys, keys, values, values)


def by_seq(shape):
    return pl.BlockSpec((1,) + shape[1:], lambda s, *_: (s,) + (0,) * (len(shape) - 1))


def forward(scalars, mine, recv, kvs, doc_mine, doc_recv):
    seqs, rows, width = mine.shape
    keys = 2 * rows * len(kvs)
    outs = (
        jax.ShapeDtypeStruct((seqs, 2 * rows, width), jnp.bfloat16),
        jax.ShapeDtypeStruct((seqs, 2, keys, 2 * rows), jnp.bfloat16),
    )
    query_spec = by_seq(mine.shape)
    recv_spec = pl.BlockSpec((1, rows, width), lambda s, *_: (s, 0, 0))
    return pl.pallas_call(
        forward_kernel,
        out_shape=outs,
        grid_spec=pltpu.PrefetchScalarGridSpec(
            num_scalar_prefetch=1,
            grid=(seqs,),
            in_specs=[query_spec, recv_spec]
            + [by_seq(kv.shape) for kv in kvs]
            + [by_seq(doc_mine.shape), by_seq(doc_recv.shape)],
            out_specs=[by_seq(o.shape) for o in outs],
        ),
        compiler_params=pltpu.CompilerParams(vmem_limit_bytes=20 << 20),
        cost_estimate=pl.CostEstimate(
            flops=4 * seqs * 2 * 2 * rows * keys * HEAD_SIZE,
            transcendentals=seqs * 2 * 2 * rows * keys,
            bytes_accessed=8 << 20,
        ),
        name="attention_forward",
    )(scalars, mine, recv, *kvs, doc_mine, doc_recv)


def early_projection(scalars, pieces, o_weight):
    rows = sum(p.shape[0] * p.shape[1] for p in pieces)
    features, both = o_weight.shape
    width = both // 2
    steps = 7
    block = features // steps
    outs = (
        jax.ShapeDtypeStruct((rows, width), jnp.bfloat16),
        jax.ShapeDtypeStruct((features, rows), jnp.bfloat16),
    )
    return pl.pallas_call(
        early_kernel,
        out_shape=outs,
        grid_spec=pltpu.PrefetchScalarGridSpec(
            num_scalar_prefetch=1,
            grid=(steps,),
            in_specs=[pl.BlockSpec(p.shape[:2] + (block,), lambda i, *_: (0, 0, i)) for p in pieces]
            + [pl.BlockSpec((block, width), lambda i, scalars: (i, scalars[0]))],
            out_specs=[
                pl.BlockSpec((rows, width), lambda i, *_: (0, 0)),
                pl.BlockSpec((block, rows), lambda i, *_: (i, 0)),
            ],
            scratch_shapes=[pltpu.VMEM((rows, width), jnp.float32)],
        ),
        compiler_params=pltpu.CompilerParams(vmem_limit_bytes=16 << 20),
        cost_estimate=pl.CostEstimate(
            flops=20 * rows * features * width, transcendentals=0, bytes_accessed=12 << 20
        ),
        name="projection_early",
    )(scalars, *pieces, o_weight)


def late_projection(scalars, pieces, rows_t, attn, early, o_weight):
    width = attn.shape[-1]
    features = o_weight.shape[0]
    late_rows = sum(p.shape[0] * p.shape[1] for p in pieces)
    steps = 2
    block = features // steps
    out_rows = features // (CHIPS_Y * CHIPS_Z)
    slab = jax.ShapeDtypeStruct((2, CHIPS_Z // 2, out_rows, width), jnp.bfloat16)

    def whole(a):
        return pl.BlockSpec(a.shape, lambda i, *_: (0,) * len(a.shape))

    return pl.pallas_call(
        late_kernel,
        out_shape=(jax.ShapeDtypeStruct(attn.shape, jnp.bfloat16),) + (slab,) * 4,
        grid_spec=pltpu.PrefetchScalarGridSpec(
            num_scalar_prefetch=1,
            grid=(steps,),
            in_specs=[pl.BlockSpec(p.shape[:2] + (block,), lambda i, *_: (0, 0, i)) for p in pieces]
            + [pl.BlockSpec((block, r.shape[1]), lambda i, *_: (i, 0)) for r in rows_t]
            + [whole(attn)]
            + [whole(e) for e in early]
            + [pl.BlockSpec((block, width), lambda i, scalars: (i, scalars[0]))],
            out_specs=[whole(attn)] + [whole(slab)] * 4,
            scratch_shapes=[pltpu.VMEM((late_rows, width), jnp.float32)]
            + [pltpu.VMEM((r.shape[1], width), jnp.bfloat16) for r in rows_t]
            + [
                pltpu.VMEM((late_rows, width), jnp.bfloat16),
                pltpu.VMEM((block, width), jnp.float32),
            ],
        ),
        compiler_params=pltpu.CompilerParams(vmem_limit_bytes=32 << 20),
        cost_estimate=pl.CostEstimate(
            flops=2 * 6 * late_rows * features * width, transcendentals=0, bytes_accessed=12 << 20
        ),
        name="projection_late",
    )(scalars, *pieces, *rows_t, attn, *early, o_weight)


def backward(mine, recv, kvs, weights, attn, d_attn):
    seqs, rows, width = mine.shape
    half = jax.ShapeDtypeStruct((seqs, rows, width), jnp.bfloat16)
    shape = kvs[0].shape
    own = jax.ShapeDtypeStruct(shape, jnp.float32)
    sent = jax.ShapeDtypeStruct(shape, jnp.bfloat16)
    outs = (half, half, own) + (sent,) * (len(kvs) - 1)
    query_spec = by_seq(mine.shape)
    recv_spec = pl.BlockSpec((1, rows, width), lambda s, *_: (s, 0, 0))
    return pl.pallas_call(
        backward_kernel,
        out_shape=outs,
        grid=(seqs,),
        in_specs=[query_spec, recv_spec]
        + [by_seq(a.shape) for a in (*kvs, weights, attn, d_attn)],
        out_specs=[by_seq(o.shape) for o in outs],
        compiler_params=pltpu.CompilerParams(vmem_limit_bytes=20 << 20),
        cost_estimate=pl.CostEstimate(
            flops=10 * seqs * 2 * 2 * rows * 10 * rows * HEAD_SIZE,
            transcendentals=0,
            bytes_accessed=8 << 20,
        ),
        name="attention_backward",
    )(mine, recv, *kvs, weights, attn, d_attn)


def local(query, key_states, value_state_rows, d_out, o_weight, doc_start):
    seq_count, shard_rows, query_width = query.shape
    ctx = lax.axis_index("ctx")
    tp = lax.axis_index("tp")
    core = ctx % CORES
    y = ctx // CORES % CHIPS_Y
    chip_pos = ctx // CORES * (CORES * shard_rows)
    scalars = jnp.stack([core, tp, y, chip_pos]).astype(jnp.int32)
    first = core == 0
    q_mine, sent, kv_mine = split_heads(scalars, query, key_states, value_state_rows)

    r3 = tp_ahead(d_out, 1)
    r1 = tp_ahead(d_out, -1)
    recv = to_sibling(sent)
    doc_mine = doc_start[:, None, :]
    doc_recv = to_sibling(doc_mine)
    t0 = to_sibling(d_out)
    recv, doc_recv, t0, scalars, first = lax.optimization_barrier(
        (recv, doc_recv, t0, scalars, first)
    )
    kv0 = jnp.concatenate([kv_mine, recv[..., -2 * HEAD_SIZE :]], axis=1)
    kv1, kv3, kv4 = (chips_ahead(kv0, d) for d in (1, 3, 4))
    own, own_t = early_projection(scalars, [d_out, t0], o_weight)

    r1, r3, own, kv1, kv3, kv4, kv_again = lax.optimization_barrier(
        (r1, r3, own, kv1, kv3, kv4, kv0)
    )
    kv2 = chips_ahead(kv_again, 2)
    r2a = tp_ahead(r3[:1], 1)
    r2b = tp_ahead(r1[1:], -1)
    near, near_t = early_projection(
        scalars, [r1, r3, to_sibling(r1), to_sibling(r3)], o_weight
    )
    near, r2a, r2b, kv2 = lax.optimization_barrier((near, r2a, r2b, kv2))
    kvs = [kv0, kv1, kv2, kv3, kv4]
    attn, weights = forward(scalars, q_mine, recv, kvs, doc_mine, doc_recv)
    d_attn, sent_a, kept_a, sent_b, kept_b = late_projection(
        scalars,
        [r2a, r2b, to_sibling(r2a), to_sibling(r2b)],
        [own_t, near_t],
        attn,
        [own, near],
        o_weight,
    )
    got_a = y_route(sent_a, y_pair)
    got_b = y_route(sent_b, y_mirror)
    dq_mine, dq_other, g_own, *g_sent = backward(
        q_mine, recv, kvs, weights, attn, d_attn
    )
    g_near, g_far = g_sent[:2], g_sent[2:]
    g_far = [chips_ahead(g, -d) for d, g in enumerate(g_far, 3)]
    dq_recv = to_sibling(dq_other)
    got_a, got_b, g_own, dq_recv, *g_far = lax.optimization_barrier(
        (got_a, got_b, g_own, dq_recv, *g_far)
    )

    def added(*blocks):
        total = blocks[0].astype(jnp.float32)
        for block in blocks[1:]:
            total = total + block.astype(jnp.float32)
        return total

    next_a = added(kept_a[1], got_a[1]).astype(jnp.bfloat16)
    next_b = added(kept_b[1], got_b[1]).astype(jnp.bfloat16)
    last_a = y_route(next_a, y_mirror)
    last_b = y_route(next_b, y_pair)
    w_sum = merge(kept_a, got_a, last_a, kept_b, got_b, last_b)
    w_sum, *g_near = lax.optimization_barrier((w_sum, *g_near))
    w_all = z_exchange(w_sum)
    g_near = [chips_ahead(g, -d) for d, g in enumerate(g_near, 1)]

    grads = added(g_own, *g_near, *g_far).astype(jnp.bfloat16)
    g_mine = grads[:, :shard_rows]
    g_recv = to_sibling(grads[:, shard_rows:])

    def by_core(own, other):
        return jnp.concatenate(
            [jnp.where(first, own, other), jnp.where(first, other, own)], axis=-1
        )

    return (
        by_core(dq_mine, dq_recv),
        by_core(g_mine[..., :HEAD_SIZE], g_recv[..., :HEAD_SIZE]),
        by_core(g_mine[..., HEAD_SIZE:], g_recv[..., HEAD_SIZE:]),
        finish(w_all),
    )


def solution(mesh):
    return jax.shard_map(
        local,
        mesh=mesh,
        in_specs=(
            P(None, "ctx", "tp"),
            P(None, "ctx", "tp"),
            P(None, "ctx", "tp"),
            P(None, ("ctx", "tp"), None),
            P(None, "tp"),
            P(None, "ctx"),
        ),
        out_specs=(
            P(None, "ctx", "tp"),
            P(None, "ctx", "tp"),
            P(None, "ctx", "tp"),
            P("ctx", "tp"),
        ),
        check_vma=False,
    )
```

```python
import jax
import jax.numpy as jnp
from jax import lax
from jax.experimental import pallas as pl
from jax.experimental.pallas import tpu as pltpu
from jax.sharding import PartitionSpec as P

HEAD_SIZE = 128
WIN = 1024
CORES = 2
CHIPS_Y = 4
CHIPS_Z = 8
TP = 4
LOG2_E = 1.4426950408889634

score_scale = 168.0 ** (-0.5)

NT = (((1,), (1,)), ((), ()))
TN = (((0,), (0,)), ((), ()))
NN = (((1,), (0,)), ((), ()))


def dot(a, b, dims=NN):
    return lax.dot_general(a, b, dims, preferred_element_type=jnp.float32)


def ctx_shift(block, move):
    count = CORES * CHIPS_Y * CHIPS_Z
    return lax.ppermute(block, "ctx", [(i, move(i)) for i in range(count)])


def to_sibling(block):
    return ctx_shift(block, lambda i: i ^ 1)


def y_pair(y):
    return y ^ 1


def y_mirror(y):
    return CHIPS_Y - 1 - y


def y_route(block, target):
    def move(i):
        core, y, z = i % CORES, i // CORES % CHIPS_Y, i // (CORES * CHIPS_Y)
        return (z * CHIPS_Y + target(y)) * CORES + core

    return ctx_shift(block, move)


def z_exchange(blocks):
    groups = [
        [(z * CHIPS_Y + y) * CORES + core for z in range(CHIPS_Z) for core in range(CORES)]
        for y in range(CHIPS_Y)
    ]
    return lax.all_to_all(blocks, "ctx", 0, 0, axis_index_groups=groups, tiled=True)


def chips_ahead(block, distance):
    count = CORES * CHIPS_Y * CHIPS_Z
    return ctx_shift(block, lambda i: (i + CORES * distance) % count)


def y_ahead(block, distance):
    return y_route(block, lambda y: (y + distance) % CHIPS_Y)


def tp_ahead(block, distance):
    return lax.ppermute(block, "tp", [(i, (i + distance) % TP) for i in range(TP)])


def query_positions(core, chip_pos, rows):
    lane = lax.broadcasted_iota(jnp.int32, (1, 2 * rows), 1)
    other = lane >= rows
    first = jnp.where(other, (1 - core) * rows - rows, core * rows)
    return chip_pos + first + lane


def forward_kernel(
    scalars, mine, recv, kv0, kv1, kv2, kv3, kv4, doc_mine, doc_recv, attn, weights
):
    core, chip_pos = scalars[0], scalars[3]
    kvs = [kv[0] for kv in (kv0, kv1, kv2, kv3, kv4)]
    rows = mine.shape[1]
    query_pos = query_positions(core, chip_pos, rows)
    doc = jnp.concatenate([doc_mine[0], doc_recv[0]], axis=1)
    lowest = jnp.maximum(doc, query_pos - (WIN - 1))
    index = lax.broadcasted_iota(jnp.int32, (2 * rows, 2 * rows), 0)
    offset = index + jnp.where(index >= rows, (1 - core) * rows - rows, core * rows)
    for h in range(2):
        cols = slice(h * HEAD_SIZE, (h + 1) * HEAD_SIZE)
        q = jnp.concatenate([mine[0, :, cols], recv[0, :, cols]], axis=0)
        scores = []
        for d, kv in enumerate(kvs):
            s = dot(kv[:, :HEAD_SIZE], q, NT) * (score_scale * LOG2_E)
            key_pos = offset + (chip_pos - 2 * rows * d)
            visible = key_pos >= lowest
            if d == 0:
                visible = visible & (key_pos <= query_pos)
            scores.append(jnp.where(visible, s, -1e30))
        top = scores[0]
        for s in scores[1:]:
            top = jnp.maximum(top, s)
        top = jnp.max(top, axis=0, keepdims=True)
        expo = [jnp.exp2(s - top) for s in scores]
        total = expo[0]
        for e in expo[1:]:
            total = total + e
        inverse = 1.0 / jnp.sum(total, axis=0, keepdims=True)
        acc = None
        for d, kv in enumerate(kvs):
            w = (expo[d] * inverse).astype(jnp.bfloat16)
            weights[0, h, 2 * rows * d : 2 * rows * (d + 1), :] = w
            part = dot(kv[:, HEAD_SIZE:], w, TN)
            acc = part if acc is None else acc + part
        attn[0, :, cols] = acc.T.astype(jnp.bfloat16)


def early_kernel(scalars, *refs):
    *pieces, o_weight, d_attn, rows_t, acc = refs
    step = pl.program_id(0)
    parts = [ref[seq] for ref in pieces for seq in range(ref.shape[0])]
    rows = jnp.concatenate(parts, axis=0)
    product = dot(rows, o_weight[...])

    @pl.when(step == 0)
    def _():
        acc[...] = product

    @pl.when(step > 0)
    def _():
        acc[...] = acc[...] + product

    rows_t[...] = rows.T

    @pl.when(step == pl.num_programs(0) - 1)
    def _():
        d_attn[...] = acc[...].astype(jnp.bfloat16)


def place(tp, piece, core_block, rel, seq):
    here = TP * piece * core_block + piece * ((tp + rel) % TP)
    return seq, pl.ds(pl.multiple_of(here, piece), piece)


OWN_SLOTS = [(b, 0, q) for b in range(2) for q in range(2)]
NEAR_SLOTS = [(b, s, q) for b in range(2) for s in (1, 3) for q in range(2)]
FAR_SLOTS = [(b, 2, q) for b in range(2) for q in range(2)]


def late_kernel(
    scalars, r2a, r2b, t2a, t2b, own_t, near_t, attn, own, near, o_weight,
    d_attn, sent_a, kept_a, sent_b, kept_b, acc, attn_own, attn_near, attn_far, partial,
):
    step = pl.program_id(0)
    tp, y = scalars[1], scalars[2]
    piece = r2a.shape[1]
    out_rows = sent_a.shape[2]

    @pl.when(step == 0)
    def _():
        for slots, kept in ((OWN_SLOTS, attn_own), (NEAR_SLOTS, attn_near), (FAR_SLOTS, attn_far)):
            for n, slot in enumerate(slots):
                seq, here = place(tp, piece, *slot)
                kept[n * piece : (n + 1) * piece, :] = attn[seq, here, :]
        for slots, done in ((OWN_SLOTS, own), (NEAR_SLOTS, near)):
            for n, slot in enumerate(slots):
                seq, here = place(tp, piece, *slot)
                d_attn[seq, here, :] = done[n * piece : (n + 1) * piece, :]

    rows = jnp.concatenate([r2a[0], r2b[0], t2a[0], t2b[0]], axis=0)
    partial[...] = (
        dot(own_t[...], attn_own[...])
        + dot(near_t[...], attn_near[...])
        + dot(rows.T, attn_far[...])
    )

    def emit(out, order):
        for n, target in enumerate(order):
            for z in range(out.shape[1]):
                start = pl.multiple_of((CHIPS_Y * z + target) * out_rows, 8)
                out[n, z] = partial[pl.ds(start, out_rows), :].astype(jnp.bfloat16)

    pair = y + 1 - 2 * (y % 2)
    mirror = CHIPS_Y - 1 - y
    mirror_pair = mirror + 1 - 2 * (mirror % 2)

    product = dot(rows, o_weight[...])

    @pl.when(step == 0)
    def _():
        emit(sent_a, (pair, CHIPS_Y - 1 - pair))
        emit(kept_a, (y, mirror))
        acc[...] = product

    @pl.when(step == 1)
    def _():
        emit(sent_b, (mirror, mirror_pair))
        emit(kept_b, (y, pair))
        total = (acc[...] + product).astype(jnp.bfloat16)
        for n, slot in enumerate(FAR_SLOTS):
            seq, here = place(tp, piece, *slot)
            d_attn[seq, here, :] = total[n * piece : (n + 1) * piece, :]


def backward_kernel(
    mine, recv, kv0, kv1, kv2, kv3, kv4, weights, attn, d_attn,
    dq_mine, dq_other, g_own, g1, g2, g3, g4,
):
    rows = mine.shape[1]
    kvs = [kv[0] for kv in (kv0, kv1, kv2, kv3, kv4)]
    heads = []
    for h in range(2):
        cols = slice(h * HEAD_SIZE, (h + 1) * HEAD_SIZE)
        q = jnp.concatenate([mine[0, :, cols], recv[0, :, cols]], axis=0)
        da = d_attn[0, :, cols]
        product = da.astype(jnp.float32) * attn[0, :, cols].astype(jnp.float32)
        delta = jnp.sum(product.T, axis=0, keepdims=True)
        heads.append((q, da, delta))
    dq = [None, None]
    grads = (g_own, g1, g2, g3, g4)
    for kv_index, (kv, grad) in enumerate(zip(kvs, grads)):
        keys = kv[:, :HEAD_SIZE]
        values = kv[:, HEAD_SIZE:]
        dk = dv = None
        for h, (q, da, delta) in enumerate(heads):
            w = weights[0, h, 2 * rows * kv_index : 2 * rows * (kv_index + 1), :]
            dp = dot(values, da, NT)
            ds = (w.astype(jnp.float32) * (dp - delta)).astype(jnp.bfloat16)
            v_part = dot(w, da)
            k_part = dot(ds, q)
            q_part = dot(keys, ds, TN)
            dv = v_part if dv is None else dv + v_part
            dk = k_part if dk is None else dk + k_part
            dq[h] = q_part if dq[h] is None else dq[h] + q_part
        grad[0, :, :HEAD_SIZE] = (dk * score_scale).astype(grad.dtype)
        grad[0, :, HEAD_SIZE:] = dv.astype(grad.dtype)
    for h in range(2):
        cols = slice(h * HEAD_SIZE, (h + 1) * HEAD_SIZE)
        full = (dq[h].T * score_scale).astype(jnp.bfloat16)
        dq_mine[0, :, cols] = full[:rows]
        dq_other[0, :, cols] = full[rows:]


def merge_kernel(kept_a, got_a, last_a, kept_b, got_b, last_b, out):
    half = kept_a.shape[1]
    rows = out.shape[1]
    for part, (kept, got, last) in enumerate(((kept_a, got_a, last_a), (kept_b, got_b, last_b))):
        for z in range(half):
            total = (
                kept[0, z].astype(jnp.float32)
                + got[0, z].astype(jnp.float32)
                + last[z].astype(jnp.float32)
            )
            for core in range(CORES):
                slot = CORES * (half * part + z) + core
                out[slot] = total[core * rows : (core + 1) * rows].astype(jnp.bfloat16)


def finish_kernel(blocks, out):
    width = blocks.shape[2]
    for core in range(CORES):
        total = blocks[core].astype(jnp.float32)
        for z in range(1, CHIPS_Z):
            total = total + blocks[CORES * z + core].astype(jnp.float32)
        out[:, core * width : (core + 1) * width] = total


def merge(kept_a, got_a, last_a, kept_b, got_b, last_b):
    _, half, rows, width = kept_a.shape
    front = pl.BlockSpec((1, half, rows, width), lambda i: (0, 0, 0, 0))
    flat = pl.BlockSpec((half, rows, width), lambda i: (0, 0, 0))
    shape = (CORES * 2 * half, rows // CORES, width)
    return pl.pallas_call(
        merge_kernel,
        out_shape=jax.ShapeDtypeStruct(shape, jnp.bfloat16),
        grid=(1,),
        in_specs=[front, front, flat] * 2,
        out_specs=pl.BlockSpec(shape, lambda i: (0, 0, 0)),
        compiler_params=pltpu.CompilerParams(vmem_limit_bytes=16 << 20),
        name="projection_merge",
    )(kept_a, got_a, last_a, kept_b, got_b, last_b)


def finish(blocks):
    count, rows, width = blocks.shape
    return pl.pallas_call(
        finish_kernel,
        out_shape=jax.ShapeDtypeStruct((rows, CORES * width), jnp.float32),
        compiler_params=pltpu.CompilerParams(vmem_limit_bytes=16 << 20),
        name="projection_finish",
    )(blocks)


def split_kernel(
    scalars, q_own, q_other, k_own, k_other, v_own, v_other,
    q_mine, sent, kv_mine,
):
    width = q_other.shape[2]
    q_mine[...] = q_own[...]
    sent[:, :, :width] = q_other[...]
    sent[:, :, width : width + HEAD_SIZE] = k_other[...]
    sent[:, :, width + HEAD_SIZE :] = v_other[...]
    kv_mine[:, :, :HEAD_SIZE] = k_own[...]
    kv_mine[:, :, HEAD_SIZE:] = v_own[...]


def split_heads(scalars, query, keys, values):
    seqs, rows, width = query.shape
    out = jax.ShapeDtypeStruct((seqs, rows, width // 2), jnp.bfloat16)
    whole = jax.ShapeDtypeStruct(query.shape, jnp.bfloat16)
    outs = (out, whole, out)

    def half(a):
        shape = a.shape[:2] + (a.shape[2] // 2,)
        return [
            pl.BlockSpec(shape, lambda i, scalars: (0, 0, scalars[0])),
            pl.BlockSpec(shape, lambda i, scalars: (0, 0, 1 - scalars[0])),
        ]

    return pl.pallas_call(
        split_kernel,
        out_shape=outs,
        grid_spec=pltpu.PrefetchScalarGridSpec(
            num_scalar_prefetch=1,
            grid=(1,),
            in_specs=half(query) + half(keys) + half(values),
            out_specs=[pl.BlockSpec(o.shape, lambda i, *_: (0, 0, 0)) for o in outs],
        ),
        compiler_params=pltpu.CompilerParams(vmem_limit_bytes=16 << 20),
        name="split_heads",
    )(scalars, query, query, keys, keys, values, values)


def by_seq(shape):
    return pl.BlockSpec((1,) + shape[1:], lambda s, *_: (s,) + (0,) * (len(shape) - 1))


def forward(scalars, mine, recv, kvs, doc_mine, doc_recv):
    seqs, rows, width = mine.shape
    keys = 2 * rows * len(kvs)
    outs = (
        jax.ShapeDtypeStruct((seqs, 2 * rows, width), jnp.bfloat16),
        jax.ShapeDtypeStruct((seqs, 2, keys, 2 * rows), jnp.bfloat16),
    )
    query_spec = by_seq(mine.shape)
    recv_spec = pl.BlockSpec((1, rows, width), lambda s, *_: (s, 0, 0))
    return pl.pallas_call(
        forward_kernel,
        out_shape=outs,
        grid_spec=pltpu.PrefetchScalarGridSpec(
            num_scalar_prefetch=1,
            grid=(seqs,),
            in_specs=[query_spec, recv_spec]
            + [by_seq(kv.shape) for kv in kvs]
            + [by_seq(doc_mine.shape), by_seq(doc_recv.shape)],
            out_specs=[by_seq(o.shape) for o in outs],
        ),
        compiler_params=pltpu.CompilerParams(vmem_limit_bytes=20 << 20),
        cost_estimate=pl.CostEstimate(
            flops=4 * seqs * 2 * 2 * rows * keys * HEAD_SIZE,
            transcendentals=seqs * 2 * 2 * rows * keys,
            bytes_accessed=8 << 20,
        ),
        name="attention_forward",
    )(scalars, mine, recv, *kvs, doc_mine, doc_recv)


def early_projection(scalars, pieces, o_weight):
    rows = sum(p.shape[0] * p.shape[1] for p in pieces)
    features, both = o_weight.shape
    width = both // 2
    steps = 7
    block = features // steps
    outs = (
        jax.ShapeDtypeStruct((rows, width), jnp.bfloat16),
        jax.ShapeDtypeStruct((features, rows), jnp.bfloat16),
    )
    return pl.pallas_call(
        early_kernel,
        out_shape=outs,
        grid_spec=pltpu.PrefetchScalarGridSpec(
            num_scalar_prefetch=1,
            grid=(steps,),
            in_specs=[pl.BlockSpec(p.shape[:2] + (block,), lambda i, *_: (0, 0, i)) for p in pieces]
            + [pl.BlockSpec((block, width), lambda i, scalars: (i, scalars[0]))],
            out_specs=[
                pl.BlockSpec((rows, width), lambda i, *_: (0, 0)),
                pl.BlockSpec((block, rows), lambda i, *_: (i, 0)),
            ],
            scratch_shapes=[pltpu.VMEM((rows, width), jnp.float32)],
        ),
        compiler_params=pltpu.CompilerParams(vmem_limit_bytes=16 << 20),
        cost_estimate=pl.CostEstimate(
            flops=20 * rows * features * width, transcendentals=0, bytes_accessed=12 << 20
        ),
        name="projection_early",
    )(scalars, *pieces, o_weight)


def late_projection(scalars, pieces, rows_t, attn, early, o_weight):
    width = attn.shape[-1]
    features = o_weight.shape[0]
    late_rows = sum(p.shape[0] * p.shape[1] for p in pieces)
    steps = 2
    block = features // steps
    out_rows = features // (CHIPS_Y * CHIPS_Z)
    slab = jax.ShapeDtypeStruct((2, CHIPS_Z // 2, out_rows, width), jnp.bfloat16)

    def whole(a):
        return pl.BlockSpec(a.shape, lambda i, *_: (0,) * len(a.shape))

    return pl.pallas_call(
        late_kernel,
        out_shape=(jax.ShapeDtypeStruct(attn.shape, jnp.bfloat16),) + (slab,) * 4,
        grid_spec=pltpu.PrefetchScalarGridSpec(
            num_scalar_prefetch=1,
            grid=(steps,),
            in_specs=[pl.BlockSpec(p.shape[:2] + (block,), lambda i, *_: (0, 0, i)) for p in pieces]
            + [pl.BlockSpec((block, r.shape[1]), lambda i, *_: (i, 0)) for r in rows_t]
            + [whole(attn)]
            + [whole(e) for e in early]
            + [pl.BlockSpec((block, width), lambda i, scalars: (i, scalars[0]))],
            out_specs=[whole(attn)] + [whole(slab)] * 4,
            scratch_shapes=[pltpu.VMEM((late_rows, width), jnp.float32)]
            + [pltpu.VMEM((r.shape[1], width), jnp.bfloat16) for r in rows_t]
            + [
                pltpu.VMEM((late_rows, width), jnp.bfloat16),
                pltpu.VMEM((block, width), jnp.float32),
            ],
        ),
        compiler_params=pltpu.CompilerParams(vmem_limit_bytes=32 << 20),
        cost_estimate=pl.CostEstimate(
            flops=2 * 6 * late_rows * features * width, transcendentals=0, bytes_accessed=12 << 20
        ),
        name="projection_late",
    )(scalars, *pieces, *rows_t, attn, *early, o_weight)


def backward(mine, recv, kvs, weights, attn, d_attn):
    seqs, rows, width = mine.shape
    half = jax.ShapeDtypeStruct((seqs, rows, width), jnp.bfloat16)
    shape = kvs[0].shape
    own = jax.ShapeDtypeStruct(shape, jnp.float32)
    sent = jax.ShapeDtypeStruct(shape, jnp.bfloat16)
    outs = (half, half, own) + (sent,) * (len(kvs) - 1)
    query_spec = by_seq(mine.shape)
    recv_spec = pl.BlockSpec((1, rows, width), lambda s, *_: (s, 0, 0))
    return pl.pallas_call(
        backward_kernel,
        out_shape=outs,
        grid=(seqs,),
        in_specs=[query_spec, recv_spec]
        + [by_seq(a.shape) for a in (*kvs, weights, attn, d_attn)],
        out_specs=[by_seq(o.shape) for o in outs],
        compiler_params=pltpu.CompilerParams(vmem_limit_bytes=20 << 20),
        cost_estimate=pl.CostEstimate(
            flops=10 * seqs * 2 * 2 * rows * 10 * rows * HEAD_SIZE,
            transcendentals=0,
            bytes_accessed=8 << 20,
        ),
        name="attention_backward",
    )(mine, recv, *kvs, weights, attn, d_attn)


def local(query, key_states, value_state_rows, d_out, o_weight, doc_start):
    seq_count, shard_rows, query_width = query.shape
    ctx = lax.axis_index("ctx")
    tp = lax.axis_index("tp")
    core = ctx % CORES
    y = ctx // CORES % CHIPS_Y
    chip_pos = ctx // CORES * (CORES * shard_rows)
    scalars = jnp.stack([core, tp, y, chip_pos]).astype(jnp.int32)
    first = core == 0
    q_mine, sent, kv_mine = split_heads(scalars, query, key_states, value_state_rows)

    r3 = tp_ahead(d_out, 1)
    r1 = tp_ahead(d_out, -1)
    recv = to_sibling(sent)
    doc_mine = doc_start[:, None, :]
    doc_recv = to_sibling(doc_mine)
    t0 = to_sibling(d_out)
    recv, doc_recv, t0, scalars, first, one_row, two_rows = lax.optimization_barrier(
        (recv, doc_recv, t0, scalars, first, y < 1, y < 2)
    )
    kv0 = jnp.concatenate([kv_mine, recv[..., -2 * HEAD_SIZE :]], axis=1)
    kv4, kv1 = (chips_ahead(kv0, d) for d in (4, 1))
    own, own_t = early_projection(scalars, [d_out, t0], o_weight)

    kv_two = jnp.where(two_rows, kv0, kv4)
    kv_three = jnp.where(one_row, kv0, kv4)
    r1, r3, own, kv1, kv_two, kv_three = lax.optimization_barrier(
        (r1, r3, own, kv1, kv_two, kv_three)
    )
    kv2, kv3 = y_ahead(kv_two, 2), y_ahead(kv_three, 3)
    r2a = tp_ahead(r3[:1], 1)
    r2b = tp_ahead(r1[1:], -1)
    near, near_t = early_projection(
        scalars, [r1, r3, to_sibling(r1), to_sibling(r3)], o_weight
    )
    near, r2a, r2b, kv2, kv3 = lax.optimization_barrier((near, r2a, r2b, kv2, kv3))
    kvs = [kv0, kv1, kv2, kv3, kv4]
    attn, weights = forward(scalars, q_mine, recv, kvs, doc_mine, doc_recv)
    d_attn, sent_a, kept_a, sent_b, kept_b = late_projection(
        scalars,
        [r2a, r2b, to_sibling(r2a), to_sibling(r2b)],
        [own_t, near_t],
        attn,
        [own, near],
        o_weight,
    )
    got_a = y_route(sent_a, y_pair)
    got_b = y_route(sent_b, y_mirror)
    dq_mine, dq_other, g_own, *g_sent = backward(
        q_mine, recv, kvs, weights, attn, d_attn
    )
    *g_near, g_far = (chips_ahead(g, -d) for d, g in enumerate(g_sent, 1))
    got_a, got_b, g_own, *g_near = lax.optimization_barrier((got_a, got_b, g_own, *g_near))
    dq_recv = to_sibling(dq_other)

    def added(*blocks):
        total = blocks[0].astype(jnp.float32)
        for block in blocks[1:]:
            total = total + block.astype(jnp.float32)
        return total

    next_a = added(kept_a[1], got_a[1]).astype(jnp.bfloat16)
    next_b = added(kept_b[1], got_b[1]).astype(jnp.bfloat16)
    last_a = y_route(next_a, y_mirror)
    last_b = y_route(next_b, y_pair)
    last_a, last_b, g_far = lax.optimization_barrier((last_a, last_b, g_far))
    w_sum = merge(kept_a, got_a, last_a, kept_b, got_b, last_b)
    w_all = z_exchange(w_sum)

    grads = added(g_own, *g_near, g_far).astype(jnp.bfloat16)
    g_mine = grads[:, :shard_rows]
    g_recv = to_sibling(grads[:, shard_rows:])

    def by_core(own, other):
        return jnp.concatenate(
            [jnp.where(first, own, other), jnp.where(first, other, own)], axis=-1
        )

    return (
        by_core(dq_mine, dq_recv),
        by_core(g_mine[..., :HEAD_SIZE], g_recv[..., :HEAD_SIZE]),
        by_core(g_mine[..., HEAD_SIZE:], g_recv[..., HEAD_SIZE:]),
        finish(w_all),
    )


def solution(mesh):
    return jax.shard_map(
        local,
        mesh=mesh,
        in_specs=(
            P(None, "ctx", "tp"),
            P(None, "ctx", "tp"),
            P(None, "ctx", "tp"),
            P(None, ("ctx", "tp"), None),
            P(None, "tp"),
            P(None, "ctx"),
        ),
        out_specs=(
            P(None, "ctx", "tp"),
            P(None, "ctx", "tp"),
            P(None, "ctx", "tp"),
            P("ctx", "tp"),
        ),
        check_vma=False,
    )
```

```python
import jax
import jax.numpy as jnp
from jax import lax
from jax.experimental import pallas as pl
from jax.experimental.pallas import tpu as pltpu
from jax.sharding import PartitionSpec as P

HEAD_SIZE = 128
WIN = 1024
CORES = 2
CHIPS_Y = 4
CHIPS_Z = 8
TP = 4
LOG2_E = 1.4426950408889634

score_scale = 168.0 ** (-0.5)

NT = (((1,), (1,)), ((), ()))
TN = (((0,), (0,)), ((), ()))
NN = (((1,), (0,)), ((), ()))


def dot(a, b, dims=NN):
    return lax.dot_general(a, b, dims, preferred_element_type=jnp.float32)


def ctx_shift(block, move):
    count = CORES * CHIPS_Y * CHIPS_Z
    return lax.ppermute(block, "ctx", [(i, move(i)) for i in range(count)])


def to_sibling(block):
    return ctx_shift(block, lambda i: i ^ 1)


def y_pair(y):
    return y ^ 1


def y_mirror(y):
    return CHIPS_Y - 1 - y


def y_route(block, target):
    def move(i):
        core, y, z = i % CORES, i // CORES % CHIPS_Y, i // (CORES * CHIPS_Y)
        return (z * CHIPS_Y + target(y)) * CORES + core

    return ctx_shift(block, move)


def z_exchange(blocks):
    lanes = CORES * CHIPS_Y
    groups = [[z * lanes + lane for z in range(CHIPS_Z)] for lane in range(lanes)]
    return lax.all_to_all(blocks, "ctx", 0, 0, axis_index_groups=groups, tiled=True)


def chips_ahead(block, distance):
    count = CORES * CHIPS_Y * CHIPS_Z
    return ctx_shift(block, lambda i: (i + CORES * distance) % count)


def y_ahead(block, distance):
    return y_route(block, lambda y: (y + distance) % CHIPS_Y)


def tp_ahead(block, distance):
    return lax.ppermute(block, "tp", [(i, (i + distance) % TP) for i in range(TP)])


def query_positions(core, chip_pos, rows):
    lane = lax.broadcasted_iota(jnp.int32, (1, 2 * rows), 1)
    other = lane >= rows
    first = jnp.where(other, (1 - core) * rows - rows, core * rows)
    return chip_pos + first + lane


def forward_kernel(
    scalars, mine, recv, kv0, kv1, kv2, kv3, kv4, doc_mine, doc_recv, attn, weights
):
    core, chip_pos = scalars[0], scalars[3]
    kvs = [kv[0] for kv in (kv0, kv1, kv2, kv3, kv4)]
    rows = mine.shape[1]
    query_pos = query_positions(core, chip_pos, rows)
    doc = jnp.concatenate([doc_mine[0], doc_recv[0]], axis=1)
    lowest = jnp.maximum(doc, query_pos - (WIN - 1))
    index = lax.broadcasted_iota(jnp.int32, (2 * rows, 2 * rows), 0)
    offset = index + jnp.where(index >= rows, (1 - core) * rows - rows, core * rows)
    for h in range(2):
        cols = slice(h * HEAD_SIZE, (h + 1) * HEAD_SIZE)
        q = jnp.concatenate([mine[0, :, cols], recv[0, :, cols]], axis=0)
        scores = []
        for d, kv in enumerate(kvs):
            s = dot(kv[:, :HEAD_SIZE], q, NT) * (score_scale * LOG2_E)
            key_pos = offset + (chip_pos - 2 * rows * d)
            visible = key_pos >= lowest
            if d == 0:
                visible = visible & (key_pos <= query_pos)
            scores.append(jnp.where(visible, s, -1e30))
        top = scores[0]
        for s in scores[1:]:
            top = jnp.maximum(top, s)
        top = jnp.max(top, axis=0, keepdims=True)
        expo = [jnp.exp2(s - top) for s in scores]
        total = expo[0]
        for e in expo[1:]:
            total = total + e
        inverse = 1.0 / jnp.sum(total, axis=0, keepdims=True)
        acc = None
        for d, kv in enumerate(kvs):
            w = (expo[d] * inverse).astype(jnp.bfloat16)
            weights[0, h, 2 * rows * d : 2 * rows * (d + 1), :] = w
            part = dot(kv[:, HEAD_SIZE:], w, TN)
            acc = part if acc is None else acc + part
        attn[0, :, cols] = acc.T.astype(jnp.bfloat16)


def early_kernel(scalars, *refs):
    *pieces, o_weight, d_attn, rows_t, acc = refs
    step = pl.program_id(0)
    parts = [ref[seq] for ref in pieces for seq in range(ref.shape[0])]
    rows = jnp.concatenate(parts, axis=0)
    product = dot(rows, o_weight[...])

    @pl.when(step == 0)
    def _():
        acc[...] = product

    @pl.when(step > 0)
    def _():
        acc[...] = acc[...] + product

    rows_t[...] = rows.T

    @pl.when(step == pl.num_programs(0) - 1)
    def _():
        d_attn[...] = acc[...].astype(jnp.bfloat16)


def place(tp, piece, core_block, rel, seq):
    here = TP * piece * core_block + piece * ((tp + rel) % TP)
    return seq, pl.ds(pl.multiple_of(here, piece), piece)


OWN_SLOTS = [(b, 0, q) for b in range(2) for q in range(2)]
NEAR_SLOTS = [(b, s, q) for b in range(2) for s in (1, 3) for q in range(2)]
FAR_SLOTS = [(b, 2, q) for b in range(2) for q in range(2)]


def late_kernel(
    scalars, r2a, r2b, t2a, t2b, own_t, near_t, attn, own, near, o_weight,
    d_attn, sent_a, kept_a, sent_b, kept_b, acc, attn_own, attn_near, attn_far, partial,
):
    step = pl.program_id(0)
    tp, y = scalars[1], scalars[2]
    piece = r2a.shape[1]
    out_rows = sent_a.shape[2]

    @pl.when(step == 0)
    def _():
        for slots, kept in ((OWN_SLOTS, attn_own), (NEAR_SLOTS, attn_near), (FAR_SLOTS, attn_far)):
            for n, slot in enumerate(slots):
                seq, here = place(tp, piece, *slot)
                kept[n * piece : (n + 1) * piece, :] = attn[seq, here, :]
        for slots, done in ((OWN_SLOTS, own), (NEAR_SLOTS, near)):
            for n, slot in enumerate(slots):
                seq, here = place(tp, piece, *slot)
                d_attn[seq, here, :] = done[n * piece : (n + 1) * piece, :]

    rows = jnp.concatenate([r2a[0], r2b[0], t2a[0], t2b[0]], axis=0)
    partial[...] = (
        dot(own_t[...], attn_own[...])
        + dot(near_t[...], attn_near[...])
        + dot(rows.T, attn_far[...])
    )

    def emit(out, order):
        for n, target in enumerate(order):
            for z in range(out.shape[1]):
                start = pl.multiple_of((CHIPS_Y * z + target) * out_rows, 8)
                out[n, z] = partial[pl.ds(start, out_rows), :].astype(jnp.bfloat16)

    pair = y + 1 - 2 * (y % 2)
    mirror = CHIPS_Y - 1 - y
    mirror_pair = mirror + 1 - 2 * (mirror % 2)

    product = dot(rows, o_weight[...])

    @pl.when(step == 0)
    def _():
        emit(sent_a, (pair, CHIPS_Y - 1 - pair))
        emit(kept_a, (y, mirror))
        acc[...] = product

    @pl.when(step == 1)
    def _():
        emit(sent_b, (mirror, mirror_pair))
        emit(kept_b, (y, pair))
        total = (acc[...] + product).astype(jnp.bfloat16)
        for n, slot in enumerate(FAR_SLOTS):
            seq, here = place(tp, piece, *slot)
            d_attn[seq, here, :] = total[n * piece : (n + 1) * piece, :]


def backward_kernel(
    mine, recv, kv0, kv1, kv2, kv3, kv4, weights, attn, d_attn,
    dq_mine, dq_other, g_own, g1, g2, g3, g4,
):
    rows = mine.shape[1]
    kvs = [kv[0] for kv in (kv0, kv1, kv2, kv3, kv4)]
    heads = []
    for h in range(2):
        cols = slice(h * HEAD_SIZE, (h + 1) * HEAD_SIZE)
        q = jnp.concatenate([mine[0, :, cols], recv[0, :, cols]], axis=0)
        da = d_attn[0, :, cols]
        product = da.astype(jnp.float32) * attn[0, :, cols].astype(jnp.float32)
        delta = jnp.sum(product.T, axis=0, keepdims=True)
        heads.append((q, da, delta))
    dq = [None, None]
    grads = (g_own, g1, g2, g3, g4)
    for kv_index, (kv, grad) in enumerate(zip(kvs, grads)):
        keys = kv[:, :HEAD_SIZE]
        values = kv[:, HEAD_SIZE:]
        dk = dv = None
        for h, (q, da, delta) in enumerate(heads):
            w = weights[0, h, 2 * rows * kv_index : 2 * rows * (kv_index + 1), :]
            dp = dot(values, da, NT)
            ds = (w.astype(jnp.float32) * (dp - delta)).astype(jnp.bfloat16)
            v_part = dot(w, da)
            k_part = dot(ds, q)
            q_part = dot(keys, ds, TN)
            dv = v_part if dv is None else dv + v_part
            dk = k_part if dk is None else dk + k_part
            dq[h] = q_part if dq[h] is None else dq[h] + q_part
        grad[0, :, :HEAD_SIZE] = (dk * score_scale).astype(grad.dtype)
        grad[0, :, HEAD_SIZE:] = dv.astype(grad.dtype)
    for h in range(2):
        cols = slice(h * HEAD_SIZE, (h + 1) * HEAD_SIZE)
        full = (dq[h].T * score_scale).astype(jnp.bfloat16)
        dq_mine[0, :, cols] = full[:rows]
        dq_other[0, :, cols] = full[rows:]


def merge_kernel(scalars, kept_a, got_a, last_a, kept_b, got_b, last_b, own, sent):
    half = kept_a.shape[1]
    rows = own.shape[1]
    first = scalars[0] == 0
    for part, (kept, got, last) in enumerate(((kept_a, got_a, last_a), (kept_b, got_b, last_b))):
        for z in range(half):
            total = (
                kept[0, z].astype(jnp.float32)
                + got[0, z].astype(jnp.float32)
                + last[z].astype(jnp.float32)
            )
            top, bottom = total[:rows], total[rows:]
            own[half * part + z] = jnp.where(first, top, bottom).astype(jnp.bfloat16)
            sent[half * part + z] = jnp.where(first, bottom, top).astype(jnp.bfloat16)


def finish_kernel(scalars, blocks, out):
    width = blocks.shape[2] // CORES
    first = scalars[0] == 0
    total = blocks[0].astype(jnp.float32)
    for z in range(1, CHIPS_Z):
        total = total + blocks[z].astype(jnp.float32)
    own, other = total[:, :width], total[:, width:]
    out[:, :width] = jnp.where(first, own, other)
    out[:, width:] = jnp.where(first, other, own)


def merge(scalars, kept_a, got_a, last_a, kept_b, got_b, last_b):
    _, half, rows, width = kept_a.shape
    front = pl.BlockSpec((1, half, rows, width), lambda i, *_: (0, 0, 0, 0))
    flat = pl.BlockSpec((half, rows, width), lambda i, *_: (0, 0, 0))
    shape = (2 * half, rows // CORES, width)
    return pl.pallas_call(
        merge_kernel,
        out_shape=(jax.ShapeDtypeStruct(shape, jnp.bfloat16),) * 2,
        grid_spec=pltpu.PrefetchScalarGridSpec(
            num_scalar_prefetch=1,
            grid=(1,),
            in_specs=[front, front, flat] * 2,
            out_specs=[pl.BlockSpec(shape, lambda i, *_: (0, 0, 0))] * 2,
        ),
        compiler_params=pltpu.CompilerParams(vmem_limit_bytes=16 << 20),
        name="projection_merge",
    )(scalars, kept_a, got_a, last_a, kept_b, got_b, last_b)


def finish(scalars, blocks):
    _, rows, width = blocks.shape
    return pl.pallas_call(
        finish_kernel,
        out_shape=jax.ShapeDtypeStruct((rows, width), jnp.float32),
        grid_spec=pltpu.PrefetchScalarGridSpec(
            num_scalar_prefetch=1,
            grid=(1,),
            in_specs=[pl.BlockSpec(blocks.shape, lambda i, *_: (0, 0, 0))],
            out_specs=pl.BlockSpec((rows, width), lambda i, *_: (0, 0)),
        ),
        compiler_params=pltpu.CompilerParams(vmem_limit_bytes=16 << 20),
        name="projection_finish",
    )(scalars, blocks)


def split_kernel(
    scalars, q_own, q_other, k_own, k_other, v_own, v_other,
    q_mine, sent, kv_mine,
):
    width = q_other.shape[2]
    q_mine[...] = q_own[...]
    sent[:, :, :width] = q_other[...]
    sent[:, :, width : width + HEAD_SIZE] = k_other[...]
    sent[:, :, width + HEAD_SIZE :] = v_other[...]
    kv_mine[:, :, :HEAD_SIZE] = k_own[...]
    kv_mine[:, :, HEAD_SIZE:] = v_own[...]


def split_heads(scalars, query, keys, values):
    seqs, rows, width = query.shape
    out = jax.ShapeDtypeStruct((seqs, rows, width // 2), jnp.bfloat16)
    whole = jax.ShapeDtypeStruct(query.shape, jnp.bfloat16)
    outs = (out, whole, out)

    def half(a):
        shape = a.shape[:2] + (a.shape[2] // 2,)
        return [
            pl.BlockSpec(shape, lambda i, scalars: (0, 0, scalars[0])),
            pl.BlockSpec(shape, lambda i, scalars: (0, 0, 1 - scalars[0])),
        ]

    return pl.pallas_call(
        split_kernel,
        out_shape=outs,
        grid_spec=pltpu.PrefetchScalarGridSpec(
            num_scalar_prefetch=1,
            grid=(1,),
            in_specs=half(query) + half(keys) + half(values),
            out_specs=[pl.BlockSpec(o.shape, lambda i, *_: (0, 0, 0)) for o in outs],
        ),
        compiler_params=pltpu.CompilerParams(vmem_limit_bytes=16 << 20),
        name="split_heads",
    )(scalars, query, query, keys, keys, values, values)


def by_seq(shape):
    return pl.BlockSpec((1,) + shape[1:], lambda s, *_: (s,) + (0,) * (len(shape) - 1))


def forward(scalars, mine, recv, kvs, doc_mine, doc_recv):
    seqs, rows, width = mine.shape
    keys = 2 * rows * len(kvs)
    outs = (
        jax.ShapeDtypeStruct((seqs, 2 * rows, width), jnp.bfloat16),
        jax.ShapeDtypeStruct((seqs, 2, keys, 2 * rows), jnp.bfloat16),
    )
    query_spec = by_seq(mine.shape)
    recv_spec = pl.BlockSpec((1, rows, width), lambda s, *_: (s, 0, 0))
    return pl.pallas_call(
        forward_kernel,
        out_shape=outs,
        grid_spec=pltpu.PrefetchScalarGridSpec(
            num_scalar_prefetch=1,
            grid=(seqs,),
            in_specs=[query_spec, recv_spec]
            + [by_seq(kv.shape) for kv in kvs]
            + [by_seq(doc_mine.shape), by_seq(doc_recv.shape)],
            out_specs=[by_seq(o.shape) for o in outs],
        ),
        compiler_params=pltpu.CompilerParams(vmem_limit_bytes=20 << 20),
        cost_estimate=pl.CostEstimate(
            flops=4 * seqs * 2 * 2 * rows * keys * HEAD_SIZE,
            transcendentals=seqs * 2 * 2 * rows * keys,
            bytes_accessed=8 << 20,
        ),
        name="attention_forward",
    )(scalars, mine, recv, *kvs, doc_mine, doc_recv)


def early_projection(scalars, pieces, o_weight):
    rows = sum(p.shape[0] * p.shape[1] for p in pieces)
    features, both = o_weight.shape
    width = both // 2
    steps = 7
    block = features // steps
    outs = (
        jax.ShapeDtypeStruct((rows, width), jnp.bfloat16),
        jax.ShapeDtypeStruct((features, rows), jnp.bfloat16),
    )
    return pl.pallas_call(
        early_kernel,
        out_shape=outs,
        grid_spec=pltpu.PrefetchScalarGridSpec(
            num_scalar_prefetch=1,
            grid=(steps,),
            in_specs=[pl.BlockSpec(p.shape[:2] + (block,), lambda i, *_: (0, 0, i)) for p in pieces]
            + [pl.BlockSpec((block, width), lambda i, scalars: (i, scalars[0]))],
            out_specs=[
                pl.BlockSpec((rows, width), lambda i, *_: (0, 0)),
                pl.BlockSpec((block, rows), lambda i, *_: (i, 0)),
            ],
            scratch_shapes=[pltpu.VMEM((rows, width), jnp.float32)],
        ),
        compiler_params=pltpu.CompilerParams(vmem_limit_bytes=16 << 20),
        cost_estimate=pl.CostEstimate(
            flops=20 * rows * features * width, transcendentals=0, bytes_accessed=12 << 20
        ),
        name="projection_early",
    )(scalars, *pieces, o_weight)


def late_projection(scalars, pieces, rows_t, attn, early, o_weight):
    width = attn.shape[-1]
    features = o_weight.shape[0]
    late_rows = sum(p.shape[0] * p.shape[1] for p in pieces)
    steps = 2
    block = features // steps
    out_rows = features // (CHIPS_Y * CHIPS_Z)
    slab = jax.ShapeDtypeStruct((2, CHIPS_Z // 2, out_rows, width), jnp.bfloat16)

    def whole(a):
        return pl.BlockSpec(a.shape, lambda i, *_: (0,) * len(a.shape))

    return pl.pallas_call(
        late_kernel,
        out_shape=(jax.ShapeDtypeStruct(attn.shape, jnp.bfloat16),) + (slab,) * 4,
        grid_spec=pltpu.PrefetchScalarGridSpec(
            num_scalar_prefetch=1,
            grid=(steps,),
            in_specs=[pl.BlockSpec(p.shape[:2] + (block,), lambda i, *_: (0, 0, i)) for p in pieces]
            + [pl.BlockSpec((block, r.shape[1]), lambda i, *_: (i, 0)) for r in rows_t]
            + [whole(attn)]
            + [whole(e) for e in early]
            + [pl.BlockSpec((block, width), lambda i, scalars: (i, scalars[0]))],
            out_specs=[whole(attn)] + [whole(slab)] * 4,
            scratch_shapes=[pltpu.VMEM((late_rows, width), jnp.float32)]
            + [pltpu.VMEM((r.shape[1], width), jnp.bfloat16) for r in rows_t]
            + [
                pltpu.VMEM((late_rows, width), jnp.bfloat16),
                pltpu.VMEM((block, width), jnp.float32),
            ],
        ),
        compiler_params=pltpu.CompilerParams(vmem_limit_bytes=32 << 20),
        cost_estimate=pl.CostEstimate(
            flops=2 * 6 * late_rows * features * width, transcendentals=0, bytes_accessed=12 << 20
        ),
        name="projection_late",
    )(scalars, *pieces, *rows_t, attn, *early, o_weight)


def backward(mine, recv, kvs, weights, attn, d_attn):
    seqs, rows, width = mine.shape
    half = jax.ShapeDtypeStruct((seqs, rows, width), jnp.bfloat16)
    shape = kvs[0].shape
    own = jax.ShapeDtypeStruct(shape, jnp.float32)
    sent = jax.ShapeDtypeStruct(shape, jnp.bfloat16)
    outs = (half, half, own) + (sent,) * (len(kvs) - 1)
    query_spec = by_seq(mine.shape)
    recv_spec = pl.BlockSpec((1, rows, width), lambda s, *_: (s, 0, 0))
    return pl.pallas_call(
        backward_kernel,
        out_shape=outs,
        grid=(seqs,),
        in_specs=[query_spec, recv_spec]
        + [by_seq(a.shape) for a in (*kvs, weights, attn, d_attn)],
        out_specs=[by_seq(o.shape) for o in outs],
        compiler_params=pltpu.CompilerParams(vmem_limit_bytes=20 << 20),
        cost_estimate=pl.CostEstimate(
            flops=10 * seqs * 2 * 2 * rows * 10 * rows * HEAD_SIZE,
            transcendentals=0,
            bytes_accessed=8 << 20,
        ),
        name="attention_backward",
    )(mine, recv, *kvs, weights, attn, d_attn)


def local(query, key_states, value_state_rows, d_out, o_weight, doc_start):
    seq_count, shard_rows, query_width = query.shape
    ctx = lax.axis_index("ctx")
    tp = lax.axis_index("tp")
    core = ctx % CORES
    y = ctx // CORES % CHIPS_Y
    chip_pos = ctx // CORES * (CORES * shard_rows)
    scalars = jnp.stack([core, tp, y, chip_pos]).astype(jnp.int32)
    first = core == 0
    q_mine, sent, kv_mine = split_heads(scalars, query, key_states, value_state_rows)

    r3 = tp_ahead(d_out, 1)
    r1 = tp_ahead(d_out, -1)
    recv = to_sibling(sent)
    doc_mine = doc_start[:, None, :]
    doc_recv = to_sibling(doc_mine)
    t0 = to_sibling(d_out)
    recv, doc_recv, t0, scalars, first, one_row, two_rows = lax.optimization_barrier(
        (recv, doc_recv, t0, scalars, first, y < 1, y < 2)
    )
    kv0 = jnp.concatenate([kv_mine, recv[..., -2 * HEAD_SIZE :]], axis=1)
    kv4, kv1 = (chips_ahead(kv0, d) for d in (4, 1))
    own, own_t = early_projection(scalars, [d_out, t0], o_weight)

    kv_two = jnp.where(two_rows, kv0, kv4)
    kv_three = jnp.where(one_row, kv0, kv4)
    r1, r3, own, kv1, kv_two, kv_three = lax.optimization_barrier(
        (r1, r3, own, kv1, kv_two, kv_three)
    )
    kv2, kv3 = y_ahead(kv_two, 2), y_ahead(kv_three, 3)
    r2a = tp_ahead(r3[:1], 1)
    r2b = tp_ahead(r1[1:], -1)
    near, near_t = early_projection(
        scalars, [r1, r3, to_sibling(r1), to_sibling(r3)], o_weight
    )
    near, r2a, r2b, kv2, kv3 = lax.optimization_barrier((near, r2a, r2b, kv2, kv3))
    kvs = [kv0, kv1, kv2, kv3, kv4]
    attn, weights = forward(scalars, q_mine, recv, kvs, doc_mine, doc_recv)
    d_attn, sent_a, kept_a, sent_b, kept_b = late_projection(
        scalars,
        [r2a, r2b, to_sibling(r2a), to_sibling(r2b)],
        [own_t, near_t],
        attn,
        [own, near],
        o_weight,
    )
    got_a = y_route(sent_a, y_pair)
    got_b = y_route(sent_b, y_mirror)
    dq_mine, dq_other, g_own, *g_sent = backward(
        q_mine, recv, kvs, weights, attn, d_attn
    )
    *g_near, g_far = (chips_ahead(g, -d) for d, g in enumerate(g_sent, 1))
    got_a, got_b, g_own, *g_near = lax.optimization_barrier((got_a, got_b, g_own, *g_near))
    dq_recv = to_sibling(dq_other)

    def added(*blocks):
        total = blocks[0].astype(jnp.float32)
        for block in blocks[1:]:
            total = total + block.astype(jnp.float32)
        return total

    next_a = added(kept_a[1], got_a[1]).astype(jnp.bfloat16)
    next_b = added(kept_b[1], got_b[1]).astype(jnp.bfloat16)
    last_a = y_route(next_a, y_mirror)
    last_b = y_route(next_b, y_pair)
    last_a, last_b, g_far = lax.optimization_barrier((last_a, last_b, g_far))
    w_own, w_other = merge(scalars, kept_a, got_a, last_a, kept_b, got_b, last_b)
    w_all = z_exchange(jnp.concatenate([w_own, to_sibling(w_other)], axis=-1))

    grads = added(g_own, *g_near, g_far).astype(jnp.bfloat16)
    g_mine = grads[:, :shard_rows]
    g_recv = to_sibling(grads[:, shard_rows:])

    def by_core(own, other):
        return jnp.concatenate(
            [jnp.where(first, own, other), jnp.where(first, other, own)], axis=-1
        )

    return (
        by_core(dq_mine, dq_recv),
        by_core(g_mine[..., :HEAD_SIZE], g_recv[..., :HEAD_SIZE]),
        by_core(g_mine[..., HEAD_SIZE:], g_recv[..., HEAD_SIZE:]),
        finish(scalars, w_all),
    )


def solution(mesh):
    return jax.shard_map(
        local,
        mesh=mesh,
        in_specs=(
            P(None, "ctx", "tp"),
            P(None, "ctx", "tp"),
            P(None, "ctx", "tp"),
            P(None, ("ctx", "tp"), None),
            P(None, "tp"),
            P(None, "ctx"),
        ),
        out_specs=(
            P(None, "ctx", "tp"),
            P(None, "ctx", "tp"),
            P(None, "ctx", "tp"),
            P("ctx", "tp"),
        ),
        check_vma=False,
    )
```

```python
import jax
import jax.numpy as jnp
from jax import lax
from jax.experimental import pallas as pl
from jax.experimental.pallas import tpu as pltpu
from jax.sharding import PartitionSpec as P

HEAD_SIZE = 128
WIN = 1024
CORES = 2
CHIPS_Y = 4
CHIPS_Z = 8
TP = 4
LOG2_E = 1.4426950408889634

score_scale = 168.0 ** (-0.5)

NT = (((1,), (1,)), ((), ()))
TN = (((0,), (0,)), ((), ()))
NN = (((1,), (0,)), ((), ()))


def dot(a, b, dims=NN):
    return lax.dot_general(a, b, dims, preferred_element_type=jnp.float32)


def ctx_shift(block, move):
    count = CORES * CHIPS_Y * CHIPS_Z
    return lax.ppermute(block, "ctx", [(i, move(i)) for i in range(count)])


def to_sibling(block):
    return ctx_shift(block, lambda i: i ^ 1)


def y_pair(y):
    return y ^ 1


def y_mirror(y):
    return CHIPS_Y - 1 - y


def y_route(block, target):
    def move(i):
        core, y, z = i % CORES, i // CORES % CHIPS_Y, i // (CORES * CHIPS_Y)
        return (z * CHIPS_Y + target(y)) * CORES + core

    return ctx_shift(block, move)


def z_exchange(blocks):
    groups = [
        [(z * CHIPS_Y + y) * CORES + core for z in range(CHIPS_Z) for core in range(CORES)]
        for y in range(CHIPS_Y)
    ]
    return lax.all_to_all(blocks, "ctx", 0, 0, axis_index_groups=groups, tiled=True)


def chips_ahead(block, distance):
    count = CORES * CHIPS_Y * CHIPS_Z
    return ctx_shift(block, lambda i: (i + CORES * distance) % count)


def y_ahead(block, distance):
    return y_route(block, lambda y: (y + distance) % CHIPS_Y)


def tp_ahead(block, distance):
    return lax.ppermute(block, "tp", [(i, (i + distance) % TP) for i in range(TP)])


def query_positions(core, chip_pos, rows):
    lane = lax.broadcasted_iota(jnp.int32, (1, 2 * rows), 1)
    other = lane >= rows
    first = jnp.where(other, (1 - core) * rows - rows, core * rows)
    return chip_pos + first + lane


def forward_kernel(
    scalars, mine, recv, kv0, kv1, kv2, kv3, kv4, doc_mine, doc_recv, attn, weights
):
    core, chip_pos = scalars[0], scalars[3]
    kvs = [kv[0] for kv in (kv0, kv1, kv2, kv3, kv4)]
    rows = mine.shape[1]
    query_pos = query_positions(core, chip_pos, rows)
    doc = jnp.concatenate([doc_mine[0], doc_recv[0]], axis=1)
    lowest = jnp.maximum(doc, query_pos - (WIN - 1))
    index = lax.broadcasted_iota(jnp.int32, (2 * rows, 2 * rows), 0)
    offset = index + jnp.where(index >= rows, (1 - core) * rows - rows, core * rows)
    for h in range(2):
        cols = slice(h * HEAD_SIZE, (h + 1) * HEAD_SIZE)
        q = jnp.concatenate([mine[0, :, cols], recv[0, :, cols]], axis=0)
        scores = []
        for d, kv in enumerate(kvs):
            s = dot(kv[:, :HEAD_SIZE], q, NT) * (score_scale * LOG2_E)
            key_pos = offset + (chip_pos - 2 * rows * d)
            visible = key_pos >= lowest
            if d == 0:
                visible = visible & (key_pos <= query_pos)
            scores.append(jnp.where(visible, s, -1e30))
        top = scores[0]
        for s in scores[1:]:
            top = jnp.maximum(top, s)
        top = jnp.max(top, axis=0, keepdims=True)
        expo = [jnp.exp2(s - top) for s in scores]
        total = expo[0]
        for e in expo[1:]:
            total = total + e
        inverse = 1.0 / jnp.sum(total, axis=0, keepdims=True)
        acc = None
        for d, kv in enumerate(kvs):
            w = (expo[d] * inverse).astype(jnp.bfloat16)
            weights[0, h, 2 * rows * d : 2 * rows * (d + 1), :] = w
            part = dot(kv[:, HEAD_SIZE:], w, TN)
            acc = part if acc is None else acc + part
        attn[0, :, cols] = acc.T.astype(jnp.bfloat16)


def early_kernel(scalars, *refs):
    *pieces, o_weight, d_attn, rows_t, acc = refs
    step = pl.program_id(0)
    parts = [ref[seq] for ref in pieces for seq in range(ref.shape[0])]
    rows = jnp.concatenate(parts, axis=0)
    product = dot(rows, o_weight[...])

    @pl.when(step == 0)
    def _():
        acc[...] = product

    @pl.when(step > 0)
    def _():
        acc[...] = acc[...] + product

    rows_t[...] = rows.T

    @pl.when(step == pl.num_programs(0) - 1)
    def _():
        d_attn[...] = acc[...].astype(jnp.bfloat16)


def place(tp, piece, core_block, rel, seq):
    here = TP * piece * core_block + piece * ((tp + rel) % TP)
    return seq, pl.ds(pl.multiple_of(here, piece), piece)


OWN_SLOTS = [(b, 0, q) for b in range(2) for q in range(2)]
NEAR_SLOTS = [(b, s, q) for b in range(2) for s in (1, 3) for q in range(2)]
FAR_SLOTS = [(b, 2, q) for b in range(2) for q in range(2)]


def late_kernel(
    scalars, r2a, r2b, t2a, t2b, own_t, near_t, attn, own, near, o_weight,
    d_attn, sent_a, kept_a, sent_b, kept_b, acc, attn_own, attn_near, attn_far, partial,
):
    step = pl.program_id(0)
    tp, y = scalars[1], scalars[2]
    piece = r2a.shape[1]
    out_rows = sent_a.shape[2]

    @pl.when(step == 0)
    def _():
        for slots, kept in ((OWN_SLOTS, attn_own), (NEAR_SLOTS, attn_near), (FAR_SLOTS, attn_far)):
            for n, slot in enumerate(slots):
                seq, here = place(tp, piece, *slot)
                kept[n * piece : (n + 1) * piece, :] = attn[seq, here, :]
        for slots, done in ((OWN_SLOTS, own), (NEAR_SLOTS, near)):
            for n, slot in enumerate(slots):
                seq, here = place(tp, piece, *slot)
                d_attn[seq, here, :] = done[n * piece : (n + 1) * piece, :]

    rows = jnp.concatenate([r2a[0], r2b[0], t2a[0], t2b[0]], axis=0)
    partial[...] = (
        dot(own_t[...], attn_own[...])
        + dot(near_t[...], attn_near[...])
        + dot(rows.T, attn_far[...])
    )

    def emit(out, order):
        for n, target in enumerate(order):
            for z in range(out.shape[1]):
                start = pl.multiple_of((CHIPS_Y * z + target) * out_rows, 8)
                out[n, z] = partial[pl.ds(start, out_rows), :].astype(jnp.bfloat16)

    pair = y + 1 - 2 * (y % 2)
    mirror = CHIPS_Y - 1 - y
    mirror_pair = mirror + 1 - 2 * (mirror % 2)

    product = dot(rows, o_weight[...])

    @pl.when(step == 0)
    def _():
        emit(sent_a, (pair, CHIPS_Y - 1 - pair))
        emit(kept_a, (y, mirror))
        acc[...] = product

    @pl.when(step == 1)
    def _():
        emit(sent_b, (mirror, mirror_pair))
        emit(kept_b, (y, pair))
        total = (acc[...] + product).astype(jnp.bfloat16)
        for n, slot in enumerate(FAR_SLOTS):
            seq, here = place(tp, piece, *slot)
            d_attn[seq, here, :] = total[n * piece : (n + 1) * piece, :]


def backward_kernel(
    mine, recv, kv0, kv1, kv2, kv3, kv4, weights, attn, d_attn,
    dq_mine, dq_other, g_own, g1, g2, g3, g4,
):
    rows = mine.shape[1]
    kvs = [kv[0] for kv in (kv0, kv1, kv2, kv3, kv4)]
    heads = []
    for h in range(2):
        cols = slice(h * HEAD_SIZE, (h + 1) * HEAD_SIZE)
        q = jnp.concatenate([mine[0, :, cols], recv[0, :, cols]], axis=0)
        da = d_attn[0, :, cols]
        product = da.astype(jnp.float32) * attn[0, :, cols].astype(jnp.float32)
        delta = jnp.sum(product.T, axis=0, keepdims=True)
        heads.append((q, da, delta))
    dq = [None, None]
    grads = (g_own, g1, g2, g3, g4)
    for kv_index, (kv, grad) in enumerate(zip(kvs, grads)):
        keys = kv[:, :HEAD_SIZE]
        values = kv[:, HEAD_SIZE:]
        dk = dv = None
        for h, (q, da, delta) in enumerate(heads):
            w = weights[0, h, 2 * rows * kv_index : 2 * rows * (kv_index + 1), :]
            dp = dot(values, da, NT)
            ds = (w.astype(jnp.float32) * (dp - delta)).astype(jnp.bfloat16)
            v_part = dot(w, da)
            k_part = dot(ds, q)
            q_part = dot(keys, ds, TN)
            dv = v_part if dv is None else dv + v_part
            dk = k_part if dk is None else dk + k_part
            dq[h] = q_part if dq[h] is None else dq[h] + q_part
        grad[0, :, :HEAD_SIZE] = (dk * score_scale).astype(grad.dtype)
        grad[0, :, HEAD_SIZE:] = dv.astype(grad.dtype)
    for h in range(2):
        cols = slice(h * HEAD_SIZE, (h + 1) * HEAD_SIZE)
        full = (dq[h].T * score_scale).astype(jnp.bfloat16)
        dq_mine[0, :, cols] = full[:rows]
        dq_other[0, :, cols] = full[rows:]


def merge_kernel(kept_a, got_a, last_a, kept_b, got_b, last_b, out):
    half = kept_a.shape[1]
    rows = out.shape[1]
    for part, (kept, got, last) in enumerate(((kept_a, got_a, last_a), (kept_b, got_b, last_b))):
        for z in range(half):
            total = (
                kept[0, z].astype(jnp.float32)
                + got[0, z].astype(jnp.float32)
                + last[z].astype(jnp.float32)
            )
            for core in range(CORES):
                slot = CORES * (half * part + z) + core
                out[slot] = total[core * rows : (core + 1) * rows].astype(jnp.bfloat16)


def finish_kernel(blocks, out):
    width = blocks.shape[2]
    for core in range(CORES):
        total = blocks[core].astype(jnp.float32)
        for z in range(1, CHIPS_Z):
            total = total + blocks[CORES * z + core].astype(jnp.float32)
        out[:, core * width : (core + 1) * width] = total


def merge(kept_a, got_a, last_a, kept_b, got_b, last_b):
    _, half, rows, width = kept_a.shape
    front = pl.BlockSpec((1, half, rows, width), lambda i: (0, 0, 0, 0))
    flat = pl.BlockSpec((half, rows, width), lambda i: (0, 0, 0))
    shape = (CORES * 2 * half, rows // CORES, width)
    return pl.pallas_call(
        merge_kernel,
        out_shape=jax.ShapeDtypeStruct(shape, jnp.bfloat16),
        grid=(1,),
        in_specs=[front, front, flat] * 2,
        out_specs=pl.BlockSpec(shape, lambda i: (0, 0, 0)),
        compiler_params=pltpu.CompilerParams(vmem_limit_bytes=16 << 20),
        name="projection_merge",
    )(kept_a, got_a, last_a, kept_b, got_b, last_b)


def finish(blocks):
    count, rows, width = blocks.shape
    return pl.pallas_call(
        finish_kernel,
        out_shape=jax.ShapeDtypeStruct((rows, CORES * width), jnp.float32),
        compiler_params=pltpu.CompilerParams(vmem_limit_bytes=16 << 20),
        name="projection_finish",
    )(blocks)


def split_kernel(
    scalars, q_own, q_other, k_own, k_other, v_own, v_other,
    q_mine, sent, kv_mine,
):
    width = q_other.shape[2]
    q_mine[...] = q_own[...]
    sent[:, :, :width] = q_other[...]
    sent[:, :, width : width + HEAD_SIZE] = k_other[...]
    sent[:, :, width + HEAD_SIZE :] = v_other[...]
    kv_mine[:, :, :HEAD_SIZE] = k_own[...]
    kv_mine[:, :, HEAD_SIZE:] = v_own[...]


def split_heads(scalars, query, keys, values):
    seqs, rows, width = query.shape
    out = jax.ShapeDtypeStruct((seqs, rows, width // 2), jnp.bfloat16)
    whole = jax.ShapeDtypeStruct(query.shape, jnp.bfloat16)
    outs = (out, whole, out)

    def half(a):
        shape = a.shape[:2] + (a.shape[2] // 2,)
        return [
            pl.BlockSpec(shape, lambda i, scalars: (0, 0, scalars[0])),
            pl.BlockSpec(shape, lambda i, scalars: (0, 0, 1 - scalars[0])),
        ]

    return pl.pallas_call(
        split_kernel,
        out_shape=outs,
        grid_spec=pltpu.PrefetchScalarGridSpec(
            num_scalar_prefetch=1,
            grid=(1,),
            in_specs=half(query) + half(keys) + half(values),
            out_specs=[pl.BlockSpec(o.shape, lambda i, *_: (0, 0, 0)) for o in outs],
        ),
        compiler_params=pltpu.CompilerParams(vmem_limit_bytes=16 << 20),
        name="split_heads",
    )(scalars, query, query, keys, keys, values, values)


def by_seq(shape):
    return pl.BlockSpec((1,) + shape[1:], lambda s, *_: (s,) + (0,) * (len(shape) - 1))


def forward(scalars, mine, recv, kvs, doc_mine, doc_recv):
    seqs, rows, width = mine.shape
    keys = 2 * rows * len(kvs)
    outs = (
        jax.ShapeDtypeStruct((seqs, 2 * rows, width), jnp.bfloat16),
        jax.ShapeDtypeStruct((seqs, 2, keys, 2 * rows), jnp.bfloat16),
    )
    query_spec = by_seq(mine.shape)
    recv_spec = pl.BlockSpec((1, rows, width), lambda s, *_: (s, 0, 0))
    return pl.pallas_call(
        forward_kernel,
        out_shape=outs,
        grid_spec=pltpu.PrefetchScalarGridSpec(
            num_scalar_prefetch=1,
            grid=(seqs,),
            in_specs=[query_spec, recv_spec]
            + [by_seq(kv.shape) for kv in kvs]
            + [by_seq(doc_mine.shape), by_seq(doc_recv.shape)],
            out_specs=[by_seq(o.shape) for o in outs],
        ),
        compiler_params=pltpu.CompilerParams(vmem_limit_bytes=20 << 20),
        cost_estimate=pl.CostEstimate(
            flops=4 * seqs * 2 * 2 * rows * keys * HEAD_SIZE,
            transcendentals=seqs * 2 * 2 * rows * keys,
            bytes_accessed=8 << 20,
        ),
        name="attention_forward",
    )(scalars, mine, recv, *kvs, doc_mine, doc_recv)


def early_projection(scalars, pieces, o_weight):
    rows = sum(p.shape[0] * p.shape[1] for p in pieces)
    features, both = o_weight.shape
    width = both // 2
    steps = 7
    block = features // steps
    outs = (
        jax.ShapeDtypeStruct((rows, width), jnp.bfloat16),
        jax.ShapeDtypeStruct((features, rows), jnp.bfloat16),
    )
    return pl.pallas_call(
        early_kernel,
        out_shape=outs,
        grid_spec=pltpu.PrefetchScalarGridSpec(
            num_scalar_prefetch=1,
            grid=(steps,),
            in_specs=[pl.BlockSpec(p.shape[:2] + (block,), lambda i, *_: (0, 0, i)) for p in pieces]
            + [pl.BlockSpec((block, width), lambda i, scalars: (i, scalars[0]))],
            out_specs=[
                pl.BlockSpec((rows, width), lambda i, *_: (0, 0)),
                pl.BlockSpec((block, rows), lambda i, *_: (i, 0)),
            ],
            scratch_shapes=[pltpu.VMEM((rows, width), jnp.float32)],
        ),
        compiler_params=pltpu.CompilerParams(vmem_limit_bytes=16 << 20),
        cost_estimate=pl.CostEstimate(
            flops=20 * rows * features * width, transcendentals=0, bytes_accessed=12 << 20
        ),
        name="projection_early",
    )(scalars, *pieces, o_weight)


def late_projection(scalars, pieces, rows_t, attn, early, o_weight):
    width = attn.shape[-1]
    features = o_weight.shape[0]
    late_rows = sum(p.shape[0] * p.shape[1] for p in pieces)
    steps = 2
    block = features // steps
    out_rows = features // (CHIPS_Y * CHIPS_Z)
    slab = jax.ShapeDtypeStruct((2, CHIPS_Z // 2, out_rows, width), jnp.bfloat16)

    def whole(a):
        return pl.BlockSpec(a.shape, lambda i, *_: (0,) * len(a.shape))

    return pl.pallas_call(
        late_kernel,
        out_shape=(jax.ShapeDtypeStruct(attn.shape, jnp.bfloat16),) + (slab,) * 4,
        grid_spec=pltpu.PrefetchScalarGridSpec(
            num_scalar_prefetch=1,
            grid=(steps,),
            in_specs=[pl.BlockSpec(p.shape[:2] + (block,), lambda i, *_: (0, 0, i)) for p in pieces]
            + [pl.BlockSpec((block, r.shape[1]), lambda i, *_: (i, 0)) for r in rows_t]
            + [whole(attn)]
            + [whole(e) for e in early]
            + [pl.BlockSpec((block, width), lambda i, scalars: (i, scalars[0]))],
            out_specs=[whole(attn)] + [whole(slab)] * 4,
            scratch_shapes=[pltpu.VMEM((late_rows, width), jnp.float32)]
            + [pltpu.VMEM((r.shape[1], width), jnp.bfloat16) for r in rows_t]
            + [
                pltpu.VMEM((late_rows, width), jnp.bfloat16),
                pltpu.VMEM((block, width), jnp.float32),
            ],
        ),
        compiler_params=pltpu.CompilerParams(vmem_limit_bytes=32 << 20),
        cost_estimate=pl.CostEstimate(
            flops=2 * 6 * late_rows * features * width, transcendentals=0, bytes_accessed=12 << 20
        ),
        name="projection_late",
    )(scalars, *pieces, *rows_t, attn, *early, o_weight)


def backward(mine, recv, kvs, weights, attn, d_attn):
    seqs, rows, width = mine.shape
    half = jax.ShapeDtypeStruct((seqs, rows, width), jnp.bfloat16)
    shape = kvs[0].shape
    own = jax.ShapeDtypeStruct(shape, jnp.float32)
    sent = jax.ShapeDtypeStruct(shape, jnp.bfloat16)
    outs = (half, half, own) + (sent,) * (len(kvs) - 1)
    query_spec = by_seq(mine.shape)
    recv_spec = pl.BlockSpec((1, rows, width), lambda s, *_: (s, 0, 0))
    return pl.pallas_call(
        backward_kernel,
        out_shape=outs,
        grid=(seqs,),
        in_specs=[query_spec, recv_spec]
        + [by_seq(a.shape) for a in (*kvs, weights, attn, d_attn)],
        out_specs=[by_seq(o.shape) for o in outs],
        compiler_params=pltpu.CompilerParams(vmem_limit_bytes=20 << 20),
        cost_estimate=pl.CostEstimate(
            flops=10 * seqs * 2 * 2 * rows * 10 * rows * HEAD_SIZE,
            transcendentals=0,
            bytes_accessed=8 << 20,
        ),
        name="attention_backward",
    )(mine, recv, *kvs, weights, attn, d_attn)


def local(query, key_states, value_state_rows, d_out, o_weight, doc_start):
    seq_count, shard_rows, query_width = query.shape
    ctx = lax.axis_index("ctx")
    tp = lax.axis_index("tp")
    core = ctx % CORES
    y = ctx // CORES % CHIPS_Y
    chip_pos = ctx // CORES * (CORES * shard_rows)
    scalars = jnp.stack([core, tp, y, chip_pos]).astype(jnp.int32)
    first = core == 0
    q_mine, sent, kv_mine = split_heads(scalars, query, key_states, value_state_rows)

    r3 = tp_ahead(d_out, 1)
    r1 = tp_ahead(d_out, -1)
    recv = to_sibling(sent)
    doc_mine = doc_start[:, None, :]
    doc_recv = to_sibling(doc_mine)
    t0 = to_sibling(d_out)
    recv, doc_recv, t0, scalars, first, one_row = lax.optimization_barrier(
        (recv, doc_recv, t0, scalars, first, y < 1)
    )
    kv0 = jnp.concatenate([kv_mine, recv[..., -2 * HEAD_SIZE :]], axis=1)
    kv4, kv2, kv1 = (chips_ahead(kv0, d) for d in (4, 2, 1))
    own, own_t = early_projection(scalars, [d_out, t0], o_weight)

    kv_three = jnp.where(one_row, kv0, kv4)
    r1, r3, own, kv1, kv2, kv_three = lax.optimization_barrier(
        (r1, r3, own, kv1, kv2, kv_three)
    )
    kv3 = y_ahead(kv_three, 3)
    r2a = tp_ahead(r3[:1], 1)
    r2b = tp_ahead(r1[1:], -1)
    near, near_t = early_projection(
        scalars, [r1, r3, to_sibling(r1), to_sibling(r3)], o_weight
    )
    near, r2a, r2b, kv3 = lax.optimization_barrier((near, r2a, r2b, kv3))
    kvs = [kv0, kv1, kv2, kv3, kv4]
    attn, weights = forward(scalars, q_mine, recv, kvs, doc_mine, doc_recv)
    d_attn, sent_a, kept_a, sent_b, kept_b = late_projection(
        scalars,
        [r2a, r2b, to_sibling(r2a), to_sibling(r2b)],
        [own_t, near_t],
        attn,
        [own, near],
        o_weight,
    )
    got_a = y_route(sent_a, y_pair)
    got_b = y_route(sent_b, y_mirror)
    dq_mine, dq_other, g_own, *g_sent = backward(
        q_mine, recv, kvs, weights, attn, d_attn
    )
    *g_near, g_far = (chips_ahead(g, -d) for d, g in enumerate(g_sent, 1))
    got_a, got_b, g_own, *g_near = lax.optimization_barrier((got_a, got_b, g_own, *g_near))
    dq_recv = to_sibling(dq_other)

    def added(*blocks):
        total = blocks[0].astype(jnp.float32)
        for block in blocks[1:]:
            total = total + block.astype(jnp.float32)
        return total

    next_a = added(kept_a[1], got_a[1]).astype(jnp.bfloat16)
    next_b = added(kept_b[1], got_b[1]).astype(jnp.bfloat16)
    last_a = y_route(next_a, y_mirror)
    last_b = y_route(next_b, y_pair)
    last_a, last_b, g_far = lax.optimization_barrier((last_a, last_b, g_far))
    w_sum = merge(kept_a, got_a, last_a, kept_b, got_b, last_b)
    w_all = z_exchange(w_sum)

    grads = added(g_own, *g_near, g_far).astype(jnp.bfloat16)
    g_mine = grads[:, :shard_rows]
    g_recv = to_sibling(grads[:, shard_rows:])

    def by_core(own, other):
        return jnp.concatenate(
            [jnp.where(first, own, other), jnp.where(first, other, own)], axis=-1
        )

    return (
        by_core(dq_mine, dq_recv),
        by_core(g_mine[..., :HEAD_SIZE], g_recv[..., :HEAD_SIZE]),
        by_core(g_mine[..., HEAD_SIZE:], g_recv[..., HEAD_SIZE:]),
        finish(w_all),
    )


def solution(mesh):
    return jax.shard_map(
        local,
        mesh=mesh,
        in_specs=(
            P(None, "ctx", "tp"),
            P(None, "ctx", "tp"),
            P(None, "ctx", "tp"),
            P(None, ("ctx", "tp"), None),
            P(None, "tp"),
            P(None, "ctx"),
        ),
        out_specs=(
            P(None, "ctx", "tp"),
            P(None, "ctx", "tp"),
            P(None, "ctx", "tp"),
            P("ctx", "tp"),
        ),
        check_vma=False,
    )
```

```python
import jax
import jax.numpy as jnp
from jax import lax
from jax.experimental import pallas as pl
from jax.experimental.pallas import tpu as pltpu
from jax.sharding import PartitionSpec as P

HEAD_SIZE = 128
WIN = 1024
CORES = 2
CHIPS_Y = 4
CHIPS_Z = 8
TP = 4
LOG2_E = 1.4426950408889634

score_scale = 168.0 ** (-0.5)

NT = (((1,), (1,)), ((), ()))
TN = (((0,), (0,)), ((), ()))
NN = (((1,), (0,)), ((), ()))


def dot(a, b, dims=NN):
    return lax.dot_general(a, b, dims, preferred_element_type=jnp.float32)


def ctx_shift(block, move):
    count = CORES * CHIPS_Y * CHIPS_Z
    return lax.ppermute(block, "ctx", [(i, move(i)) for i in range(count)])


def to_sibling(block):
    return ctx_shift(block, lambda i: i ^ 1)


def y_pair(y):
    return y ^ 1


def y_mirror(y):
    return CHIPS_Y - 1 - y


def y_route(block, target):
    def move(i):
        core, y, z = i % CORES, i // CORES % CHIPS_Y, i // (CORES * CHIPS_Y)
        return (z * CHIPS_Y + target(y)) * CORES + core

    return ctx_shift(block, move)


def z_exchange(blocks):
    groups = [
        [(z * CHIPS_Y + y) * CORES + core for z in range(CHIPS_Z) for core in range(CORES)]
        for y in range(CHIPS_Y)
    ]
    return lax.all_to_all(blocks, "ctx", 0, 0, axis_index_groups=groups, tiled=True)


def chips_ahead(block, distance):
    count = CORES * CHIPS_Y * CHIPS_Z
    return ctx_shift(block, lambda i: (i + CORES * distance) % count)


def y_ahead(block, distance):
    return y_route(block, lambda y: (y + distance) % CHIPS_Y)


def tp_ahead(block, distance):
    return lax.ppermute(block, "tp", [(i, (i + distance) % TP) for i in range(TP)])


def query_positions(core, chip_pos, rows):
    lane = lax.broadcasted_iota(jnp.int32, (1, 2 * rows), 1)
    other = lane >= rows
    first = jnp.where(other, (1 - core) * rows - rows, core * rows)
    return chip_pos + first + lane


def forward_kernel(
    scalars, mine, recv, kv0, kv1, kv2, kv3, kv4, doc_mine, doc_recv, attn, weights
):
    core, chip_pos = scalars[0], scalars[3]
    kvs = [kv[0] for kv in (kv0, kv1, kv2, kv3, kv4)]
    rows = mine.shape[1]
    query_pos = query_positions(core, chip_pos, rows)
    doc = jnp.concatenate([doc_mine[0], doc_recv[0]], axis=1)
    lowest = jnp.maximum(doc, query_pos - (WIN - 1))
    index = lax.broadcasted_iota(jnp.int32, (2 * rows, 2 * rows), 0)
    offset = index + jnp.where(index >= rows, (1 - core) * rows - rows, core * rows)
    for h in range(2):
        cols = slice(h * HEAD_SIZE, (h + 1) * HEAD_SIZE)
        q = jnp.concatenate([mine[0, :, cols], recv[0, :, cols]], axis=0)
        scores = []
        for d, kv in enumerate(kvs):
            s = dot(kv[:, :HEAD_SIZE], q, NT) * (score_scale * LOG2_E)
            key_pos = offset + (chip_pos - 2 * rows * d)
            visible = key_pos >= lowest
            if d == 0:
                visible = visible & (key_pos <= query_pos)
            scores.append(jnp.where(visible, s, -1e30))
        top = scores[0]
        for s in scores[1:]:
            top = jnp.maximum(top, s)
        top = jnp.max(top, axis=0, keepdims=True)
        expo = [jnp.exp2(s - top) for s in scores]
        total = expo[0]
        for e in expo[1:]:
            total = total + e
        inverse = 1.0 / jnp.sum(total, axis=0, keepdims=True)
        acc = None
        for d, kv in enumerate(kvs):
            w = (expo[d] * inverse).astype(jnp.bfloat16)
            weights[0, h, 2 * rows * d : 2 * rows * (d + 1), :] = w
            part = dot(kv[:, HEAD_SIZE:], w, TN)
            acc = part if acc is None else acc + part
        attn[0, :, cols] = acc.T.astype(jnp.bfloat16)


def early_kernel(scalars, *refs):
    *pieces, o_weight, d_attn, rows_t, acc = refs
    step = pl.program_id(0)
    parts = [ref[seq] for ref in pieces for seq in range(ref.shape[0])]
    rows = jnp.concatenate(parts, axis=0)
    product = dot(rows, o_weight[...])

    @pl.when(step == 0)
    def _():
        acc[...] = product

    @pl.when(step > 0)
    def _():
        acc[...] = acc[...] + product

    rows_t[...] = rows.T

    @pl.when(step == pl.num_programs(0) - 1)
    def _():
        d_attn[...] = acc[...].astype(jnp.bfloat16)


def place(tp, piece, core_block, rel, seq):
    here = TP * piece * core_block + piece * ((tp + rel) % TP)
    return seq, pl.ds(pl.multiple_of(here, piece), piece)


OWN_SLOTS = [(b, 0, q) for b in range(2) for q in range(2)]
NEAR_SLOTS = [(b, s, q) for b in range(2) for s in (1, 3) for q in range(2)]
FAR_SLOTS = [(b, 2, q) for b in range(2) for q in range(2)]


def late_kernel(
    scalars, r2a, r2b, t2a, t2b, own_t, near_t, attn, own, near, o_weight,
    d_attn, sent_a, kept_a, sent_b, kept_b, acc, attn_own, attn_near, attn_far, partial,
):
    step = pl.program_id(0)
    tp, y = scalars[1], scalars[2]
    piece = r2a.shape[1]
    out_rows = sent_a.shape[2]

    @pl.when(step == 0)
    def _():
        for slots, kept in ((OWN_SLOTS, attn_own), (NEAR_SLOTS, attn_near), (FAR_SLOTS, attn_far)):
            for n, slot in enumerate(slots):
                seq, here = place(tp, piece, *slot)
                kept[n * piece : (n + 1) * piece, :] = attn[seq, here, :]
        for slots, done in ((OWN_SLOTS, own), (NEAR_SLOTS, near)):
            for n, slot in enumerate(slots):
                seq, here = place(tp, piece, *slot)
                d_attn[seq, here, :] = done[n * piece : (n + 1) * piece, :]

    rows = jnp.concatenate([r2a[0], r2b[0], t2a[0], t2b[0]], axis=0)
    partial[...] = (
        dot(own_t[...], attn_own[...])
        + dot(near_t[...], attn_near[...])
        + dot(rows.T, attn_far[...])
    )

    def emit(out, order):
        for n, target in enumerate(order):
            for z in range(out.shape[1]):
                start = pl.multiple_of((CHIPS_Y * z + target) * out_rows, 8)
                out[n, z] = partial[pl.ds(start, out_rows), :].astype(jnp.bfloat16)

    pair = y + 1 - 2 * (y % 2)
    mirror = CHIPS_Y - 1 - y
    mirror_pair = mirror + 1 - 2 * (mirror % 2)

    product = dot(rows, o_weight[...])

    @pl.when(step == 0)
    def _():
        emit(sent_a, (pair, CHIPS_Y - 1 - pair))
        emit(kept_a, (y, mirror))
        acc[...] = product

    @pl.when(step == 1)
    def _():
        emit(sent_b, (mirror, mirror_pair))
        emit(kept_b, (y, pair))
        total = (acc[...] + product).astype(jnp.bfloat16)
        for n, slot in enumerate(FAR_SLOTS):
            seq, here = place(tp, piece, *slot)
            d_attn[seq, here, :] = total[n * piece : (n + 1) * piece, :]


def backward_kernel(
    mine, recv, kv0, kv1, kv2, kv3, kv4, weights, attn, d_attn,
    dq_mine, dq_other, g_own, g1, g2, g3, g4,
):
    rows = mine.shape[1]
    kvs = [kv[0] for kv in (kv0, kv1, kv2, kv3, kv4)]
    heads = []
    for h in range(2):
        cols = slice(h * HEAD_SIZE, (h + 1) * HEAD_SIZE)
        q = jnp.concatenate([mine[0, :, cols], recv[0, :, cols]], axis=0)
        da = d_attn[0, :, cols]
        product = da.astype(jnp.float32) * attn[0, :, cols].astype(jnp.float32)
        delta = jnp.sum(product.T, axis=0, keepdims=True)
        heads.append((q, da, delta))
    dq = [None, None]
    grads = (g_own, g1, g2, g3, g4)
    for kv_index, (kv, grad) in enumerate(zip(kvs, grads)):
        keys = kv[:, :HEAD_SIZE]
        values = kv[:, HEAD_SIZE:]
        dk = dv = None
        for h, (q, da, delta) in enumerate(heads):
            w = weights[0, h, 2 * rows * kv_index : 2 * rows * (kv_index + 1), :]
            dp = dot(values, da, NT)
            ds = (w.astype(jnp.float32) * (dp - delta)).astype(jnp.bfloat16)
            v_part = dot(w, da)
            k_part = dot(ds, q)
            q_part = dot(keys, ds, TN)
            dv = v_part if dv is None else dv + v_part
            dk = k_part if dk is None else dk + k_part
            dq[h] = q_part if dq[h] is None else dq[h] + q_part
        grad[0, :, :HEAD_SIZE] = (dk * score_scale).astype(grad.dtype)
        grad[0, :, HEAD_SIZE:] = dv.astype(grad.dtype)
    for h in range(2):
        cols = slice(h * HEAD_SIZE, (h + 1) * HEAD_SIZE)
        full = (dq[h].T * score_scale).astype(jnp.bfloat16)
        dq_mine[0, :, cols] = full[:rows]
        dq_other[0, :, cols] = full[rows:]


def merge_kernel(kept_a, got_a, last_a, kept_b, got_b, last_b, out):
    half = kept_a.shape[1]
    rows = out.shape[1]
    for part, (kept, got, last) in enumerate(((kept_a, got_a, last_a), (kept_b, got_b, last_b))):
        for z in range(half):
            total = (
                kept[0, z].astype(jnp.float32)
                + got[0, z].astype(jnp.float32)
                + last[z].astype(jnp.float32)
            )
            for core in range(CORES):
                slot = CORES * (half * part + z) + core
                out[slot] = total[core * rows : (core + 1) * rows].astype(jnp.bfloat16)


def finish_kernel(blocks, out):
    width = blocks.shape[2]
    for core in range(CORES):
        total = blocks[core].astype(jnp.float32)
        for z in range(1, CHIPS_Z):
            total = total + blocks[CORES * z + core].astype(jnp.float32)
        out[:, core * width : (core + 1) * width] = total


def merge(kept_a, got_a, last_a, kept_b, got_b, last_b):
    _, half, rows, width = kept_a.shape
    front = pl.BlockSpec((1, half, rows, width), lambda i: (0, 0, 0, 0))
    flat = pl.BlockSpec((half, rows, width), lambda i: (0, 0, 0))
    shape = (CORES * 2 * half, rows // CORES, width)
    return pl.pallas_call(
        merge_kernel,
        out_shape=jax.ShapeDtypeStruct(shape, jnp.bfloat16),
        grid=(1,),
        in_specs=[front, front, flat] * 2,
        out_specs=pl.BlockSpec(shape, lambda i: (0, 0, 0)),
        compiler_params=pltpu.CompilerParams(vmem_limit_bytes=16 << 20),
        name="projection_merge",
    )(kept_a, got_a, last_a, kept_b, got_b, last_b)


def finish(blocks):
    count, rows, width = blocks.shape
    return pl.pallas_call(
        finish_kernel,
        out_shape=jax.ShapeDtypeStruct((rows, CORES * width), jnp.float32),
        compiler_params=pltpu.CompilerParams(vmem_limit_bytes=16 << 20),
        name="projection_finish",
    )(blocks)


def split_kernel(
    scalars, q_own, q_other, k_own, k_other, v_own, v_other,
    q_mine, sent, kv_mine,
):
    width = q_other.shape[2]
    q_mine[...] = q_own[...]
    sent[:, :, :width] = q_other[...]
    sent[:, :, width : width + HEAD_SIZE] = k_other[...]
    sent[:, :, width + HEAD_SIZE :] = v_other[...]
    kv_mine[:, :, :HEAD_SIZE] = k_own[...]
    kv_mine[:, :, HEAD_SIZE:] = v_own[...]


def split_heads(scalars, query, keys, values):
    seqs, rows, width = query.shape
    out = jax.ShapeDtypeStruct((seqs, rows, width // 2), jnp.bfloat16)
    whole = jax.ShapeDtypeStruct(query.shape, jnp.bfloat16)
    outs = (out, whole, out)

    def half(a):
        shape = a.shape[:2] + (a.shape[2] // 2,)
        return [
            pl.BlockSpec(shape, lambda i, scalars: (0, 0, scalars[0])),
            pl.BlockSpec(shape, lambda i, scalars: (0, 0, 1 - scalars[0])),
        ]

    return pl.pallas_call(
        split_kernel,
        out_shape=outs,
        grid_spec=pltpu.PrefetchScalarGridSpec(
            num_scalar_prefetch=1,
            grid=(1,),
            in_specs=half(query) + half(keys) + half(values),
            out_specs=[pl.BlockSpec(o.shape, lambda i, *_: (0, 0, 0)) for o in outs],
        ),
        compiler_params=pltpu.CompilerParams(vmem_limit_bytes=16 << 20),
        name="split_heads",
    )(scalars, query, query, keys, keys, values, values)


def by_seq(shape):
    return pl.BlockSpec((1,) + shape[1:], lambda s, *_: (s,) + (0,) * (len(shape) - 1))


def forward(scalars, mine, recv, kvs, doc_mine, doc_recv):
    seqs, rows, width = mine.shape
    keys = 2 * rows * len(kvs)
    outs = (
        jax.ShapeDtypeStruct((seqs, 2 * rows, width), jnp.bfloat16),
        jax.ShapeDtypeStruct((seqs, 2, keys, 2 * rows), jnp.bfloat16),
    )
    query_spec = by_seq(mine.shape)
    recv_spec = pl.BlockSpec((1, rows, width), lambda s, *_: (s, 0, 0))
    return pl.pallas_call(
        forward_kernel,
        out_shape=outs,
        grid_spec=pltpu.PrefetchScalarGridSpec(
            num_scalar_prefetch=1,
            grid=(seqs,),
            in_specs=[query_spec, recv_spec]
            + [by_seq(kv.shape) for kv in kvs]
            + [by_seq(doc_mine.shape), by_seq(doc_recv.shape)],
            out_specs=[by_seq(o.shape) for o in outs],
        ),
        compiler_params=pltpu.CompilerParams(vmem_limit_bytes=20 << 20),
        cost_estimate=pl.CostEstimate(
            flops=4 * seqs * 2 * 2 * rows * keys * HEAD_SIZE,
            transcendentals=seqs * 2 * 2 * rows * keys,
            bytes_accessed=8 << 20,
        ),
        name="attention_forward",
    )(scalars, mine, recv, *kvs, doc_mine, doc_recv)


def early_projection(scalars, pieces, o_weight):
    rows = sum(p.shape[0] * p.shape[1] for p in pieces)
    features, both = o_weight.shape
    width = both // 2
    steps = 7
    block = features // steps
    outs = (
        jax.ShapeDtypeStruct((rows, width), jnp.bfloat16),
        jax.ShapeDtypeStruct((features, rows), jnp.bfloat16),
    )
    return pl.pallas_call(
        early_kernel,
        out_shape=outs,
        grid_spec=pltpu.PrefetchScalarGridSpec(
            num_scalar_prefetch=1,
            grid=(steps,),
            in_specs=[pl.BlockSpec(p.shape[:2] + (block,), lambda i, *_: (0, 0, i)) for p in pieces]
            + [pl.BlockSpec((block, width), lambda i, scalars: (i, scalars[0]))],
            out_specs=[
                pl.BlockSpec((rows, width), lambda i, *_: (0, 0)),
                pl.BlockSpec((block, rows), lambda i, *_: (i, 0)),
            ],
            scratch_shapes=[pltpu.VMEM((rows, width), jnp.float32)],
        ),
        compiler_params=pltpu.CompilerParams(vmem_limit_bytes=16 << 20),
        cost_estimate=pl.CostEstimate(
            flops=20 * rows * features * width, transcendentals=0, bytes_accessed=12 << 20
        ),
        name="projection_early",
    )(scalars, *pieces, o_weight)


def late_projection(scalars, pieces, rows_t, attn, early, o_weight):
    width = attn.shape[-1]
    features = o_weight.shape[0]
    late_rows = sum(p.shape[0] * p.shape[1] for p in pieces)
    steps = 2
    block = features // steps
    out_rows = features // (CHIPS_Y * CHIPS_Z)
    slab = jax.ShapeDtypeStruct((2, CHIPS_Z // 2, out_rows, width), jnp.bfloat16)

    def whole(a):
        return pl.BlockSpec(a.shape, lambda i, *_: (0,) * len(a.shape))

    return pl.pallas_call(
        late_kernel,
        out_shape=(jax.ShapeDtypeStruct(attn.shape, jnp.bfloat16),) + (slab,) * 4,
        grid_spec=pltpu.PrefetchScalarGridSpec(
            num_scalar_prefetch=1,
            grid=(steps,),
            in_specs=[pl.BlockSpec(p.shape[:2] + (block,), lambda i, *_: (0, 0, i)) for p in pieces]
            + [pl.BlockSpec((block, r.shape[1]), lambda i, *_: (i, 0)) for r in rows_t]
            + [whole(attn)]
            + [whole(e) for e in early]
            + [pl.BlockSpec((block, width), lambda i, scalars: (i, scalars[0]))],
            out_specs=[whole(attn)] + [whole(slab)] * 4,
            scratch_shapes=[pltpu.VMEM((late_rows, width), jnp.float32)]
            + [pltpu.VMEM((r.shape[1], width), jnp.bfloat16) for r in rows_t]
            + [
                pltpu.VMEM((late_rows, width), jnp.bfloat16),
                pltpu.VMEM((block, width), jnp.float32),
            ],
        ),
        compiler_params=pltpu.CompilerParams(vmem_limit_bytes=32 << 20),
        cost_estimate=pl.CostEstimate(
            flops=2 * 6 * late_rows * features * width, transcendentals=0, bytes_accessed=12 << 20
        ),
        name="projection_late",
    )(scalars, *pieces, *rows_t, attn, *early, o_weight)


def backward(mine, recv, kvs, weights, attn, d_attn):
    seqs, rows, width = mine.shape
    half = jax.ShapeDtypeStruct((seqs, rows, width), jnp.bfloat16)
    shape = kvs[0].shape
    own = jax.ShapeDtypeStruct(shape, jnp.float32)
    sent = jax.ShapeDtypeStruct(shape, jnp.bfloat16)
    outs = (half, half, own) + (sent,) * (len(kvs) - 1)
    query_spec = by_seq(mine.shape)
    recv_spec = pl.BlockSpec((1, rows, width), lambda s, *_: (s, 0, 0))
    return pl.pallas_call(
        backward_kernel,
        out_shape=outs,
        grid=(seqs,),
        in_specs=[query_spec, recv_spec]
        + [by_seq(a.shape) for a in (*kvs, weights, attn, d_attn)],
        out_specs=[by_seq(o.shape) for o in outs],
        compiler_params=pltpu.CompilerParams(vmem_limit_bytes=20 << 20),
        cost_estimate=pl.CostEstimate(
            flops=10 * seqs * 2 * 2 * rows * 10 * rows * HEAD_SIZE,
            transcendentals=0,
            bytes_accessed=8 << 20,
        ),
        name="attention_backward",
    )(mine, recv, *kvs, weights, attn, d_attn)


def local(query, key_states, value_state_rows, d_out, o_weight, doc_start):
    seq_count, shard_rows, query_width = query.shape
    ctx = lax.axis_index("ctx")
    tp = lax.axis_index("tp")
    core = ctx % CORES
    y = ctx // CORES % CHIPS_Y
    chip_pos = ctx // CORES * (CORES * shard_rows)
    scalars = jnp.stack([core, tp, y, chip_pos]).astype(jnp.int32)
    first = core == 0
    q_mine, sent, kv_mine = split_heads(scalars, query, key_states, value_state_rows)

    r3 = tp_ahead(d_out, 1)
    r1 = tp_ahead(d_out, -1)
    recv = to_sibling(sent)
    doc_mine = doc_start[:, None, :]
    doc_recv = to_sibling(doc_mine)
    t0 = to_sibling(d_out)
    recv, doc_recv, t0, scalars, first, one_row, two_rows = lax.optimization_barrier(
        (recv, doc_recv, t0, scalars, first, y < 1, y < 2)
    )
    kv0 = jnp.concatenate([kv_mine, recv[..., -2 * HEAD_SIZE :]], axis=1)
    kv4, kv1 = (chips_ahead(kv0, d) for d in (4, 1))
    own, own_t = early_projection(scalars, [d_out, t0], o_weight)

    kv_two = jnp.where(two_rows, kv0, kv4)
    kv_three = jnp.where(one_row, kv0, kv4)
    r1, r3, own, kv1, kv_two, kv_three = lax.optimization_barrier(
        (r1, r3, own, kv1, kv_two, kv_three)
    )
    kv2, kv3 = y_ahead(kv_two, 2), y_ahead(kv_three, 3)
    r2a = tp_ahead(r3[:1], 1)
    r2b = tp_ahead(r1[1:], -1)
    near, near_t = early_projection(
        scalars, [r1, r3, to_sibling(r1), to_sibling(r3)], o_weight
    )
    near, r2a, r2b, kv2, kv3 = lax.optimization_barrier((near, r2a, r2b, kv2, kv3))
    kvs = [kv0, kv1, kv2, kv3, kv4]
    attn, weights = forward(scalars, q_mine, recv, kvs, doc_mine, doc_recv)
    d_attn, sent_a, kept_a, sent_b, kept_b = late_projection(
        scalars,
        [r2a, r2b, to_sibling(r2a), to_sibling(r2b)],
        [own_t, near_t],
        attn,
        [own, near],
        o_weight,
    )
    got_a = y_route(sent_a, y_pair)
    got_b = y_route(sent_b, y_mirror)
    dq_mine, dq_other, g_own, *g_sent = backward(
        q_mine, recv, kvs, weights, attn, d_attn
    )
    *g_near, g_far = (chips_ahead(g, -d) for d, g in enumerate(g_sent, 1))
    dq_recv = to_sibling(dq_other)
    got_a, got_b, g_own, g_far, dq_recv, *g_near = lax.optimization_barrier(
        (got_a, got_b, g_own, g_far, dq_recv, *g_near)
    )

    def added(*blocks):
        total = blocks[0].astype(jnp.float32)
        for block in blocks[1:]:
            total = total + block.astype(jnp.float32)
        return total

    next_a = added(kept_a[1], got_a[1]).astype(jnp.bfloat16)
    next_b = added(kept_b[1], got_b[1]).astype(jnp.bfloat16)
    last_a = y_route(next_a, y_mirror)
    last_b = y_route(next_b, y_pair)
    w_sum = merge(kept_a, got_a, last_a, kept_b, got_b, last_b)
    w_all = z_exchange(w_sum)

    grads = added(g_own, *g_near, g_far).astype(jnp.bfloat16)
    g_mine = grads[:, :shard_rows]
    g_recv = to_sibling(grads[:, shard_rows:])

    def by_core(own, other):
        return jnp.concatenate(
            [jnp.where(first, own, other), jnp.where(first, other, own)], axis=-1
        )

    return (
        by_core(dq_mine, dq_recv),
        by_core(g_mine[..., :HEAD_SIZE], g_recv[..., :HEAD_SIZE]),
        by_core(g_mine[..., HEAD_SIZE:], g_recv[..., HEAD_SIZE:]),
        finish(w_all),
    )


def solution(mesh):
    return jax.shard_map(
        local,
        mesh=mesh,
        in_specs=(
            P(None, "ctx", "tp"),
            P(None, "ctx", "tp"),
            P(None, "ctx", "tp"),
            P(None, ("ctx", "tp"), None),
            P(None, "tp"),
            P(None, "ctx"),
        ),
        out_specs=(
            P(None, "ctx", "tp"),
            P(None, "ctx", "tp"),
            P(None, "ctx", "tp"),
            P("ctx", "tp"),
        ),
        check_vma=False,
    )
```
